32 devices in a mesh: doc: 8 (over y, x, core), seq: 4 (over z).
Axes of the slice: x: 2, y: 2, z: 4, core: 2. Of those that a mesh axis runs over, the one named last changes fastest.
Arguments:
- inputs: bfloat16 [16, 1024, 768], P('doc', 'seq'), may hold values from -6 to 6
- attn_gain: float32 [768], replicated, may hold values from 0.5 to 1.5
- qkv_weight: bfloat16 [768, 2304], replicated, may hold values from -0.25 to 0.25
- attn_out_weight: bfloat16 [768, 768], replicated, may hold values from -2 to 2
- mlp_gain: float32 [768], replicated, may hold values from 0.5 to 1.5
- mlp_in_weight: bfloat16 [768, 2304], replicated, may hold values from -0.21875 to 0.21875
- mlp_out_weight: bfloat16 [1152, 768], replicated, may hold values from -0.1875 to 0.1875
- cotangent: bfloat16 [16, 1024, 768], P('doc', 'seq'), may hold values from -6 to 6
Outputs:
- output: bfloat16 [16, 1024, 768], P('doc', 'seq')
- input_grad: bfloat16 [16, 1024, 768], P('doc', 'seq')
- attn_gain_grad: float32 [768], replicated
- qkv_weight_grad: float32 [768, 2304], replicated
- attn_out_weight_grad: float32 [768, 768], replicated
- mlp_gain_grad: float32 [768], replicated
- mlp_in_weight_grad: float32 [768, 2304], replicated
- mlp_out_weight_grad: float32 [1152, 768], replicated
The draws below stay inside these ranges and needn't reach their ends.
All inputs are finite; a program needn't handle non-finite values.
Results may differ from the reference program's by a relative error of at most 0.015.
Values may be sent and summed in bfloat16 or wider, within the bound.
A program may use at most 128 MiB of HBM per device.

```python
import jax
import jax.numpy as jnp
from jax import lax

D = 768
HEADS = 12
HEAD_DIM = 64
FF = 1152
SEQ_LEN = 1024
DOC_GROUP = 2
DOCUMENTS = 16
N_DOC = 8


def steps_of(rng, extent, shards, low, largest):
    loudness, own = 1.0, jax.random.fold_in(rng, 6)
    for dim, blocks in shards:
        draws = jnp.exp(jax.random.uniform(jax.random.fold_in(own, dim), (blocks,), jnp.float32, low / len(shards), largest / len(shards)))
        loudness = loudness * jnp.repeat(draws, extent[dim] // blocks).reshape([-1 if axis == dim else 1 for axis in range(len(extent))])
    return loudness


def scatter_about(rng, extent, deviation, bound, pieces=(), kind=jnp.bfloat16):
    drawn = deviation * jax.random.normal(rng, extent, jnp.float32)
    if pieces:
        drawn = drawn * steps_of(rng, extent, pieces, -0.22, 0.18)
    return jnp.clip(drawn, -bound, bound).astype(kind)


def setup_inputs(seed: int = 0) -> dict:
    arg_keys = jax.random.split(jax.random.key(seed), 9)
    return {
        "inputs": scatter_about(arg_keys[0], (DOCUMENTS, SEQ_LEN, D), 1.0, 6.0, ((0, 8), (1, 4))),
        "attn_gain": jnp.clip(1.0 + 0.1 * jax.random.normal(arg_keys[1], (D,), jnp.float32), 0.5, 1.5),
        "qkv_weight": scatter_about(arg_keys[2], (D, 3 * D), (2 * D // 3) ** -0.5, 0.25),
        "attn_out_weight": scatter_about(arg_keys[3], (D, D), (max(12 * D // SEQ_LEN, 1)) ** -0.5, 2.0),
        "mlp_gain": jnp.clip(1.0 + 0.1 * jax.random.normal(arg_keys[4], (D,), jnp.float32), 0.5, 1.5),
        "mlp_in_weight": scatter_about(arg_keys[5], (D, 2 * FF), D ** -0.5, 0.21875),
        "mlp_out_weight": scatter_about(arg_keys[6], (FF, D), FF ** -0.5, 0.1875),
        "cotangent": scatter_about(arg_keys[7], (DOCUMENTS, SEQ_LEN, D), 1.0, 6.0, ((0, 8), (1, 4))),
    }


HIGHEST = lax.Precision.HIGHEST
ROPE_THETA = 160000.0
NORM_EPSILON = 1e-05

@jax.custom_vjp
def low(v):
    return lax.optimization_barrier(v.astype(jnp.bfloat16)).astype(jnp.float32)

@jax.custom_vjp
def low_back(v):
    return v

def low_keep(v):
    return (low(v), None)

def low_pass(kept, grad):
    return (grad,)

def back_keep(v):
    return (v, None)

def back_low(kept, grad):
    return (low(grad),)
low.defvjp(low_keep, low_pass)
low_back.defvjp(back_keep, back_low)

def norm_rows(values, scale_gain):
    row_mean = lax.optimization_barrier(jnp.mean(values, axis=-1, keepdims=True))
    centered = values - row_mean
    variance = lax.optimization_barrier(jnp.mean(centered * centered, axis=-1, keepdims=True))
    return centered * lax.rsqrt(variance + NORM_EPSILON) * scale_gain

def rotary_tables(length, head_width):
    half_width = head_width // 2
    frequency = ROPE_THETA ** (-(jnp.arange(half_width, dtype=jnp.float32) * 2.0) / head_width)
    angles = jnp.arange(length, dtype=jnp.float32)[:, None] * frequency[None, :]
    angles = jnp.concatenate([angles, angles], axis=-1)
    return (jnp.cos(angles)[:, None, :], jnp.sin(angles)[:, None, :])

def rotate(values, cosine_table, sine_table):
    half_width = values.shape[-1] // 2
    turned = jnp.concatenate([-values[..., half_width:], values[..., :half_width]], axis=-1)
    return values * cosine_table + turned * sine_table

def attend_doc(queries, key_rows, value_rows):
    scores = low_back(jnp.einsum('qhd,khd->hqk', queries, key_rows, precision=HIGHEST) * 0.125)
    softmax_out = jax.nn.softmax(scores, axis=-1)
    return jnp.einsum('hqk,khd->qhd', low(softmax_out), value_rows, precision=HIGHEST)

def forward(inputs_f, attn_gain, qkv_weight, attn_out_weight, mlp_gain, mlp_in_weight, mlp_out_weight):
    doc_count = inputs_f.shape[0]
    flat_in = inputs_f.reshape(doc_count * SEQ_LEN, D)
    normed = low(norm_rows(flat_in, attn_gain))
    projected = low_back(jnp.dot(normed, qkv_weight, precision=HIGHEST))
    projected = projected.reshape(doc_count, SEQ_LEN, 3, HEADS, HEAD_DIM)
    cosine_table, sine_table = rotary_tables(SEQ_LEN, HEAD_DIM)
    queries = low(rotate(projected[:, :, 0], cosine_table, sine_table))
    key_rows = low(rotate(projected[:, :, 1], cosine_table, sine_table))
    value_rows = low(projected[:, :, 2])
    attended = lax.map(lambda bundle: jax.checkpoint(attend_doc)(*bundle), (queries, key_rows, value_rows))
    attended = low(low_back(attended)).reshape(doc_count * SEQ_LEN, D)
    hidden_res = flat_in + low_back(jnp.dot(attended, attn_out_weight, precision=HIGHEST))
    normed_two = low(norm_rows(hidden_res, mlp_gain))
    gate_up = low_back(jnp.dot(normed_two, mlp_in_weight, precision=HIGHEST))
    inner_act = low(jax.nn.gelu(gate_up[:, :FF], approximate=False) * gate_up[:, FF:])
    result = hidden_res + low_back(jnp.dot(inner_act, mlp_out_weight, precision=HIGHEST))
    return result.reshape(doc_count, SEQ_LEN, D)

def reference(inputs, attn_gain, qkv_weight, attn_out_weight, mlp_gain, mlp_in_weight, mlp_out_weight, cotangent):
    params = (attn_gain.astype(jnp.float32), qkv_weight.astype(jnp.float32), attn_out_weight.astype(jnp.float32), mlp_gain.astype(jnp.float32), mlp_in_weight.astype(jnp.float32), mlp_out_weight.astype(jnp.float32))
    grouped_inputs = inputs.astype(jnp.float32).reshape(N_DOC, DOC_GROUP, SEQ_LEN, D)
    grouped_cotangent = cotangent.astype(jnp.float32).reshape(N_DOC, DOC_GROUP, SEQ_LEN, D)

    def group_step(summed, bundle):
        group_inputs, group_cotangent = bundle
        result, pullback = jax.vjp(forward, group_inputs, *params)
        gradients = pullback(group_cotangent)
        summed = tuple((running + update for running, update in zip(summed, gradients[1:])))
        return (summed, (result.astype(jnp.bfloat16), gradients[0].astype(jnp.bfloat16)))
    start_sums = tuple((jnp.zeros_like(parameter) for parameter in params))
    summed, (outputs, input_grads) = lax.scan(group_step, start_sums, (grouped_inputs, grouped_cotangent))
    return (outputs.reshape(DOCUMENTS, SEQ_LEN, D), input_grads.reshape(DOCUMENTS, SEQ_LEN, D), summed[0], summed[1], summed[2], summed[3], summed[4], summed[5])
```

```python
import functools

import jax
import jax.numpy as jnp
import numpy as np
from jax import lax
from jax.experimental import pallas as pl
from jax.experimental.pallas import tpu as pltpu
from jax.sharding import PartitionSpec as P

HEAD_DIM = 64
ROPE_THETA = 160000.0
NORM_EPSILON = 1e-05
F32 = jnp.float32
BF16 = jnp.bfloat16
MESH = pl.DeviceIdType.MESH
LANES = 128
VMEM_LIMIT = 60 << 20


def nn(a, b):
    return lax.dot_general(a, b, (((1,), (0,)), ((), ())), preferred_element_type=F32)


def nt(a, b):
    return lax.dot_general(a, b, (((1,), (1,)), ((), ())), preferred_element_type=F32)


def lane_of(shape):
    return lax.broadcasted_iota(jnp.int32, shape, 1)


def one_head(pair, sub):
    lane = lane_of(pair.shape)
    mine = (lane < HEAD_DIM) if sub == 0 else (lane >= HEAD_DIM)
    return jnp.where(mine, pair, jnp.zeros_like(pair))


def turned(values):
    back = pltpu.roll(values, HEAD_DIM // 2, 1)
    ahead = pltpu.roll(values, LANES - HEAD_DIM // 2, 1)
    return jnp.where(lane_of(values.shape) % HEAD_DIM < HEAD_DIM // 2, ahead, back)


def row_stats(values):
    mean = jnp.mean(values, axis=1, keepdims=True)
    centered = values - mean
    scale = lax.rsqrt(jnp.mean(centered * centered, axis=1, keepdims=True) + NORM_EPSILON)
    return centered * scale, scale


def norm_back(grad, unit, scale, gain):
    weighted = grad * gain
    along = jnp.mean(weighted, axis=1, keepdims=True)
    across = jnp.mean(weighted * unit, axis=1, keepdims=True)
    return scale * (weighted - along - unit * across)


def bit_of(index, weight):
    return (index // weight) % 2


def flipped(index, weight):
    return index + weight - 2 * weight * bit_of(index, weight)


def greet(partners):
    barrier = pltpu.get_barrier_semaphore()
    for partner in partners:
        pl.semaphore_signal(barrier, inc=1, device_id=partner, device_id_type=MESH)
    pl.semaphore_wait(barrier, len(partners))


def group_partners(doc, seq, n_seq):
    core = doc % 2
    found = []
    for other_core in range(2):
        for step in range(n_seq):
            if other_core == 0 and step == 0:
                continue
            found.append(
                (doc - core + (core + other_core) % 2, (seq + step) % n_seq)
            )
    return found


class Exchange:
    def __init__(self, doc, seq, n_seq):
        core = doc % 2
        half = n_seq // 2
        base = doc - core
        self.out_targets = [(base + seq // half, 2 * core + block) for block in range(2)]
        self.out_slot = seq % half
        self.back_targets = [(base + seq // 2, half * core + slot) for slot in range(2)]
        self.back_block = seq % 2
        self.doc, self.seq = doc, seq

    def is_self(self, target):
        return jnp.logical_and(target[0] == self.doc, target[1] == self.seq)


def send_or_keep(ex, target, src, dst, send_sem, recv_sem):
    mine = ex.is_self(target)

    @pl.when(mine)
    def _():
        pltpu.make_async_copy(src, dst, recv_sem).start()

    @pl.when(jnp.logical_not(mine))
    def _():
        pltpu.make_async_remote_copy(
            src_ref=src, dst_ref=dst, send_sem=send_sem, recv_sem=recv_sem,
            device_id=target, device_id_type=MESH,
        ).start()


def wait_sent(ex, target, src, dst, send_sem, recv_sem):
    @pl.when(jnp.logical_not(ex.is_self(target)))
    def _():
        pltpu.make_async_remote_copy(
            src_ref=src, dst_ref=dst, send_sem=send_sem, recv_sem=recv_sem,
            device_id=target, device_id_type=MESH,
        ).wait_send()


def wait_bytes(ref, sem):
    pltpu.make_async_copy(ref, ref, sem).wait()


def front_kernel(
    n_seq,
    x_in, cot_in, gain1, gain2, wqkv_in, wo_in, win_in, wout_in, cos_in, sin_in,
    out_o, x_o, xn_o, q_o, k_o, v_o, do_o, lse_o, dd_o, dh_o, g_o,
    xs, cs, outs, wqkv, wo, win, wout, cos, sin, xn, q, k, v, att, h, xn2, xn2t, hid, dgu, dmt, grads, do, dh, lse, dd, acc,
    w_sem, send_sem, recv_sem, kv_send, kv_recv, out_sem,
):
    doc, seq = lax.axis_index("doc"), lax.axis_index("seq")
    core = doc % 2
    ex = Exchange(doc, seq, n_seq)
    rows = x_in.shape[1]
    tokens, width = xs.shape
    ff = wout.shape[0]
    pairs = width // LANES

    loads = [
        pltpu.make_async_copy(s, d, w_sem.at[i])
        for i, (s, d) in enumerate(
            [(wqkv_in, wqkv), (wo_in, wo), (win_in, win), (wout_in, wout)]
            + [(t.at[pl.ds(core * tokens, tokens)], d) for t, d in ((cos_in, cos), (sin_in, sin))]
        )
    ]
    for load in loads:
        load.start()
    greet(group_partners(doc, seq, n_seq))

    def spread(src, dst, base):
        for block in range(2):
            send_or_keep(
                ex, ex.out_targets[block], src.at[block],
                dst.at[pl.ds(ex.out_slot * rows, rows)],
                send_sem.at[base + block], recv_sem.at[base + ex.out_slot],
            )

    def spread_sent(src, dst, base):
        for block in range(2):
            wait_sent(
                ex, ex.out_targets[block], src.at[block],
                dst.at[pl.ds(ex.out_slot * rows, rows)],
                send_sem.at[base + block], recv_sem.at[base + ex.out_slot],
            )

    spread(x_in, xs, 0)
    for slot in range(2):
        wait_bytes(xs.at[pl.ds(slot * rows, rows)], recv_sem.at[slot])
    spread(cot_in, cs, 2)

    unit, _ = row_stats(xs[...].astype(F32))
    xn[...] = (unit * gain1[...]).astype(BF16)
    for i in (0, 4, 5):
        loads[i].wait()

    def roped(tile, scale):
        return ((tile * cos[...] + turned(tile) * sin[...]) * scale).astype(BF16)

    def project(j, _):
        lanes = pl.ds(pl.multiple_of(j * LANES, LANES), LANES)
        k_lanes = pl.ds(pl.multiple_of(width + j * LANES, LANES), LANES)
        v_lanes = pl.ds(pl.multiple_of(2 * width + j * LANES, LANES), LANES)
        k[:tokens, lanes] = roped(nn(xn[...], wqkv[:, k_lanes]), 1.0)
        v[:tokens, lanes] = nn(xn[...], wqkv[:, v_lanes]).astype(BF16)
        return 0

    lax.fori_loop(0, pairs, project, 0)
    sibling = (flipped(doc, 1), seq)
    kv_copies = [
        pltpu.make_async_remote_copy(
            src_ref=ref.at[pl.ds(0, tokens)], dst_ref=ref.at[pl.ds(tokens, tokens)],
            send_sem=kv_send.at[i], recv_sem=kv_recv.at[i],
            device_id=sibling, device_id_type=MESH,
        )
        for i, ref in enumerate((k, v))
    ]
    for copy in kv_copies:
        copy.start()

    def project_q(j, _):
        lanes = pl.ds(pl.multiple_of(j * LANES, LANES), LANES)
        q[:, lanes] = roped(nn(xn[...], wqkv[:, lanes]), 0.125)
        return 0

    lax.fori_loop(0, pairs, project_q, 0)
    for copy in kv_copies:
        copy.wait()

    def attend(j, _):
        lanes = pl.ds(pl.multiple_of(j * LANES, LANES), LANES)
        k2, vt, q2 = k[:, lanes], v[:, lanes].T, q[:, lanes]
        mixed = []
        for sub in range(2):
            scores = nt(one_head(k2, sub), q2)
            top = jnp.max(scores, axis=0, keepdims=True)
            weights = jnp.exp(scores - top)
            total = jnp.sum(weights, axis=0, keepdims=True)
            lse[j, sub : sub + 1, :] = top + jnp.log(total)
            mixed.append(
                nn(vt[sub * HEAD_DIM : (sub + 1) * HEAD_DIM], weights.astype(BF16)) * (1.0 / total)
            )
        att[:, lanes] = jnp.concatenate(mixed, axis=0).T.astype(BF16)
        return 0

    lax.fori_loop(0, pairs, attend, 0)

    loads[1].wait()
    h[...] = xs[...].astype(F32) + nn(att[...], wo[...])
    unit2, _ = row_stats(h[...])
    xn2[...] = (unit2 * gain2[...]).astype(BF16)
    xn2t[...] = xn2[...].T
    loads[2].wait()
    loads[3].wait()
    for slot in range(2):
        wait_bytes(cs.at[pl.ds(slot * rows, rows)], recv_sem.at[2 + slot])
    dmt[...] = cs[...].T

    def feed(j, _):
        gate_lanes = pl.ds(pl.multiple_of(j * LANES, LANES), LANES)
        up_lanes = pl.ds(pl.multiple_of(ff + j * LANES, LANES), LANES)
        gate = nn(xn2[...], win[:, gate_lanes])
        up = nn(xn2[...], win[:, up_lanes])
        phi = 0.5 * (1.0 + lax.erf(gate * 0.7071067811865476))
        slope = phi + gate * (0.3989422804014327 * jnp.exp(-0.5 * gate * gate))
        active = gate * phi
        hid[:, gate_lanes] = (active * up).astype(BF16)
        dhid = nt(cs[...], wout[pl.ds(pl.multiple_of(j * LANES, LANES), LANES), :])
        dgu[:, gate_lanes] = (dhid * up * slope).astype(BF16)
        dgu[:, up_lanes] = (dhid * active).astype(BF16)
        return 0

    lax.fori_loop(0, ff // LANES, feed, 0)

    outs[...] = (h[...] + nn(hid[...], wout[...])).astype(BF16)
    for slot in range(2):
        send_or_keep(
            ex, ex.back_targets[slot], outs.at[pl.ds(slot * rows, rows)],
            out_o.at[ex.back_block], send_sem.at[4 + slot], recv_sem.at[4 + ex.back_block],
        )

    step = 3 * LANES

    def grad_out(j, _):
        lanes = pl.ds(pl.multiple_of(j * step, LANES), step)
        grads[:, lanes] = nn(dmt[...], hid[:, lanes]).astype(BF16)
        return 0

    lax.fori_loop(0, ff // step, grad_out, 0)

    def grad_in(j, _):
        lanes = pl.ds(pl.multiple_of(j * step, LANES), step)
        g_lanes = pl.ds(pl.multiple_of(ff + j * step, LANES), step)
        grads[:, g_lanes] = nn(xn2t[...], dgu[:, lanes]).astype(BF16)
        return 0

    lax.fori_loop(0, 2 * ff // step, grad_in, 0)

    acc[...] = nt(dgu[...], win[...])
    unit2, scale2 = row_stats(h[...])
    grad2 = acc[...]
    dh[...] = cs[...].astype(F32) + norm_back(grad2, unit2, scale2, gain2[...])
    gain_terms = (grad2 * unit2).astype(BF16).T
    grads[:, 3 * ff + width :] = nn(gain_terms, jnp.ones((tokens, LANES), BF16)).astype(BF16)
    datt = dh[...].astype(BF16)
    att_t = att[...].T
    grads[:, 3 * ff : 3 * ff + width] = nn(att_t, datt).astype(BF16)
    do[...] = nt(datt, wo[...]).astype(BF16)

    lane = lax.broadcasted_iota(jnp.int32, (8, LANES), 1)
    row = lax.broadcasted_iota(jnp.int32, (8, LANES), 0)
    pick = jnp.where(lane // HEAD_DIM == row, 1.0, 0.0).astype(F32)
    for j in range(pairs):
        lanes = slice(j * LANES, (j + 1) * LANES)
        product = do[:, lanes].astype(F32) * att[:, lanes].astype(F32)
        sums = lax.dot_general(
            pick, product, (((1,), (1,)), ((), ())),
            precision=lax.Precision.HIGHEST, preferred_element_type=F32,
        )
        dd[j] = sums[:2]

    stores = [
        pltpu.make_async_copy(s, d, out_sem.at[i])
        for i, (s, d) in enumerate(
            [(xs, x_o), (xn, xn_o), (q, q_o), (k, k_o), (v, v_o), (do, do_o), (lse, lse_o), (dd, dd_o), (dh, dh_o), (grads, g_o)]
        )
    ]
    for store in stores:
        store.start()
    spread_sent(x_in, xs, 0)
    spread_sent(cot_in, cs, 2)
    for block in range(2):
        wait_bytes(out_o.at[block], recv_sem.at[4 + block])
    for slot in range(2):
        wait_sent(
            ex, ex.back_targets[slot], outs.at[pl.ds(slot * rows, rows)],
            out_o.at[ex.back_block], send_sem.at[4 + slot], recv_sem.at[4 + ex.back_block],
        )
    for store in stores:
        store.wait()


def front(n_seq, inputs, cotangent, gain1, gain2, wqkv, wo, win, wout, cos, sin):
    blocks, rows, width = inputs.shape
    tokens = blocks * rows
    ff = wout.shape[0]
    pairs = width // LANES
    cols = 3 * ff + width + LANES
    hbm, vmem = pl.BlockSpec(memory_space=pl.ANY), pl.BlockSpec(memory_space=pltpu.VMEM)
    sds = jax.ShapeDtypeStruct
    return pl.pallas_call(
        functools.partial(front_kernel, n_seq),
        out_shape=[
            sds((blocks, rows, width), BF16), sds((tokens, width), BF16), sds((tokens, width), BF16),
            sds((tokens, width), BF16), sds((2 * tokens, width), BF16), sds((2 * tokens, width), BF16),
            sds((tokens, width), BF16), sds((pairs, 2, tokens), F32), sds((pairs, 2, tokens), F32),
            sds((tokens, width), F32), sds((width, cols), BF16),
        ],
        in_specs=[hbm, hbm, vmem, vmem] + [hbm] * 6,
        out_specs=[hbm] * 11,
        scratch_shapes=[
            pltpu.VMEM((tokens, width), BF16), pltpu.VMEM((tokens, width), BF16), pltpu.VMEM((tokens, width), BF16),
            pltpu.VMEM(wqkv.shape, BF16), pltpu.VMEM(wo.shape, BF16), pltpu.VMEM(win.shape, BF16), pltpu.VMEM(wout.shape, BF16),
            pltpu.VMEM((tokens, LANES), F32), pltpu.VMEM((tokens, LANES), F32),
            pltpu.VMEM((tokens, width), BF16), pltpu.VMEM((tokens, width), BF16),
            pltpu.VMEM((2 * tokens, width), BF16), pltpu.VMEM((2 * tokens, width), BF16),
            pltpu.VMEM((tokens, width), BF16), pltpu.VMEM((tokens, width), F32),
            pltpu.VMEM((tokens, width), BF16), pltpu.VMEM((width, tokens), BF16),
            pltpu.VMEM((tokens, ff), BF16), pltpu.VMEM((tokens, 2 * ff), BF16), pltpu.VMEM((width, tokens), BF16),
            pltpu.VMEM((width, cols), BF16), pltpu.VMEM((tokens, width), BF16), pltpu.VMEM((tokens, width), F32),
            pltpu.VMEM((pairs, 2, tokens), F32), pltpu.VMEM((pairs, 2, tokens), F32),
            pltpu.VMEM((tokens, width), F32),
            pltpu.SemaphoreType.DMA((6,)), pltpu.SemaphoreType.DMA((6,)), pltpu.SemaphoreType.DMA((6,)),
            pltpu.SemaphoreType.DMA((2,)), pltpu.SemaphoreType.DMA((2,)), pltpu.SemaphoreType.DMA((10,)),
        ],
        compiler_params=pltpu.CompilerParams(collective_id=0, has_side_effects=True, vmem_limit_bytes=VMEM_LIMIT),
        name="front",
    )(inputs, cotangent, gain1, gain2, wqkv, wo, win, wout, cos, sin)


class Reduction:
    def __init__(self, rows, src, lanes, width, acc, landing, final, sems, partners, weights, out):
        self.src, self.lanes, self.width = src, lanes, width
        self.acc, self.landing, self.final, self.sems, self.out = acc, landing, final, sems, out
        self.core, self.bits, self.partners = weights[0], weights[1:], partners
        self.rows = rows
        self.plan = []
        offset, extent, base = 0, rows, rows
        for bit in self.bits:
            split = (extent // 2) % 16 == 0
            keep = extent // 2 if split else extent
            self.plan.append((offset, extent, keep, split, base))
            base += keep
            if split:
                offset = offset + bit * keep
            extent = keep
        self.final_offset, self.final_extent = offset, extent
        self.rounds = len(self.bits)

    @staticmethod
    def landing_rows(rows, rounds):
        total, extent = rows, rows
        for _ in range(rounds):
            extent = extent // 2 if (extent // 2) % 16 == 0 else extent
            total += extent
        return total

    def part(self, which):
        return pl.ds(pl.multiple_of(self.lanes[0] + which * self.lanes[1], LANES), self.width)

    def rows_at(self, start, extent):
        return pl.ds(pl.multiple_of(start, 16) if not isinstance(start, int) else start, extent)

    def copy(self, src, dst, slot, partner):
        return pltpu.make_async_remote_copy(
            src_ref=src, dst_ref=dst, send_sem=self.sems[0].at[slot], recv_sem=self.sems[1].at[slot],
            device_id=partner, device_id_type=MESH,
        )

    def core_copy(self):
        return self.copy(
            self.src.at[:, self.part(1 - self.core)], self.landing.at[pl.ds(0, self.rows)], 0, self.partners[0]
        )

    def own_copy(self):
        return pltpu.make_async_copy(self.src.at[:, self.part(self.core)], self.acc, self.sems[2])

    def down_copy(self, r):
        offset, extent, keep, split, base = self.plan[r]
        start = offset + (1 - self.bits[r]) * keep if split else offset
        return self.copy(
            self.acc.at[self.rows_at(start, keep)], self.landing.at[pl.ds(base, keep)], 1 + r, self.partners[1 + r]
        )

    def up_copy(self, r):
        offset, extent, keep, split, base = self.plan[r]
        start = self.rows_at(offset + self.bits[r] * keep, keep)
        return self.copy(self.final.at[start], self.final.at[start], 1 + self.rounds + r, self.partners[1 + r])

    def up_wait(self, r):
        offset, extent, keep, split, base = self.plan[r]
        start = self.rows_at(offset + (1 - self.bits[r]) * keep, keep)
        copy = self.copy(self.final.at[start], self.final.at[start], 1 + self.rounds + r, self.partners[1 + r])
        copy.wait_recv()
        self.up_copy(r).wait_send()

    def last_copy(self):
        return self.copy(self.final, self.out.at[:, self.part(self.core)], 1 + 2 * self.rounds, self.partners[0])

    def last_own(self):
        return pltpu.make_async_copy(self.final, self.out.at[:, self.part(self.core)], self.sems[2])

    def add(self, offset, base, keep, target):
        block = 96
        while keep % block:
            block //= 2

        def body(i, _):
            mine = self.rows_at(offset + i * block, block)
            theirs = pl.ds(pl.multiple_of(base + i * block, 16), block)
            target[mine] = (self.acc[mine].astype(F32) + self.landing[theirs].astype(F32)).astype(BF16)
            return 0

        lax.fori_loop(0, keep // block, body, 0)

    def start(self):
        self.core_copy().start()
        self.own_copy().start()

    def steps(self):
        ups = [r for r in reversed(range(self.rounds)) if self.plan[r][3]]

        def core_done():
            self.core_copy().wait()
            self.own_copy().wait()
            self.add(0, 0, self.rows, self.acc)
            self.down_copy(0).start()

        def down_done(r):
            offset, extent, keep, split, base = self.plan[r]
            self.down_copy(r).wait()
            target = self.acc if r + 1 < self.rounds else self.final
            self.add(offset + self.bits[r] * keep if split else offset, base, keep, target)
            if r + 1 < self.rounds:
                self.down_copy(r + 1).start()
            else:
                self.up_copy(ups[0]).start()

        def up_done(i):
            self.up_wait(ups[i])
            if i + 1 < len(ups):
                self.up_copy(ups[i + 1]).start()
            else:
                self.last_copy().start()
                self.last_own().start()

        def last_done():
            copy = self.copy(
                self.final, self.out.at[:, self.part(1 - self.core)], 1 + 2 * self.rounds, self.partners[0]
            )
            copy.wait_recv()
            self.last_copy().wait_send()
            self.last_own().wait()

        return (
            [core_done]
            + [functools.partial(down_done, r) for r in range(self.rounds)]
            + [functools.partial(up_done, i) for i in range(len(ups))]
            + [last_done]
        )


def log2(n):
    return n.bit_length() - 1


def back_kernel(
    n_doc, n_seq,
    x_in, xn_in, q_in, k_in, v_in, do_in, lse_in, dd_in, dh_in, g1_in, wqkv_in, gain1, cos_in, sin_in,
    dx_o, g1_o, g2_o,
    xs, xn, q, k, v, do, lse, dd, dh, wqkv, cos, sin, dqkv, dqt, away, own, landed, xnt, g2, dx,
    acc_a, acc_b, acc_c, acc_d, land_a, land_b, land_c, land_d, fin_a, fin_b, fin_c, fin_d,
    in_sem, kv_send, kv_recv, dx_send, dx_recv, send_a, recv_a, send_b, recv_b, send_c, recv_c, send_d, recv_d, own_sem,
):
    doc, seq = lax.axis_index("doc"), lax.axis_index("seq")
    core = doc % 2
    ex = Exchange(doc, seq, n_seq)
    tokens, width = xs.shape
    rows = tokens // 2
    pairs = width // LANES

    loads = [
        pltpu.make_async_copy(s, d, in_sem.at[i])
        for i, (s, d) in enumerate(
            [(q_in, q), (k_in, k), (v_in, v), (do_in, do), (lse_in, lse), (dd_in, dd), (xn_in, xn), (x_in, xs), (dh_in, dh), (wqkv_in, wqkv)]
            + [(t.at[pl.ds(core * tokens, tokens)], d) for t, d in ((cos_in, cos), (sin_in, sin))]
        )
    ]
    for load in loads:
        load.start()

    doc_weights = [1 << i for i in range(1, log2(n_doc))]
    seq_weights = [1 << i for i in range(log2(n_seq))]
    sibling = (flipped(doc, 1), seq)
    greet(group_partners(doc, seq, n_seq) + [(flipped(doc, w), seq) for w in doc_weights])

    def reduction(src, lanes, part_width, acc, landing, final, sems, turn, out):
        order = doc_weights[turn:] + doc_weights[:turn]
        partners = [sibling] + [(flipped(doc, w), seq) for w in order] + [(doc, flipped(seq, w)) for w in seq_weights]
        weights = [core] + [bit_of(doc, w) for w in order] + [bit_of(seq, w) for w in seq_weights]
        return Reduction(width, src, lanes, part_width, acc, landing, final, sems, partners, weights, out)

    half1, half2 = g1_in.shape[1] // 2, g2.shape[1] // 2
    wa, wc = acc_a.shape[1], acc_c.shape[1]
    red_a = reduction(g1_in, (0, half1), wa, acc_a, land_a, fin_a, (send_a, recv_a, own_sem.at[0]), 0, g1_o)
    red_b = reduction(g1_in, (wa, half1), half1 - wa, acc_b, land_b, fin_b, (send_b, recv_b, own_sem.at[1]), 1, g1_o)
    red_c = reduction(g2, (0, half2), wc, acc_c, land_c, fin_c, (send_c, recv_c, own_sem.at[2]), 0, g2_o)
    red_d = reduction(g2, (wc, half2), half2 - wc, acc_d, land_d, fin_d, (send_d, recv_d, own_sem.at[3]), 1, g2_o)
    first = list(zip(red_a.steps(), red_b.steps()))
    second = list(zip(red_c.steps(), red_d.steps()))
    progress = [0, 0]

    def advance(which):
        for step in (first, second)[which][progress[which]]:
            step()
        progress[which] += 1

    red_a.start()
    red_b.start()
    for load in loads:
        load.wait()

    def attend_back(keys, j, store_k, store_v, accumulate):
        lanes = pl.ds(pl.multiple_of(j * LANES, LANES), LANES)
        q2, do2 = q[:, lanes], do[:, lanes]
        k2, v2 = k[keys, lanes], v[keys, lanes]
        kt = k2.T
        dks, dvs, dqs = [], [], []
        for sub in range(2):
            probs = jnp.exp(nt(one_head(k2, sub), q2) - lse[j, sub : sub + 1, :])
            dprobs = nt(one_head(v2, sub), do2)
            dscores = (probs * (dprobs - dd[j, sub : sub + 1, :])).astype(BF16)
            dvs.append(nn(probs.astype(BF16), do2))
            dks.append(nn(dscores, q2))
            dqs.append(nn(kt[sub * HEAD_DIM : (sub + 1) * HEAD_DIM], dscores))
        low = lane_of(dks[0].shape) < HEAD_DIM
        store_k(j, lanes, jnp.where(low, dks[0], dks[1]))
        store_v(j, lanes, jnp.where(low, dvs[0], dvs[1]))
        accumulate(j, lanes, jnp.concatenate(dqs, axis=0))

    def unrope(tile):
        return (tile * cos[...] - turned(tile) * sin[...]).astype(BF16)

    def far(j, _):
        def store_k(j, lanes, tile):
            away[0, :, lanes] = tile.astype(BF16)

        def store_v(j, lanes, tile):
            away[1, :, lanes] = tile.astype(BF16)

        def accumulate(j, lanes, tile):
            dqt[j] = tile

        attend_back(pl.ds(tokens, tokens), j, store_k, store_v, accumulate)
        return 0

    def near(j, _):
        def store_k(j, lanes, tile):
            own[0, :, lanes] = tile

        def store_v(j, lanes, tile):
            own[1, :, lanes] = tile

        def accumulate(j, lanes, tile):
            dqkv[:, lanes] = unrope((dqt[j] + tile).T * 0.125)

        attend_back(pl.ds(0, tokens), j, store_k, store_v, accumulate)
        return 0

    lax.fori_loop(0, 4, far, 0)
    advance(0)
    lax.fori_loop(4, pairs, far, 0)
    sends = [
        pltpu.make_async_remote_copy(
            src_ref=away.at[i], dst_ref=landed.at[i], send_sem=kv_send.at[i], recv_sem=kv_recv.at[i],
            device_id=sibling, device_id_type=MESH,
        )
        for i in range(2)
    ]
    for send in sends:
        send.start()
    lax.fori_loop(0, pairs, near, 0)
    for send in sends:
        send.wait()

    def join(j, _):
        lanes = pl.ds(pl.multiple_of(j * LANES, LANES), LANES)
        k_lanes = pl.ds(pl.multiple_of(width + j * LANES, LANES), LANES)
        v_lanes = pl.ds(pl.multiple_of(2 * width + j * LANES, LANES), LANES)
        dqkv[:, k_lanes] = unrope(own[0, :, lanes] + landed[0, :, lanes].astype(F32))
        dqkv[:, v_lanes] = (own[1, :, lanes] + landed[1, :, lanes].astype(F32)).astype(BF16)
        return 0

    lax.fori_loop(0, pairs, join, 0)
    advance(0)
    xnt[...] = xn[...].T
    step = 3 * LANES

    def grad_qkv(j, _):
        lanes = pl.ds(pl.multiple_of(j * step, LANES), step)
        g2[:, lanes] = nn(xnt[...], dqkv[:, lanes]).astype(BF16)
        return 0

    lax.fori_loop(0, 3 * width // step, grad_qkv, 0)
    red_c.start()
    red_d.start()
    grad1 = nt(dqkv[...], wqkv[...])
    unit, scale = row_stats(xs[...].astype(F32))
    dx[...] = (dh[...] + norm_back(grad1, unit, scale, gain1[...])).astype(BF16)
    for slot in range(2):
        send_or_keep(
            ex, ex.back_targets[slot], dx.at[pl.ds(slot * rows, rows)],
            dx_o.at[ex.back_block], dx_send.at[slot], dx_recv.at[ex.back_block],
        )
    advance(0)
    advance(1)
    while progress[0] < len(first) or progress[1] < len(second):
        if progress[0] < len(first):
            advance(0)
        if progress[1] < len(second):
            advance(1)
    for block in range(2):
        wait_bytes(dx_o.at[block], dx_recv.at[block])
    for slot in range(2):
        wait_sent(
            ex, ex.back_targets[slot], dx.at[pl.ds(slot * rows, rows)],
            dx_o.at[ex.back_block], dx_send.at[slot], dx_recv.at[ex.back_block],
        )


def back(n_doc, n_seq, shape, x, xn, q, k, v, do, lse, dd, dh, g1, wqkv, gain1, cos, sin):
    tokens, width = x.shape
    pairs = width // LANES
    cols1, cols2 = g1.shape[1], 3 * width
    rounds = log2(n_doc) - 1 + log2(n_seq)
    tall = Reduction.landing_rows(width, rounds)
    wa = cols1 // 2 // LANES // 2 * LANES
    wb = cols1 // 2 - wa
    wc = cols2 // 2 // LANES // 2 * LANES
    wd = cols2 // 2 - wc
    hbm, vmem = pl.BlockSpec(memory_space=pl.ANY), pl.BlockSpec(memory_space=pltpu.VMEM)
    sds = jax.ShapeDtypeStruct
    rounds_sem = pltpu.SemaphoreType.DMA((2 + 2 * rounds,))
    return pl.pallas_call(
        functools.partial(back_kernel, n_doc, n_seq),
        out_shape=[sds(shape, BF16), sds((width, cols1), BF16), sds((width, cols2), BF16)],
        in_specs=[hbm] * 11 + [vmem] + [hbm] * 2,
        out_specs=[hbm] * 3,
        scratch_shapes=[
            pltpu.VMEM((tokens, width), BF16), pltpu.VMEM((tokens, width), BF16), pltpu.VMEM((tokens, width), BF16),
            pltpu.VMEM((2 * tokens, width), BF16), pltpu.VMEM((2 * tokens, width), BF16), pltpu.VMEM((tokens, width), BF16),
            pltpu.VMEM((pairs, 2, tokens), F32), pltpu.VMEM((pairs, 2, tokens), F32), pltpu.VMEM((tokens, width), F32),
            pltpu.VMEM((width, cols2), BF16), pltpu.VMEM((tokens, LANES), F32), pltpu.VMEM((tokens, LANES), F32),
            pltpu.VMEM((tokens, cols2), BF16), pltpu.VMEM((pairs, LANES, tokens), F32),
            pltpu.VMEM((2, tokens, width), BF16), pltpu.VMEM((2, tokens, width), F32), pltpu.VMEM((2, tokens, width), BF16),
            pltpu.VMEM((width, tokens), BF16), pltpu.VMEM((width, cols2), BF16), pltpu.VMEM((tokens, width), BF16),
        ]
        + [pltpu.VMEM((width, w), BF16) for w in (wa, wb, wc, wd)]
        + [pltpu.VMEM((tall, w), BF16) for w in (wa, wb, wc, wd)]
        + [pltpu.VMEM((width, w), BF16) for w in (wa, wb, wc, wd)]
        + [pltpu.SemaphoreType.DMA((12,))]
        + [pltpu.SemaphoreType.DMA((2,))] * 4
        + [rounds_sem] * 8
        + [pltpu.SemaphoreType.DMA((4,))],
        compiler_params=pltpu.CompilerParams(collective_id=1, has_side_effects=True, vmem_limit_bytes=VMEM_LIMIT),
        name="back",
    )(x, xn, q, k, v, do, lse, dd, dh, g1, wqkv, gain1, cos, sin)


def widen_kernel(ff, g1, g2, wqkv, gain1, dqkv_o, dwo_o, dwin_o, dwout_o, gain1_o, gain2_o):
    width = g1.shape[1] - 3 * ff - LANES
    dwout_o[...] = g1[:, :ff].astype(F32).T
    dwin_o[...] = g1[:, ff : 3 * ff].astype(F32)
    dwo_o[...] = g1[:, 3 * ff : 3 * ff + width].astype(F32)
    gain2_o[...] = g1[:, 3 * ff + width :].astype(F32).T[:8]
    dqkv = g2[...].astype(F32)
    dqkv_o[...] = dqkv
    along = jnp.sum(dqkv * wqkv[...].astype(F32), axis=1, keepdims=True)
    gain1_o[...] = jnp.broadcast_to(along, (LANES, LANES)).T[:8] / gain1[...]


def widen(ff, g1, g2, wqkv, gain1):
    width, cols1 = g1.shape
    cols2 = g2.shape[1]
    sds = jax.ShapeDtypeStruct
    across = lambda i: (i, 0)
    down = lambda i: (0, i)
    return pl.pallas_call(
        functools.partial(widen_kernel, ff),
        grid=(width // LANES,),
        out_shape=[
            sds((width, cols2), F32), sds((width, width), F32), sds((width, 2 * ff), F32), sds((ff, width), F32),
            sds((8, width), F32), sds((8, width), F32),
        ],
        in_specs=[
            pl.BlockSpec((LANES, cols1), across), pl.BlockSpec((LANES, cols2), across),
            pl.BlockSpec((LANES, cols2), across), pl.BlockSpec((1, LANES), down),
        ],
        out_specs=[
            pl.BlockSpec((LANES, cols2), across), pl.BlockSpec((LANES, width), across),
            pl.BlockSpec((LANES, 2 * ff), across), pl.BlockSpec((ff, LANES), down),
            pl.BlockSpec((8, LANES), down), pl.BlockSpec((8, LANES), down),
        ],
        compiler_params=pltpu.CompilerParams(vmem_limit_bytes=VMEM_LIMIT),
        name="widen",
    )(g1, g2, wqkv, gain1)


def rotary_tables(length):
    half = HEAD_DIM // 2
    frequency = ROPE_THETA ** (-(np.arange(half) * 2.0) / HEAD_DIM)
    angles = np.arange(length)[:, None] * frequency[None, :]
    cos, sin = np.cos(angles), np.sin(angles)
    per_tile = LANES // HEAD_DIM
    cos = np.tile(np.concatenate([cos, cos], axis=1), (1, per_tile))
    sin = np.tile(np.concatenate([-sin, sin], axis=1), (1, per_tile))
    return jnp.asarray(cos, F32), jnp.asarray(sin, F32)


def per_device(
    n_doc, n_seq,
    inputs, attn_gain, qkv_weight, attn_out_weight, mlp_gain, mlp_in_weight, mlp_out_weight, cotangent,
):
    blocks, rows, width = inputs.shape
    ff = mlp_out_weight.shape[0]
    cos, sin = rotary_tables(rows * n_seq)
    gain1, gain2 = attn_gain[None], mlp_gain[None]
    output, x, xn, q, k, v, do, lse, dd, dh, g1 = front(
        n_seq, inputs, cotangent, gain1, gain2, qkv_weight, attn_out_weight, mlp_in_weight, mlp_out_weight, cos, sin
    )
    dx, g1, g2 = back(
        n_doc, n_seq, inputs.shape, x, xn, q, k, v, do, lse, dd, dh, g1, qkv_weight, gain1, cos, sin
    )
    dqkv, dwo, dwin, dwout, dgain1, dgain2 = widen(ff, g1, g2, qkv_weight, gain1)
    return output, dx, dgain1[0], dqkv, dwo, dgain2[0], dwin, dwout


def solution(mesh):
    n_doc, n_seq = mesh.shape["doc"], mesh.shape["seq"]
    placed = (P("doc", "seq", None), P(), P(), P(), P(), P(), P(), P("doc", "seq", None))
    return jax.shard_map(
        functools.partial(per_device, n_doc, n_seq),
        mesh=mesh,
        in_specs=placed,
        out_specs=(P("doc", "seq", None), P("doc", "seq", None), P(), P(), P(), P(), P(), P()),
        check_vma=False,
    )
```

```python
import functools

import jax
import jax.numpy as jnp
import numpy as np
from jax import lax
from jax.experimental import pallas as pl
from jax.experimental.pallas import tpu as pltpu
from jax.sharding import PartitionSpec as P

HEAD_DIM = 64
ROPE_THETA = 160000.0
NORM_EPSILON = 1e-05
F32 = jnp.float32
BF16 = jnp.bfloat16
MESH = pl.DeviceIdType.MESH
LANES = 128
VMEM_LIMIT = 60 << 20


def nn(a, b):
    return lax.dot_general(a, b, (((1,), (0,)), ((), ())), preferred_element_type=F32)


def nt(a, b):
    return lax.dot_general(a, b, (((1,), (1,)), ((), ())), preferred_element_type=F32)


def lane_of(shape):
    return lax.broadcasted_iota(jnp.int32, shape, 1)


def one_head(pair, sub):
    lane = lane_of(pair.shape)
    mine = (lane < HEAD_DIM) if sub == 0 else (lane >= HEAD_DIM)
    return jnp.where(mine, pair, jnp.zeros_like(pair))


def turned(values):
    back = pltpu.roll(values, HEAD_DIM // 2, 1)
    ahead = pltpu.roll(values, LANES - HEAD_DIM // 2, 1)
    return jnp.where(lane_of(values.shape) % HEAD_DIM < HEAD_DIM // 2, ahead, back)


def row_stats(values):
    mean = jnp.mean(values, axis=1, keepdims=True)
    centered = values - mean
    scale = lax.rsqrt(jnp.mean(centered * centered, axis=1, keepdims=True) + NORM_EPSILON)
    return centered * scale, scale


def norm_back(grad, unit, scale, gain):
    weighted = grad * gain
    along = jnp.mean(weighted, axis=1, keepdims=True)
    across = jnp.mean(weighted * unit, axis=1, keepdims=True)
    return scale * (weighted - along - unit * across)


def bit_of(index, weight):
    return (index // weight) % 2


def flipped(index, weight):
    return index + weight - 2 * weight * bit_of(index, weight)


def greet(partners):
    barrier = pltpu.get_barrier_semaphore()
    for partner in partners:
        pl.semaphore_signal(barrier, inc=1, device_id=partner, device_id_type=MESH)
    pl.semaphore_wait(barrier, len(partners))


def group_partners(doc, seq, n_seq):
    core = doc % 2
    found = []
    for other_core in range(2):
        for step in range(n_seq):
            if other_core == 0 and step == 0:
                continue
            found.append(
                (doc - core + (core + other_core) % 2, (seq + step) % n_seq)
            )
    return found


class Exchange:
    def __init__(self, doc, seq, n_seq):
        core = doc % 2
        half = n_seq // 2
        base = doc - core
        self.out_targets = [(base + seq // half, 2 * core + block) for block in range(2)]
        self.out_slot = seq % half
        self.back_targets = [(base + seq // 2, half * core + slot) for slot in range(2)]
        self.back_block = seq % 2
        self.doc, self.seq = doc, seq

    def is_self(self, target):
        return jnp.logical_and(target[0] == self.doc, target[1] == self.seq)


def send_or_keep(ex, target, src, dst, send_sem, recv_sem):
    mine = ex.is_self(target)

    @pl.when(mine)
    def _():
        pltpu.make_async_copy(src, dst, recv_sem).start()

    @pl.when(jnp.logical_not(mine))
    def _():
        pltpu.make_async_remote_copy(
            src_ref=src, dst_ref=dst, send_sem=send_sem, recv_sem=recv_sem,
            device_id=target, device_id_type=MESH,
        ).start()


def wait_sent(ex, target, src, dst, send_sem, recv_sem):
    @pl.when(jnp.logical_not(ex.is_self(target)))
    def _():
        pltpu.make_async_remote_copy(
            src_ref=src, dst_ref=dst, send_sem=send_sem, recv_sem=recv_sem,
            device_id=target, device_id_type=MESH,
        ).wait_send()


def wait_bytes(ref, sem):
    pltpu.make_async_copy(ref, ref, sem).wait()


LINK_RATE, CORE_RATE, ROUND_LATENCY = 44e3, 500e3, 2.5
STEP_TIME, ADD_TIME = 0.1, 0.4e-6
PIECE_TIME = {"feed": 1.1, "mix": 1.8, "norm": 2.8, "wo": 1.5, "do": 2.0, "far": 1.25, "near": 1.25, "join": 1.8, "dx": 2.2}
FEED_GROUPS = ((0, 2), (2, 4), (4, 6), (6, 8))
FIRST_PAIRS = 4


def log2(n):
    return n.bit_length() - 1


class Stream:
    def __init__(self, first, second, count):
        self.first, self.second, self.count = first, second, count


def halvings(rows, rounds):
    kept, extent = [], rows
    for _ in range(rounds):
        split = (extent // 2) % 16 == 0
        extent = extent // 2 if split else extent
        kept.append((extent, split))
    return kept


def axes_of(n_doc, n_seq):
    doc_axes = [("doc", 1 << i) for i in range(1, log2(n_doc))]
    seq_axes = [("seq", 1 << i) for i in range(log2(n_seq))]
    return doc_axes, seq_axes


def axis_order(index, n_doc, n_seq):
    doc_axes, seq_axes = axes_of(n_doc, n_seq)
    turn = (0, 1, 0, 0, 1, 1)[index % 6] * (len(doc_axes) // 2)
    doc_axes = doc_axes[turn:] + doc_axes[:turn]
    near, far = seq_axes[:-1], seq_axes[-1:]
    return (near + doc_axes if index % 3 == 2 else doc_axes + near) + far


def stream_plan(width, ff):
    ffs, pairs = ff // LANES, width // LANES
    streams, ready = [], {}

    def add(piece, first, second, count):
        ready.setdefault(piece, []).append(len(streams))
        streams.append(Stream(first, second, count))

    for low, high in FEED_GROUPS:
        count = (high - low) // 2
        for base in (0, ffs, 2 * ffs):
            add(("feed", high - 1), base + low, base + low + count, count)
    covered = FEED_GROUPS[-1][1]
    assert ffs - covered == 1 and pairs % 2 == 0
    add(("feed", ffs - 1), covered, ffs + covered, 1)
    add(("norm", 0), 2 * ffs + covered, 3 * ffs + pairs, 1)
    half = pairs // 2
    add(("wo", 0), 3 * ffs, 3 * ffs + half, half)
    base = 3 * ffs + pairs + 1
    for part, (low, high) in enumerate(((0, FIRST_PAIRS), (FIRST_PAIRS, pairs))):
        for third in range(3):
            start, count = base + third * pairs + low, (high - low) // 2
            add(("join", part), start, start + count, count)
    return streams, ready, base + 3 * pairs


def piece_list(ff, pairs):
    ffs = ff // LANES
    pieces = [("feed", j) for j in range(ffs)]
    pieces += [("mix", 0), ("norm", 0), ("wo", 0), ("do", 0)]
    for part, (low, high) in enumerate(((0, FIRST_PAIRS), (FIRST_PAIRS, pairs))):
        pieces += [("far", j) for j in range(low, high)] + [("near", j) for j in range(low, high)]
        pieces.append(("join", part))
    return pieces + [("dx", 0)]


def agenda(streams, ready, pieces, rows, n_doc, n_seq):
    rounds = log2(n_doc) - 1 + log2(n_seq)
    kept = halvings(rows, rounds)
    ups = [r for r in reversed(range(rounds)) if kept[r][1]]
    free, flying, steps = {}, [], {}
    near, far = axes_of(n_doc, n_seq)[1]

    def legs(index):
        order = axis_order(index, n_doc, n_seq)
        unit = streams[index].count * LANES * 2
        trip = [("core", rows * unit)]
        trip += [(order[r], kept[r][0] * unit) for r in range(rounds)]
        trip += [(order[r], kept[r][0] * unit) for r in ups]
        return trip + [("core", rows * unit)]

    def occupy(axis, size, when):
        rate = CORE_RATE if axis == "core" else LINK_RATE / 2 if axis == far else LINK_RATE
        begin = max(when, free.get(axis, 0.0))
        free[axis] = begin + size / rate
        if axis == far:
            free[near] = max(free.get(near, 0.0), begin) + 0.5 * size / LINK_RATE
        return free[axis]

    def depart(index, leg, when):
        flying.append((occupy(*legs(index)[leg], when) + ROUND_LATENCY, index, leg))

    def serve(now):
        flying.sort()
        done, index, leg = flying.pop(0)
        trip = legs(index)
        now = max(now, done) + STEP_TIME + (trip[leg][1] * ADD_TIME if leg <= rounds else 0.0)
        if leg + 1 < len(trip):
            depart(index, leg + 1, now)
        return now, (index, leg)

    now = 0.0
    for piece in pieces:
        now += PIECE_TIME[piece[0]]
        actions = steps.setdefault(piece, [])
        if piece[0] in ("mix", "dx"):
            occupy(far, 393e3, now)
            occupy(near, 200e3, now)
        for index in ready.get(piece, ()):
            actions.append((index, -1))
            depart(index, 0, now)
            now += STEP_TIME
        while flying and min(flying)[0] <= now:
            now, action = serve(now)
            actions.append(action)
    last = steps.setdefault("end", [])
    while flying:
        now, action = serve(now)
        last.append(action)
    return steps


class Reducer:
    def __init__(self, streams, n_doc, n_seq, doc, seq, grads, landing, final, out, send_sem, recv_sem, own_sem):
        self.streams, self.grads, self.landing, self.final, self.out = streams, grads, landing, final, out
        self.send_sem, self.recv_sem, self.own_sem = send_sem, recv_sem, own_sem
        self.core = doc % 2
        self.rows = grads.shape[1]
        self.rounds = log2(n_doc) - 1 + log2(n_seq)
        self.kept = halvings(self.rows, self.rounds)
        self.ups = [r for r in reversed(range(self.rounds)) if self.kept[r][1]]
        self.legs = 2 + self.rounds + len(self.ups)
        self.sibling = (flipped(doc, 1), seq)
        self.bits, self.partners = {}, {}
        for name, weight in sum(axes_of(n_doc, n_seq), []):
            index = doc if name == "doc" else seq
            self.bits[name, weight] = bit_of(index, weight)
            self.partners[name, weight] = (flipped(doc, weight), seq) if name == "doc" else (doc, flipped(seq, weight))
        self.orders = [axis_order(i, n_doc, n_seq) for i in range(len(streams))]
        self.slots, used = [], 0
        for stream in streams:
            self.slots.append(pl.ds(used, stream.count))
            used += stream.count
        self.plans = []
        for order in self.orders:
            offset, base, plan = 0, 0, []
            for (keep, split), axis in zip(self.kept, order):
                bit = self.bits[axis]
                mine = offset + bit * keep if split else offset
                theirs = offset + (1 - bit) * keep if split else offset
                plan.append((mine, theirs, base, keep))
                base += keep
                offset = mine
            self.plans.append(plan)

    @staticmethod
    def landing_rows(rows, rounds):
        return sum(keep for keep, _ in halvings(rows, rounds))

    def tiles(self, index, other=False):
        stream = self.streams[index]
        side = 1 - self.core if other else self.core
        return pl.ds(stream.first + side * (stream.second - stream.first), stream.count)

    def span(self, start, extent):
        return pl.ds(start if isinstance(start, int) else pl.multiple_of(start, 16), extent)

    def copy(self, index, leg, receiving=False):
        slot = self.slots[index]
        if leg == 0:
            src, dst, partner = self.grads.at[self.tiles(index, True)], self.final.at[slot], self.sibling
        elif leg <= self.rounds:
            mine, theirs, base, keep = self.plans[index][leg - 1]
            src = self.grads.at[self.tiles(index), self.span(theirs, keep)]
            dst, partner = self.landing.at[slot, pl.ds(base, keep)], self.partners[self.orders[index][leg - 1]]
        elif leg < self.legs - 1:
            r = self.ups[leg - 1 - self.rounds]
            mine, theirs, base, keep = self.plans[index][r]
            src = dst = self.final.at[slot, self.span(theirs if receiving else mine, keep)]
            partner = self.partners[self.orders[index][r]]
        else:
            src, dst, partner = self.final.at[slot], self.out.at[self.tiles(index, receiving)], self.sibling
        return pltpu.make_async_remote_copy(
            src_ref=src, dst_ref=dst, send_sem=self.send_sem.at[index, leg], recv_sem=self.recv_sem.at[index, leg],
            device_id=partner, device_id_type=MESH,
        )

    def own(self, index):
        return pltpu.make_async_copy(self.final.at[self.slots[index]], self.out.at[self.tiles(index)], self.own_sem.at[index])

    def add(self, index, leg):
        stream, slot = self.streams[index], self.slots[index]
        start = stream.first + self.core * (stream.second - stream.first)
        low = slot.start
        if leg == 0:
            mine, base, keep = 0, 0, self.rows
        else:
            mine, _, base, keep = self.plans[index][leg - 1]
        block = keep
        while block > 96:
            block //= 2

        def body(i, _):
            here = self.span(mine + i * block, block)
            for t in range(stream.count):
                if leg == 0:
                    other = self.final[low + t, here]
                else:
                    other = self.landing[low + t, self.span(base + i * block, block)]
                total = (self.grads[start + t, here].astype(F32) + other.astype(F32)).astype(BF16)
                if leg == self.rounds:
                    self.final[low + t, here] = total
                else:
                    self.grads[start + t, here] = total
            return 0

        lax.fori_loop(0, keep // block, body, 0)

    def act(self, index, leg):
        if leg >= 0:
            self.copy(index, leg).wait_send()
            self.copy(index, leg, True).wait_recv()
            if leg <= self.rounds:
                self.add(index, leg)
            if leg == self.legs - 1:
                self.own(index).wait()
        if leg + 1 < self.legs:
            self.copy(index, leg + 1).start()
        if leg + 1 == self.legs - 1:
            self.own(index).start()


def layer_kernel(
    n_doc, n_seq,
    x_in, cot_in, gain1_in, gain2_in, wqkv_in, wo_in, win_in, wout_in, cos_in, sin_in,
    out_o, dx_o, g_o,
    xs, cs, outs, wqkv, wo, win, wout, cos, sin, xn, q, k, v, att, h, xn2, xn2t, hid, dgu, dmt, do, dh, acc, lse, dd,
    dqt, landed, grads, landing, final,
    w_sem, send_sem, recv_sem, kv_send, kv_recv, sum_send, sum_recv, own_sem,
):
    doc, seq = lax.axis_index("doc"), lax.axis_index("seq")
    core = doc % 2
    ex = Exchange(doc, seq, n_seq)
    rows = x_in.shape[1]
    tokens, width = xs.shape
    ff = wout.shape[0]
    ffs, pairs = ff // LANES, width // LANES
    sibling = (flipped(doc, 1), seq)

    loads = [
        pltpu.make_async_copy(s, d, w_sem.at[i])
        for i, (s, d) in enumerate(
            [(wqkv_in, wqkv), (wo_in, wo), (win_in, win), (wout_in, wout)]
            + [(t.at[pl.ds(core * tokens, tokens)], d) for t, d in ((cos_in, cos), (sin_in, sin))]
        )
    ]
    greet(group_partners(doc, seq, n_seq) + [(flipped(doc, w), seq) for _, w in axes_of(n_doc, n_seq)[0]])

    def spread(src, dst, base, act):
        for block in range(2):
            act(
                ex, ex.out_targets[block], src.at[block], dst.at[pl.ds(ex.out_slot * rows, rows)],
                send_sem.at[base + block], recv_sem.at[base + ex.out_slot],
            )

    def gather(src, dst, base, act):
        for slot in range(2):
            act(
                ex, ex.back_targets[slot], src.at[pl.ds(slot * rows, rows)], dst.at[ex.back_block],
                send_sem.at[base + slot], recv_sem.at[base + ex.back_block],
            )

    spread(x_in, xs, 0, send_or_keep)
    for load in loads:
        load.start()
    gain1, gain2 = gain1_in[...].reshape(1, width), gain2_in[...].reshape(1, width)

    streams, ready, _ = stream_plan(width, ff)
    steps = agenda(streams, ready, piece_list(ff, pairs), width, n_doc, n_seq)
    reducer = Reducer(streams, n_doc, n_seq, doc, seq, grads, landing, final, g_o, sum_send, sum_recv, own_sem)

    def after(piece):
        for action in steps.get(piece, ()):
            reducer.act(*action)

    def loop(name, low, high, body):
        def one(j, _):
            body(j)
            for at in range(low, high):
                if steps.get((name, at)):
                    pl.when(j == at)(functools.partial(after, (name, at)))
            return 0

        lax.fori_loop(low, high, one, 0)

    def tile(j, base=0, count=1):
        return pl.ds(pl.multiple_of(base + j * LANES * count, LANES), LANES * count)

    for slot in range(2):
        wait_bytes(xs.at[pl.ds(slot * rows, rows)], recv_sem.at[slot])
    spread(cot_in, cs, 2, send_or_keep)

    unit, _ = row_stats(xs[...].astype(F32))
    xn[...] = (unit * gain1).astype(BF16)
    for i in (0, 4, 5):
        loads[i].wait()

    def roped(part, scale):
        return ((part * cos[...] + turned(part) * sin[...]) * scale).astype(BF16)

    def project(j, _):
        weights = jnp.concatenate([wqkv[:, tile(j, width)], wqkv[:, tile(j, 2 * width)]], axis=1)
        both = nn(xn[...], weights)
        k[:tokens, tile(j)] = roped(both[:, :LANES], 1.0)
        v[:tokens, tile(j)] = both[:, LANES:].astype(BF16)
        return 0

    lax.fori_loop(0, pairs, project, 0)
    kv_copies = [
        pltpu.make_async_remote_copy(
            src_ref=ref.at[pl.ds(0, tokens)], dst_ref=ref.at[pl.ds(tokens, tokens)],
            send_sem=kv_send.at[i], recv_sem=kv_recv.at[i], device_id=sibling, device_id_type=MESH,
        )
        for i, ref in enumerate((k, v))
    ]
    for copy in kv_copies:
        copy.start()

    def project_q(j, _):
        both = nn(xn[...], wqkv[:, tile(j, 0, 2)])
        for t in range(2):
            q[:, tile(2 * j + t)] = roped(both[:, t * LANES : (t + 1) * LANES], 0.125)
        return 0

    lax.fori_loop(0, pairs // 2, project_q, 0)
    for copy in kv_copies:
        copy.wait()

    def attend(j, _):
        lanes = tile(j)
        k2, vt, q2 = k[:, lanes], v[:, lanes].T, q[:, lanes]
        mixed = []
        for sub in range(2):
            scores = nt(one_head(k2, sub), q2)
            top = jnp.max(scores, axis=0, keepdims=True)
            weights = jnp.exp(scores - top)
            total = jnp.sum(weights, axis=0, keepdims=True)
            lse[j, sub : sub + 1, :] = top + jnp.log(total)
            mixed.append(
                nn(vt[sub * HEAD_DIM : (sub + 1) * HEAD_DIM], weights.astype(BF16)) * (1.0 / total)
            )
        att[:, lanes] = jnp.concatenate(mixed, axis=0).T.astype(BF16)
        return 0

    lax.fori_loop(0, pairs, attend, 0)

    loads[1].wait()
    h[...] = xs[...].astype(F32) + nn(att[...], wo[...])
    unit2, _ = row_stats(h[...])
    xn2[...] = (unit2 * gain2).astype(BF16)
    xn2t[...] = xn2[...].T
    loads[2].wait()
    loads[3].wait()
    for slot in range(2):
        wait_bytes(cs.at[pl.ds(slot * rows, rows)], recv_sem.at[2 + slot])
    dmt[...] = cs[...].T

    def feed(j):
        both = nn(xn2[...], jnp.concatenate([win[:, tile(j)], win[:, tile(j, ff)]], axis=1))
        gate, up = both[:, :LANES], both[:, LANES:]
        phi = 0.5 * (1.0 + lax.erf(gate * 0.7071067811865476))
        slope = phi + gate * (0.3989422804014327 * jnp.exp(-0.5 * gate * gate))
        active = gate * phi
        inner = (active * up).astype(BF16)
        hid[:, tile(j)] = inner
        dhid = nt(cs[...], wout[tile(j), :])
        dgate, dup = (dhid * up * slope).astype(BF16), (dhid * active).astype(BF16)
        dgu[:, tile(j)] = dgate
        dgu[:, tile(j, ff)] = dup
        grads[j] = nn(dmt[...], inner).astype(BF16)
        pair = nn(xn2t[...], jnp.concatenate([dgate, dup], axis=1)).astype(BF16)
        grads[ffs + j] = pair[:, :LANES]
        grads[2 * ffs + j] = pair[:, LANES:]

    loop("feed", 0, ffs, feed)

    outs[...] = (h[...] + nn(hid[...], wout[...])).astype(BF16)
    gather(outs, out_o, 4, send_or_keep)
    after(("mix", 0))

    acc[...] = nt(dgu[...], win[...])
    unit2, scale2 = row_stats(h[...])
    grad2 = acc[...]
    dh[...] = cs[...].astype(F32) + norm_back(grad2, unit2, scale2, gain2)
    gain_terms = (grad2 * unit2).astype(BF16).T
    grads[3 * ffs + pairs] = nn(gain_terms, jnp.ones((tokens, LANES), BF16)).astype(BF16)
    after(("norm", 0))

    datt = dh[...].astype(BF16)
    att_t = att[...].T
    for j in range(pairs // 2):
        both = nn(att_t, datt[:, 2 * j * LANES : (2 * j + 2) * LANES]).astype(BF16)
        for t in range(2):
            grads[3 * ffs + 2 * j + t] = both[:, t * LANES : (t + 1) * LANES]
    after(("wo", 0))

    do[...] = nt(datt, wo[...]).astype(BF16)
    lane = lax.broadcasted_iota(jnp.int32, (8, LANES), 1)
    row = lax.broadcasted_iota(jnp.int32, (8, LANES), 0)
    pick = jnp.where(lane // HEAD_DIM == row, 1.0, 0.0).astype(F32)
    for j in range(pairs):
        lanes = slice(j * LANES, (j + 1) * LANES)
        product = do[:, lanes].astype(F32) * att[:, lanes].astype(F32)
        sums = lax.dot_general(
            pick, product, (((1,), (1,)), ((), ())),
            precision=lax.Precision.HIGHEST, preferred_element_type=F32,
        )
        dd[j] = sums[:2]
    after(("do", 0))

    dqkv, xnt, dx = win.at[pl.ds(0, tokens)], xn2t, do
    away, own = (xn2, att), (h, acc)
    xnt[...] = xn[...].T

    def attend_back(keys, j):
        lanes = tile(j)
        q2, do2 = q[:, lanes], do[:, lanes]
        k2, v2 = k[keys, lanes], v[keys, lanes]
        kt = k2.T
        dks, dvs, dqs = [], [], []
        for sub in range(2):
            probs = jnp.exp(nt(one_head(k2, sub), q2) - lse[j, sub : sub + 1, :])
            dprobs = nt(one_head(v2, sub), do2)
            dscores = (probs * (dprobs - dd[j, sub : sub + 1, :])).astype(BF16)
            dvs.append(nn(probs.astype(BF16), do2))
            dks.append(nn(dscores, q2))
            dqs.append(nn(kt[sub * HEAD_DIM : (sub + 1) * HEAD_DIM], dscores))
        low = lane_of(dks[0].shape) < HEAD_DIM
        return jnp.where(low, dks[0], dks[1]), jnp.where(low, dvs[0], dvs[1]), jnp.concatenate(dqs, axis=0)

    def unrope(part):
        return (part * cos[...] - turned(part) * sin[...]).astype(BF16)

    def far(j):
        dk, dv, dq = attend_back(pl.ds(tokens, tokens), j)
        away[0][:, tile(j)] = dk.astype(BF16)
        away[1][:, tile(j)] = dv.astype(BF16)
        dqt[j] = dq

    def near(j):
        dk, dv, dq = attend_back(pl.ds(0, tokens), j)
        own[0][:, tile(j)] = dk
        own[1][:, tile(j)] = dv
        dqkv[:, tile(j)] = unrope((dqt[j] + dq).T * 0.125)

    def join(j, _):
        dqkv[:, tile(j, width)] = unrope(own[0][:, tile(j)] + landed[0, :, tile(j)].astype(F32))
        dqkv[:, tile(j, 2 * width)] = (own[1][:, tile(j)] + landed[1, :, tile(j)].astype(F32)).astype(BF16)
        return 0

    base = 3 * ffs + pairs + 1
    for part, (low, high) in enumerate(((0, FIRST_PAIRS), (FIRST_PAIRS, pairs))):
        loop("far", low, high, far)
        lanes = pl.ds(low * LANES, (high - low) * LANES)
        sends = [
            pltpu.make_async_remote_copy(
                src_ref=away[i].at[:, lanes], dst_ref=landed.at[i, :, lanes],
                send_sem=kv_send.at[2 + 2 * part + i], recv_sem=kv_recv.at[2 + 2 * part + i],
                device_id=sibling, device_id_type=MESH,
            )
            for i in range(2)
        ]
        for send in sends:
            send.start()
        loop("near", low, high, near)
        for send in sends:
            send.wait()
        lax.fori_loop(low, high, join, 0)

        def weight_grads(j, _):
            for third in range(3):
                both = nn(xnt[...], dqkv[:, tile(j, third * width, 2)]).astype(BF16)
                for t in range(2):
                    grads[base + third * pairs + 2 * j + t] = both[:, t * LANES : (t + 1) * LANES]
            return 0

        lax.fori_loop(low // 2, high // 2, weight_grads, 0)
        after(("join", part))

    grad1 = nt(dqkv[...], wqkv[...])
    unit, scale = row_stats(xs[...].astype(F32))
    dx[...] = (dh[...] + norm_back(grad1, unit, scale, gain1)).astype(BF16)
    gather(dx, dx_o, 6, send_or_keep)
    after(("dx", 0))
    after("end")

    spread(x_in, xs, 0, wait_sent)
    spread(cot_in, cs, 2, wait_sent)
    gather(outs, out_o, 4, wait_sent)
    gather(dx, dx_o, 6, wait_sent)
    for block in range(2):
        wait_bytes(out_o.at[block], recv_sem.at[4 + block])
        wait_bytes(dx_o.at[block], recv_sem.at[6 + block])


def layer(n_doc, n_seq, inputs, cotangent, gain1, gain2, wqkv, wo, win, wout, cos, sin):
    blocks, rows, width = inputs.shape
    tokens = blocks * rows
    ff = wout.shape[0]
    pairs = width // LANES
    streams, _, total = stream_plan(width, ff)
    rounds = log2(n_doc) - 1 + log2(n_seq)
    kept = halvings(width, rounds)
    legs = 2 + rounds + sum(1 for _, split in kept if split)
    slots = sum(stream.count for stream in streams)
    hbm, vmem = pl.BlockSpec(memory_space=pl.ANY), pl.BlockSpec(memory_space=pltpu.VMEM)
    sds, dma = jax.ShapeDtypeStruct, pltpu.SemaphoreType.DMA
    row_b = pltpu.VMEM((tokens, width), BF16)
    row_f = pltpu.VMEM((tokens, width), F32)
    return pl.pallas_call(
        functools.partial(layer_kernel, n_doc, n_seq),
        out_shape=[
            sds((blocks, rows, width), BF16), sds((blocks, rows, width), BF16), sds((total, width, LANES), BF16),
        ],
        in_specs=[hbm, hbm, vmem, vmem] + [hbm] * 6,
        out_specs=[hbm] * 3,
        scratch_shapes=[
            row_b, row_b, row_b,
            pltpu.VMEM(wqkv.shape, BF16), pltpu.VMEM(wo.shape, BF16), pltpu.VMEM(win.shape, BF16), pltpu.VMEM(wout.shape, BF16),
            pltpu.VMEM((tokens, LANES), F32), pltpu.VMEM((tokens, LANES), F32),
            row_b, row_b, pltpu.VMEM((2 * tokens, width), BF16), pltpu.VMEM((2 * tokens, width), BF16),
            row_b, row_f, row_b, pltpu.VMEM((width, tokens), BF16),
            pltpu.VMEM((tokens, ff), BF16), pltpu.VMEM((tokens, 2 * ff), BF16), pltpu.VMEM((width, tokens), BF16),
            row_b, row_f, row_f,
            pltpu.VMEM((pairs, 2, tokens), F32), pltpu.VMEM((pairs, 2, tokens), F32),
            pltpu.VMEM((pairs, LANES, tokens), F32), pltpu.VMEM((2, tokens, width), BF16),
            pltpu.VMEM((total, width, LANES), BF16),
            pltpu.VMEM((slots, Reducer.landing_rows(width, rounds), LANES), BF16),
            pltpu.VMEM((slots, width, LANES), BF16),
            dma((6,)), dma((8,)), dma((8,)), dma((6,)), dma((6,)),
            dma((len(streams), legs)), dma((len(streams), legs)), dma((len(streams),)),
        ],
        compiler_params=pltpu.CompilerParams(collective_id=0, has_side_effects=True, vmem_limit_bytes=VMEM_LIMIT),
        name="layer",
    )(inputs, cotangent, gain1, gain2, wqkv, wo, win, wout, cos, sin)


def widen_kernel(ff, width, g, wqkv, gain1, dqkv_o, dwo_o, dwin_o, dwout_o, gain1_o, gain2_o):
    ffs, pairs = ff // LANES, width // LANES
    base = 3 * ffs + pairs + 1
    for j in range(ffs):
        dwout_o[j * LANES : (j + 1) * LANES, :] = g[j].astype(F32).T
    for j in range(2 * ffs):
        dwin_o[:, j * LANES : (j + 1) * LANES] = g[ffs + j].astype(F32)
    for j in range(pairs):
        dwo_o[:, j * LANES : (j + 1) * LANES] = g[3 * ffs + j].astype(F32)
    gain2_o[...] = g[base - 1].astype(F32).T[0]
    along = jnp.zeros((LANES, LANES), F32)
    for j in range(3 * pairs):
        lanes = slice(j * LANES, (j + 1) * LANES)
        part = g[base + j].astype(F32)
        dqkv_o[:, lanes] = part
        along += part * wqkv[:, lanes].astype(F32)
    total = jnp.sum(along.T, axis=0, keepdims=True)
    gain1_o[...] = (total / gain1[...].reshape(1, LANES))[0]


def widen(ff, g, wqkv, gain1):
    total, width, _ = g.shape
    sds = jax.ShapeDtypeStruct
    across = lambda i: (i, 0)
    down = lambda i: (0, i)
    flat = pl.BlockSpec((LANES,), lambda i: (i,))
    return pl.pallas_call(
        functools.partial(widen_kernel, ff, width),
        grid=(width // LANES,),
        out_shape=[
            sds(wqkv.shape, F32), sds((width, width), F32), sds((width, 2 * ff), F32), sds((ff, width), F32),
            sds((width,), F32), sds((width,), F32),
        ],
        in_specs=[
            pl.BlockSpec((total, LANES, LANES), lambda i: (0, i, 0)), pl.BlockSpec((LANES, wqkv.shape[1]), across), flat,
        ],
        out_specs=[
            pl.BlockSpec((LANES, wqkv.shape[1]), across), pl.BlockSpec((LANES, width), across),
            pl.BlockSpec((LANES, 2 * ff), across), pl.BlockSpec((ff, LANES), down), flat, flat,
        ],
        compiler_params=pltpu.CompilerParams(vmem_limit_bytes=VMEM_LIMIT),
        name="widen",
    )(g, wqkv, gain1)


def rotary_tables(length):
    half = HEAD_DIM // 2
    frequency = ROPE_THETA ** (-(np.arange(half) * 2.0) / HEAD_DIM)
    angles = np.arange(length)[:, None] * frequency[None, :]
    cos, sin = np.cos(angles), np.sin(angles)
    per_tile = LANES // HEAD_DIM
    cos = np.tile(np.concatenate([cos, cos], axis=1), (1, per_tile))
    sin = np.tile(np.concatenate([-sin, sin], axis=1), (1, per_tile))
    return jnp.asarray(cos, F32), jnp.asarray(sin, F32)


def per_device(
    n_doc, n_seq,
    inputs, attn_gain, qkv_weight, attn_out_weight, mlp_gain, mlp_in_weight, mlp_out_weight, cotangent,
):
    blocks, rows, width = inputs.shape
    ff = mlp_out_weight.shape[0]
    cos, sin = rotary_tables(rows * n_seq)
    output, dx, grads = layer(
        n_doc, n_seq, inputs, cotangent, attn_gain, mlp_gain,
        qkv_weight, attn_out_weight, mlp_in_weight, mlp_out_weight, cos, sin,
    )
    dqkv, dwo, dwin, dwout, dgain1, dgain2 = widen(ff, grads, qkv_weight, attn_gain)
    return output, dx, dgain1, dqkv, dwo, dgain2, dwin, dwout


def solution(mesh):
    n_doc, n_seq = mesh.shape["doc"], mesh.shape["seq"]
    placed = (P("doc", "seq", None), P(), P(), P(), P(), P(), P(), P("doc", "seq", None))
    return jax.shard_map(
        functools.partial(per_device, n_doc, n_seq),
        mesh=mesh,
        in_specs=placed,
        out_specs=(P("doc", "seq", None), P("doc", "seq", None), P(), P(), P(), P(), P(), P()),
        check_vma=False,
    )
```

```python
import functools

import jax
import jax.numpy as jnp
import numpy as np
from jax import lax
from jax.experimental import pallas as pl
from jax.experimental.pallas import tpu as pltpu
from jax.sharding import PartitionSpec as P

HEAD_DIM = 64
ROPE_THETA = 160000.0
NORM_EPSILON = 1e-05
F32 = jnp.float32
BF16 = jnp.bfloat16
MESH = pl.DeviceIdType.MESH
LANES = 128
VMEM_LIMIT = 60 << 20


def nn(a, b):
    return lax.dot_general(a, b, (((1,), (0,)), ((), ())), preferred_element_type=F32)


def nt(a, b):
    return lax.dot_general(a, b, (((1,), (1,)), ((), ())), preferred_element_type=F32)


def lane_of(shape):
    return lax.broadcasted_iota(jnp.int32, shape, 1)


def one_head(pair, sub):
    lane = lane_of(pair.shape)
    mine = (lane < HEAD_DIM) if sub == 0 else (lane >= HEAD_DIM)
    return jnp.where(mine, pair, jnp.zeros_like(pair))


def turned(values):
    back = pltpu.roll(values, HEAD_DIM // 2, 1)
    ahead = pltpu.roll(values, LANES - HEAD_DIM // 2, 1)
    return jnp.where(lane_of(values.shape) % HEAD_DIM < HEAD_DIM // 2, ahead, back)


def row_stats(values):
    mean = jnp.mean(values, axis=1, keepdims=True)
    centered = values - mean
    scale = lax.rsqrt(jnp.mean(centered * centered, axis=1, keepdims=True) + NORM_EPSILON)
    return centered * scale, scale


def norm_back(grad, unit, scale, gain):
    weighted = grad * gain
    along = jnp.mean(weighted, axis=1, keepdims=True)
    across = jnp.mean(weighted * unit, axis=1, keepdims=True)
    return scale * (weighted - along - unit * across)


def bit_of(index, weight):
    return (index // weight) % 2


def flipped(index, weight):
    return index + weight - 2 * weight * bit_of(index, weight)


def greet(partners):
    barrier = pltpu.get_barrier_semaphore()
    for partner in partners:
        pl.semaphore_signal(barrier, inc=1, device_id=partner, device_id_type=MESH)
    pl.semaphore_wait(barrier, len(partners))


def group_partners(doc, seq, n_seq):
    core = doc % 2
    found = []
    for other_core in range(2):
        for step in range(n_seq):
            if other_core == 0 and step == 0:
                continue
            found.append(
                (doc - core + (core + other_core) % 2, (seq + step) % n_seq)
            )
    return found


class Exchange:
    def __init__(self, doc, seq, n_seq):
        core = doc % 2
        half = n_seq // 2
        base = doc - core
        self.out_targets = [(base + seq // half, 2 * core + block) for block in range(2)]
        self.out_slot = seq % half
        self.back_targets = [(base + seq // 2, half * core + slot) for slot in range(2)]
        self.back_block = seq % 2
        self.doc, self.seq = doc, seq

    def is_self(self, target):
        return jnp.logical_and(target[0] == self.doc, target[1] == self.seq)


def send_or_keep(ex, target, src, dst, send_sem, recv_sem):
    mine = ex.is_self(target)

    @pl.when(mine)
    def _():
        pltpu.make_async_copy(src, dst, recv_sem).start()

    @pl.when(jnp.logical_not(mine))
    def _():
        pltpu.make_async_remote_copy(
            src_ref=src, dst_ref=dst, send_sem=send_sem, recv_sem=recv_sem,
            device_id=target, device_id_type=MESH,
        ).start()


def wait_sent(ex, target, src, dst, send_sem, recv_sem):
    @pl.when(jnp.logical_not(ex.is_self(target)))
    def _():
        pltpu.make_async_remote_copy(
            src_ref=src, dst_ref=dst, send_sem=send_sem, recv_sem=recv_sem,
            device_id=target, device_id_type=MESH,
        ).wait_send()


def wait_bytes(ref, sem):
    pltpu.make_async_copy(ref, ref, sem).wait()


LINK_RATE, CORE_RATE, ROUND_LATENCY = 41e3, 460e3, 3.0
STEP_TIME, ADD_TIME = 0.1, 0.4e-6
PIECE_TIME = {"feed": 1.1, "mix": 1.2, "norm": 5.0, "wo": 1.0, "do": 2.2, "far": 1.25, "near": 1.25, "join": 2.5, "dx": 4.0}
FEED_GROUPS = ((0, 2), (2, 4), (4, 6), (6, 8))
FIRST_PAIRS = 4
ORDERS = "01001051010101010301054101"


def log2(n):
    return n.bit_length() - 1


class Stream:
    def __init__(self, first, second, count):
        self.first, self.second, self.count = first, second, count


def halvings(rows, rounds):
    kept, extent = [], rows
    for _ in range(rounds):
        split = (extent // 2) % 16 == 0
        extent = extent // 2 if split else extent
        kept.append((extent, split))
    return kept


def axes_of(n_doc, n_seq):
    doc_axes = [("doc", 1 << i) for i in range(1, log2(n_doc))]
    seq_axes = [("seq", 1 << i) for i in range(log2(n_seq))]
    return doc_axes, seq_axes


def axis_order(index, n_doc, n_seq):
    doc_axes, seq_axes = axes_of(n_doc, n_seq)
    code = int(ORDERS[index % len(ORDERS)])
    turn = code % 2 * (len(doc_axes) // 2)
    doc_axes = doc_axes[turn:] + doc_axes[:turn]
    place = len(doc_axes) * (2 - code // 2) // 2
    return doc_axes[:place] + seq_axes[:-1] + doc_axes[place:] + seq_axes[-1:]


def stream_plan(width, ff):
    ffs, pairs = ff // LANES, width // LANES
    streams, ready = [], {}

    def add(piece, first, second, count):
        ready.setdefault(piece, []).append(len(streams))
        streams.append(Stream(first, second, count))

    for low, high in FEED_GROUPS:
        for base in (0, ffs, 2 * ffs):
            add(("feed", high - 1), base + low, base + low + 1, 1)
    covered = FEED_GROUPS[-1][1]
    assert ffs - covered == 1 and pairs % 2 == 0
    add(("feed", ffs - 1), covered, ffs + covered, 1)
    add(("norm", 0), 2 * ffs + covered, 3 * ffs + pairs, 1)
    for start in range(3 * ffs, 3 * ffs + pairs, 2):
        add(("wo", 0), start, start + 1, 1)
    base = 3 * ffs + pairs + 1
    for part, (low, high) in enumerate(((0, FIRST_PAIRS), (FIRST_PAIRS, pairs))):
        for third in range(3):
            for start in range(base + third * pairs + low, base + third * pairs + high, 2):
                add(("join", part), start, start + 1, 1)
    return streams, ready, base + 3 * pairs


def piece_list(ff, pairs):
    ffs = ff // LANES
    pieces = [("feed", j) for j in range(ffs)]
    pieces += [("mix", 0), ("norm", 0), ("wo", 0), ("do", 0)]
    for part, (low, high) in enumerate(((0, FIRST_PAIRS), (FIRST_PAIRS, pairs))):
        pieces += [("far", j) for j in range(low, high)] + [("near", j) for j in range(low, high)]
        pieces.append(("join", part))
    return pieces + [("dx", 0)]


def agenda(streams, ready, pieces, rows, n_doc, n_seq):
    rounds = log2(n_doc) - 1 + log2(n_seq)
    kept = halvings(rows, rounds)
    ups = [r for r in reversed(range(rounds)) if kept[r][1]]
    free, flying, steps = {}, [], {}
    near, far = axes_of(n_doc, n_seq)[1]

    def legs(index):
        order = axis_order(index, n_doc, n_seq)
        unit = streams[index].count * LANES * 2
        trip = [("core", rows * unit)]
        trip += [(order[r], kept[r][0] * unit) for r in range(rounds)]
        trip += [(order[r], kept[r][0] * unit) for r in ups]
        return trip + [("core", rows * unit)]

    def occupy(axis, size, when):
        rate = CORE_RATE if axis == "core" else LINK_RATE / 2 if axis == far else LINK_RATE
        begin = max(when, free.get(axis, 0.0))
        free[axis] = begin + size / rate
        if axis == far:
            free[near] = max(free.get(near, 0.0), begin) + size / LINK_RATE
        return free[axis]

    def depart(index, leg, when):
        flying.append((occupy(*legs(index)[leg], when) + ROUND_LATENCY, index, leg))

    def serve(now):
        flying.sort()
        done, index, leg = flying.pop(0)
        trip = legs(index)
        now = max(now, done) + STEP_TIME + (trip[leg][1] * ADD_TIME if leg <= rounds else 0.0)
        if leg + 1 < len(trip):
            depart(index, leg + 1, now)
        return now, (index, leg)

    now = 0.0
    for piece in pieces:
        now += PIECE_TIME[piece[0]]
        actions = steps.setdefault(piece, [])
        if piece[0] in ("mix", "dx"):
            occupy(far, 393e3, now)
            occupy(near, 200e3, now)
        for index in ready.get(piece, ()):
            actions.append((index, -1))
            depart(index, 0, now)
            now += STEP_TIME
        while flying and min(flying)[0] <= now:
            now, action = serve(now)
            actions.append(action)
    last = steps.setdefault("end", [])
    while flying:
        now, action = serve(now)
        last.append(action)
    return steps


class Reducer:
    def __init__(self, streams, n_doc, n_seq, doc, seq, grads, landing, final, out, send_sem, recv_sem, own_sem):
        self.streams, self.grads, self.landing, self.final, self.out = streams, grads, landing, final, out
        self.send_sem, self.recv_sem, self.own_sem = send_sem, recv_sem, own_sem
        self.core = doc % 2
        self.rows = grads.shape[1]
        self.rounds = log2(n_doc) - 1 + log2(n_seq)
        self.kept = halvings(self.rows, self.rounds)
        self.ups = [r for r in reversed(range(self.rounds)) if self.kept[r][1]]
        self.legs = 2 + self.rounds + len(self.ups)
        self.sibling = (flipped(doc, 1), seq)
        self.bits, self.partners = {}, {}
        for name, weight in sum(axes_of(n_doc, n_seq), []):
            index = doc if name == "doc" else seq
            self.bits[name, weight] = bit_of(index, weight)
            self.partners[name, weight] = (flipped(doc, weight), seq) if name == "doc" else (doc, flipped(seq, weight))
        self.orders = [axis_order(i, n_doc, n_seq) for i in range(len(streams))]
        self.slots, used = [], 0
        for stream in streams:
            self.slots.append(pl.ds(used, stream.count))
            used += stream.count
        self.plans = []
        for order in self.orders:
            offset, base, plan = 0, 0, []
            for (keep, split), axis in zip(self.kept, order):
                bit = self.bits[axis]
                mine = offset + bit * keep if split else offset
                theirs = offset + (1 - bit) * keep if split else offset
                plan.append((mine, theirs, base, keep))
                base += keep
                offset = mine
            self.plans.append(plan)

    @staticmethod
    def landing_rows(rows, rounds):
        return sum(keep for keep, _ in halvings(rows, rounds))

    def tiles(self, index, other=False):
        stream = self.streams[index]
        side = 1 - self.core if other else self.core
        return pl.ds(stream.first + side * (stream.second - stream.first), stream.count)

    def span(self, start, extent):
        return pl.ds(start if isinstance(start, int) else pl.multiple_of(start, 16), extent)

    def copy(self, index, leg, receiving=False):
        slot = self.slots[index]
        if leg == 0:
            src, dst, partner = self.grads.at[self.tiles(index, True)], self.final.at[slot], self.sibling
        elif leg <= self.rounds:
            mine, theirs, base, keep = self.plans[index][leg - 1]
            src = self.grads.at[self.tiles(index), self.span(theirs, keep)]
            dst, partner = self.landing.at[slot, pl.ds(base, keep)], self.partners[self.orders[index][leg - 1]]
        elif leg < self.legs - 1:
            r = self.ups[leg - 1 - self.rounds]
            mine, theirs, base, keep = self.plans[index][r]
            src = dst = self.final.at[slot, self.span(theirs if receiving else mine, keep)]
            partner = self.partners[self.orders[index][r]]
        else:
            src, dst, partner = self.final.at[slot], self.out.at[self.tiles(index, receiving)], self.sibling
        return pltpu.make_async_remote_copy(
            src_ref=src, dst_ref=dst, send_sem=self.send_sem.at[index, leg], recv_sem=self.recv_sem.at[index, leg],
            device_id=partner, device_id_type=MESH,
        )

    def own(self, index):
        return pltpu.make_async_copy(self.final.at[self.slots[index]], self.out.at[self.tiles(index)], self.own_sem.at[index])

    def add(self, index, leg):
        stream, slot = self.streams[index], self.slots[index]
        start = stream.first + self.core * (stream.second - stream.first)
        low = slot.start
        if leg == 0:
            mine, base, keep = 0, 0, self.rows
        else:
            mine, _, base, keep = self.plans[index][leg - 1]
        block = keep
        while block > 96:
            block //= 2

        def body(i, _):
            here = self.span(mine + i * block, block)
            for t in range(stream.count):
                if leg == 0:
                    other = self.final[low + t, here]
                else:
                    other = self.landing[low + t, self.span(base + i * block, block)]
                total = (self.grads[start + t, here].astype(F32) + other.astype(F32)).astype(BF16)
                if leg == self.rounds:
                    self.final[low + t, here] = total
                else:
                    self.grads[start + t, here] = total
            return 0

        lax.fori_loop(0, keep // block, body, 0)

    def act(self, index, leg):
        if leg >= 0:
            self.copy(index, leg).wait_send()
            self.copy(index, leg, True).wait_recv()
            if leg <= self.rounds:
                self.add(index, leg)
            if leg == self.legs - 1:
                self.own(index).wait()
        if leg + 1 < self.legs:
            self.copy(index, leg + 1).start()
        if leg + 1 == self.legs - 1:
            self.own(index).start()


def layer_kernel(
    n_doc, n_seq,
    x_in, cot_in, gain1_in, gain2_in, wqkv_in, wo_in, win_in, wout_in, cos_in, sin_in,
    out_o, dx_o, g_o,
    xs, cs, outs, wqkv, wo, win, wout, cos, sin, xn, q, k, v, att, h, xn2, xn2t, hid, dgu, dmt, do, dh, acc, lse, dd,
    dqt, landed, grads, landing, final,
    w_sem, send_sem, recv_sem, kv_send, kv_recv, sum_send, sum_recv, own_sem,
):
    doc, seq = lax.axis_index("doc"), lax.axis_index("seq")
    core = doc % 2
    ex = Exchange(doc, seq, n_seq)
    rows = x_in.shape[1]
    tokens, width = xs.shape
    ff = wout.shape[0]
    ffs, pairs = ff // LANES, width // LANES
    sibling = (flipped(doc, 1), seq)

    loads = [
        pltpu.make_async_copy(s, d, w_sem.at[i])
        for i, (s, d) in enumerate(
            [(wqkv_in, wqkv), (wo_in, wo), (win_in, win), (wout_in, wout)]
            + [(t.at[pl.ds(core * tokens, tokens)], d) for t, d in ((cos_in, cos), (sin_in, sin))]
        )
    ]
    greet(group_partners(doc, seq, n_seq) + [(flipped(doc, w), seq) for _, w in axes_of(n_doc, n_seq)[0]])

    def spread(src, dst, base, act):
        for block in range(2):
            act(
                ex, ex.out_targets[block], src.at[block], dst.at[pl.ds(ex.out_slot * rows, rows)],
                send_sem.at[base + block], recv_sem.at[base + ex.out_slot],
            )

    def gather(src, dst, base, act):
        for slot in range(2):
            act(
                ex, ex.back_targets[slot], src.at[pl.ds(slot * rows, rows)], dst.at[ex.back_block],
                send_sem.at[base + slot], recv_sem.at[base + ex.back_block],
            )

    spread(x_in, xs, 0, send_or_keep)
    for load in loads:
        load.start()
    gain1, gain2 = gain1_in[...].reshape(1, width), gain2_in[...].reshape(1, width)

    streams, ready, _ = stream_plan(width, ff)
    steps = agenda(streams, ready, piece_list(ff, pairs), width, n_doc, n_seq)
    reducer = Reducer(streams, n_doc, n_seq, doc, seq, grads, landing, final, g_o, sum_send, sum_recv, own_sem)

    def after(piece):
        for action in steps.get(piece, ()):
            reducer.act(*action)

    def loop(name, low, high, body):
        def one(j, _):
            body(j)
            for at in range(low, high):
                if steps.get((name, at)):
                    pl.when(j == at)(functools.partial(after, (name, at)))
            return 0

        lax.fori_loop(low, high, one, 0)

    def tile(j, base=0, count=1):
        return pl.ds(pl.multiple_of(base + j * LANES * count, LANES), LANES * count)

    for slot in range(2):
        here = pl.ds(slot * rows, rows)
        wait_bytes(xs.at[here], recv_sem.at[slot])
        if slot == 1:
            spread(cot_in, cs, 2, send_or_keep)
        unit, _ = row_stats(xs[here].astype(F32))
        xn[here] = (unit * gain1).astype(BF16)
    for i in (0, 4, 5):
        loads[i].wait()

    def roped(part, scale):
        return ((part * cos[...] + turned(part) * sin[...]) * scale).astype(BF16)

    def project(j, _):
        weights = jnp.concatenate([wqkv[:, tile(j, width)], wqkv[:, tile(j, 2 * width)]], axis=1)
        both = nn(xn[...], weights)
        k[:tokens, tile(j)] = roped(both[:, :LANES], 1.0)
        v[:tokens, tile(j)] = both[:, LANES:].astype(BF16)
        return 0

    def kv_copies(group):
        lanes = tile(group, 0, pairs // 2)
        return [
            pltpu.make_async_remote_copy(
                src_ref=ref.at[pl.ds(0, tokens), lanes], dst_ref=ref.at[pl.ds(tokens, tokens), lanes],
                send_sem=kv_send.at[2 * i + group], recv_sem=kv_recv.at[2 * i + group],
                device_id=sibling, device_id_type=MESH,
            )
            for i, ref in enumerate((k, v))
        ]

    for group in range(2):
        lax.fori_loop(group * (pairs // 2), (group + 1) * (pairs // 2), project, 0)
        for copy in kv_copies(group):
            copy.start()

    def project_q(j, _):
        both = nn(xn[...], wqkv[:, tile(j, 0, 2)])
        for t in range(2):
            q[:, tile(2 * j + t)] = roped(both[:, t * LANES : (t + 1) * LANES], 0.125)
        return 0

    lax.fori_loop(0, pairs // 2, project_q, 0)

    def attend(j):
        lanes = tile(j)
        k2, vt, q2 = k[:, lanes], v[:, lanes].T, q[:, lanes]
        mixed = []
        for sub in range(2):
            scores = nt(one_head(k2, sub), q2)
            top = jnp.max(scores, axis=0, keepdims=True)
            weights = jnp.exp(scores - top)
            total = jnp.sum(weights, axis=0, keepdims=True)
            lse[j, sub : sub + 1, :] = top + jnp.log(total)
            mixed.append(
                nn(vt[sub * HEAD_DIM : (sub + 1) * HEAD_DIM], weights.astype(BF16)) * (1.0 / total)
            )
        att[:, lanes] = jnp.concatenate(mixed, axis=0).T.astype(BF16)

    def attend_group(group, _):
        for copy in kv_copies(group):
            copy.wait()
        for j in range(pairs // 2):
            attend(group * (pairs // 2) + j)
        return 0

    lax.fori_loop(0, 2, attend_group, 0)

    loads[1].wait()
    h[...] = xs[...].astype(F32) + nn(att[...], wo[...])
    unit2, _ = row_stats(h[...])
    xn2[...] = (unit2 * gain2).astype(BF16)
    xn2t[...] = xn2[...].T
    loads[2].wait()
    loads[3].wait()
    for slot in range(2):
        wait_bytes(cs.at[pl.ds(slot * rows, rows)], recv_sem.at[2 + slot])
    dmt[...] = cs[...].T

    def feed(j):
        both = nn(xn2[...], jnp.concatenate([win[:, tile(j)], win[:, tile(j, ff)]], axis=1))
        gate, up = both[:, :LANES], both[:, LANES:]
        phi = 0.5 * (1.0 + lax.erf(gate * 0.7071067811865476))
        slope = phi + gate * (0.3989422804014327 * jnp.exp(-0.5 * gate * gate))
        active = gate * phi
        inner = (active * up).astype(BF16)
        hid[:, tile(j)] = inner
        dhid = nt(cs[...], wout[tile(j), :])
        dgate, dup = (dhid * up * slope).astype(BF16), (dhid * active).astype(BF16)
        dgu[:, tile(j)] = dgate
        dgu[:, tile(j, ff)] = dup
        grads[j] = nn(dmt[...], inner).astype(BF16)
        pair = nn(xn2t[...], jnp.concatenate([dgate, dup], axis=1)).astype(BF16)
        grads[ffs + j] = pair[:, :LANES]
        grads[2 * ffs + j] = pair[:, LANES:]

    loop("feed", 0, ffs, feed)

    outs[...] = (h[...] + nn(hid[...], wout[...])).astype(BF16)
    gather(outs, out_o, 4, send_or_keep)
    after(("mix", 0))

    acc[...] = nt(dgu[...], win[...])
    unit2, scale2 = row_stats(h[...])
    grad2 = acc[...]
    dh[...] = cs[...].astype(F32) + norm_back(grad2, unit2, scale2, gain2)
    gain_terms = (grad2 * unit2).astype(BF16).T
    grads[3 * ffs + pairs] = nn(gain_terms, jnp.ones((tokens, LANES), BF16)).astype(BF16)
    after(("norm", 0))

    datt = dh[...].astype(BF16)
    att_t = att[...].T
    for j in range(pairs // 2):
        both = nn(att_t, datt[:, 2 * j * LANES : (2 * j + 2) * LANES]).astype(BF16)
        for t in range(2):
            grads[3 * ffs + 2 * j + t] = both[:, t * LANES : (t + 1) * LANES]
    after(("wo", 0))

    do[...] = nt(datt, wo[...]).astype(BF16)
    lane = lax.broadcasted_iota(jnp.int32, (8, LANES), 1)
    row = lax.broadcasted_iota(jnp.int32, (8, LANES), 0)
    pick = jnp.where(lane // HEAD_DIM == row, 1.0, 0.0).astype(F32)
    for j in range(pairs):
        lanes = slice(j * LANES, (j + 1) * LANES)
        product = do[:, lanes].astype(F32) * att[:, lanes].astype(F32)
        sums = lax.dot_general(
            pick, product, (((1,), (1,)), ((), ())),
            precision=lax.Precision.HIGHEST, preferred_element_type=F32,
        )
        dd[j] = sums[:2]
    after(("do", 0))

    dqkv, xnt, dx = win.at[pl.ds(0, tokens)], xn2t, do
    away, own = (xn2, att), (h, acc)
    xnt[...] = xn[...].T

    def attend_back(keys, j):
        lanes = tile(j)
        q2, do2 = q[:, lanes], do[:, lanes]
        k2, v2 = k[keys, lanes], v[keys, lanes]
        kt = k2.T
        dks, dvs, dqs = [], [], []
        for sub in range(2):
            probs = jnp.exp(nt(one_head(k2, sub), q2) - lse[j, sub : sub + 1, :])
            dprobs = nt(one_head(v2, sub), do2)
            dscores = (probs * (dprobs - dd[j, sub : sub + 1, :])).astype(BF16)
            dvs.append(nn(probs.astype(BF16), do2))
            dks.append(nn(dscores, q2))
            dqs.append(nn(kt[sub * HEAD_DIM : (sub + 1) * HEAD_DIM], dscores))
        low = lane_of(dks[0].shape) < HEAD_DIM
        return jnp.where(low, dks[0], dks[1]), jnp.where(low, dvs[0], dvs[1]), jnp.concatenate(dqs, axis=0)

    def unrope(part):
        return (part * cos[...] - turned(part) * sin[...]).astype(BF16)

    def far(j):
        dk, dv, dq = attend_back(pl.ds(tokens, tokens), j)
        away[0][:, tile(j)] = dk.astype(BF16)
        away[1][:, tile(j)] = dv.astype(BF16)
        dqt[j] = dq

    def near(j):
        dk, dv, dq = attend_back(pl.ds(0, tokens), j)
        own[0][:, tile(j)] = dk
        own[1][:, tile(j)] = dv
        dqkv[:, tile(j)] = unrope((dqt[j] + dq).T * 0.125)

    def join(j, _):
        dqkv[:, tile(j, width)] = unrope(own[0][:, tile(j)] + landed[0, :, tile(j)].astype(F32))
        dqkv[:, tile(j, 2 * width)] = (own[1][:, tile(j)] + landed[1, :, tile(j)].astype(F32)).astype(BF16)
        return 0

    base = 3 * ffs + pairs + 1
    for part, (low, high) in enumerate(((0, FIRST_PAIRS), (FIRST_PAIRS, pairs))):
        loop("far", low, high, far)
        lanes = pl.ds(low * LANES, (high - low) * LANES)
        sends = [
            pltpu.make_async_remote_copy(
                src_ref=away[i].at[:, lanes], dst_ref=landed.at[i, :, lanes],
                send_sem=kv_send.at[4 + 2 * part + i], recv_sem=kv_recv.at[4 + 2 * part + i],
                device_id=sibling, device_id_type=MESH,
            )
            for i in range(2)
        ]
        for send in sends:
            send.start()
        loop("near", low, high, near)
        for send in sends:
            send.wait()
        lax.fori_loop(low, high, join, 0)

        def weight_grads(j, _):
            for third in range(3):
                both = nn(xnt[...], dqkv[:, tile(j, third * width, 2)]).astype(BF16)
                for t in range(2):
                    grads[base + third * pairs + 2 * j + t] = both[:, t * LANES : (t + 1) * LANES]
            return 0

        lax.fori_loop(low // 2, high // 2, weight_grads, 0)
        after(("join", part))

    grad1 = nt(dqkv[...], wqkv[...])
    unit, scale = row_stats(xs[...].astype(F32))
    dx[...] = (dh[...] + norm_back(grad1, unit, scale, gain1)).astype(BF16)
    gather(dx, dx_o, 6, send_or_keep)
    after(("dx", 0))
    after("end")

    spread(x_in, xs, 0, wait_sent)
    spread(cot_in, cs, 2, wait_sent)
    gather(outs, out_o, 4, wait_sent)
    gather(dx, dx_o, 6, wait_sent)
    for block in range(2):
        wait_bytes(out_o.at[block], recv_sem.at[4 + block])
        wait_bytes(dx_o.at[block], recv_sem.at[6 + block])


def layer(n_doc, n_seq, inputs, cotangent, gain1, gain2, wqkv, wo, win, wout, cos, sin):
    blocks, rows, width = inputs.shape
    tokens = blocks * rows
    ff = wout.shape[0]
    pairs = width // LANES
    streams, _, total = stream_plan(width, ff)
    rounds = log2(n_doc) - 1 + log2(n_seq)
    kept = halvings(width, rounds)
    legs = 2 + rounds + sum(1 for _, split in kept if split)
    slots = sum(stream.count for stream in streams)
    hbm, vmem = pl.BlockSpec(memory_space=pl.ANY), pl.BlockSpec(memory_space=pltpu.VMEM)
    sds, dma = jax.ShapeDtypeStruct, pltpu.SemaphoreType.DMA
    row_b = pltpu.VMEM((tokens, width), BF16)
    row_f = pltpu.VMEM((tokens, width), F32)
    return pl.pallas_call(
        functools.partial(layer_kernel, n_doc, n_seq),
        out_shape=[
            sds((blocks, rows, width), BF16), sds((blocks, rows, width), BF16), sds((total, width, LANES), BF16),
        ],
        in_specs=[hbm, hbm, vmem, vmem] + [hbm] * 6,
        out_specs=[hbm] * 3,
        scratch_shapes=[
            row_b, row_b, row_b,
            pltpu.VMEM(wqkv.shape, BF16), pltpu.VMEM(wo.shape, BF16), pltpu.VMEM(win.shape, BF16), pltpu.VMEM(wout.shape, BF16),
            pltpu.VMEM((tokens, LANES), F32), pltpu.VMEM((tokens, LANES), F32),
            row_b, row_b, pltpu.VMEM((2 * tokens, width), BF16), pltpu.VMEM((2 * tokens, width), BF16),
            row_b, row_f, row_b, pltpu.VMEM((width, tokens), BF16),
            pltpu.VMEM((tokens, ff), BF16), pltpu.VMEM((tokens, 2 * ff), BF16), pltpu.VMEM((width, tokens), BF16),
            row_b, row_f, row_f,
            pltpu.VMEM((pairs, 2, tokens), F32), pltpu.VMEM((pairs, 2, tokens), F32),
            pltpu.VMEM((pairs, LANES, tokens), F32), pltpu.VMEM((2, tokens, width), BF16),
            pltpu.VMEM((total, width, LANES), BF16),
            pltpu.VMEM((slots, Reducer.landing_rows(width, rounds), LANES), BF16),
            pltpu.VMEM((slots, width, LANES), BF16),
            dma((6,)), dma((8,)), dma((8,)), dma((8,)), dma((8,)),
            dma((len(streams), legs)), dma((len(streams), legs)), dma((len(streams),)),
        ],
        compiler_params=pltpu.CompilerParams(collective_id=0, has_side_effects=True, vmem_limit_bytes=VMEM_LIMIT),
        name="layer",
    )(inputs, cotangent, gain1, gain2, wqkv, wo, win, wout, cos, sin)


def widen_kernel(ff, width, g, wqkv, gain1, out, dx, dqkv_o, dwo_o, dwin_o, dwout_o, gain1_o, gain2_o, out_o, dx_o):
    out_o[...] = out[...]
    dx_o[...] = dx[...]
    ffs, pairs = ff // LANES, width // LANES
    base = 3 * ffs + pairs + 1
    for j in range(ffs):
        dwout_o[j * LANES : (j + 1) * LANES, :] = g[j].astype(F32).T
    for j in range(2 * ffs):
        dwin_o[:, j * LANES : (j + 1) * LANES] = g[ffs + j].astype(F32)
    for j in range(pairs):
        dwo_o[:, j * LANES : (j + 1) * LANES] = g[3 * ffs + j].astype(F32)
    gain2_o[...] = g[base - 1].astype(F32).T[0]
    along = jnp.zeros((LANES, LANES), F32)
    for j in range(3 * pairs):
        lanes = slice(j * LANES, (j + 1) * LANES)
        part = g[base + j].astype(F32)
        dqkv_o[:, lanes] = part
        along += part * wqkv[:, lanes].astype(F32)
    total = jnp.sum(along.T, axis=0, keepdims=True)
    gain1_o[...] = (total / gain1[...].reshape(1, LANES))[0]


def widen(ff, g, wqkv, gain1, out, dx):
    total, width, _ = g.shape
    sds = jax.ShapeDtypeStruct
    across = lambda i: (i, 0)
    down = lambda i: (0, i)
    flat = pl.BlockSpec((LANES,), lambda i: (i,))
    blocks, rows, _ = out.shape
    token = pl.BlockSpec((blocks, rows, LANES), lambda i: (0, 0, i))
    return pl.pallas_call(
        functools.partial(widen_kernel, ff, width),
        grid=(width // LANES,),
        out_shape=[
            sds(wqkv.shape, F32), sds((width, width), F32), sds((width, 2 * ff), F32), sds((ff, width), F32),
            sds((width,), F32), sds((width,), F32), sds(out.shape, BF16), sds(dx.shape, BF16),
        ],
        in_specs=[
            pl.BlockSpec((total, LANES, LANES), lambda i: (0, i, 0)), pl.BlockSpec((LANES, wqkv.shape[1]), across), flat, token, token,
        ],
        out_specs=[
            pl.BlockSpec((LANES, wqkv.shape[1]), across), pl.BlockSpec((LANES, width), across),
            pl.BlockSpec((LANES, 2 * ff), across), pl.BlockSpec((ff, LANES), down), flat, flat, token, token,
        ],
        compiler_params=pltpu.CompilerParams(vmem_limit_bytes=VMEM_LIMIT),
        name="widen",
    )(g, wqkv, gain1, out, dx)


def rotary_tables(length):
    half = HEAD_DIM // 2
    frequency = ROPE_THETA ** (-(np.arange(half) * 2.0) / HEAD_DIM)
    angles = np.arange(length)[:, None] * frequency[None, :]
    cos, sin = np.cos(angles), np.sin(angles)
    per_tile = LANES // HEAD_DIM
    cos = np.tile(np.concatenate([cos, cos], axis=1), (1, per_tile))
    sin = np.tile(np.concatenate([-sin, sin], axis=1), (1, per_tile))
    return jnp.asarray(cos, F32), jnp.asarray(sin, F32)


def per_device(
    n_doc, n_seq,
    inputs, attn_gain, qkv_weight, attn_out_weight, mlp_gain, mlp_in_weight, mlp_out_weight, cotangent,
):
    blocks, rows, width = inputs.shape
    ff = mlp_out_weight.shape[0]
    cos, sin = rotary_tables(rows * n_seq)
    output, dx, grads = layer(
        n_doc, n_seq, inputs, cotangent, attn_gain, mlp_gain,
        qkv_weight, attn_out_weight, mlp_in_weight, mlp_out_weight, cos, sin,
    )
    dqkv, dwo, dwin, dwout, dgain1, dgain2, output, dx = widen(ff, grads, qkv_weight, attn_gain, output, dx)
    return output, dx, dgain1, dqkv, dwo, dgain2, dwin, dwout


def solution(mesh):
    n_doc, n_seq = mesh.shape["doc"], mesh.shape["seq"]
    placed = (P("doc", "seq", None), P(), P(), P(), P(), P(), P(), P("doc", "seq", None))
    return jax.shard_map(
        functools.partial(per_device, n_doc, n_seq),
        mesh=mesh,
        in_specs=placed,
        out_specs=(P("doc", "seq", None), P("doc", "seq", None), P(), P(), P(), P(), P(), P()),
        check_vma=False,
    )
```

```python
import functools

import jax
import jax.numpy as jnp
import numpy as np
from jax import lax
from jax.experimental import pallas as pl
from jax.experimental.pallas import tpu as pltpu
from jax.sharding import PartitionSpec as P

HEAD_DIM = 64
ROPE_THETA = 160000.0
NORM_EPSILON = 1e-05
F32 = jnp.float32
BF16 = jnp.bfloat16
MESH = pl.DeviceIdType.MESH
LANES = 128
VMEM_LIMIT = 60 << 20


def nn(a, b):
    return lax.dot_general(a, b, (((1,), (0,)), ((), ())), preferred_element_type=F32)


def nt(a, b):
    return lax.dot_general(a, b, (((1,), (1,)), ((), ())), preferred_element_type=F32)


def lane_of(shape):
    return lax.broadcasted_iota(jnp.int32, shape, 1)


def one_head(pair, sub):
    lane = lane_of(pair.shape)
    mine = (lane < HEAD_DIM) if sub == 0 else (lane >= HEAD_DIM)
    return jnp.where(mine, pair, jnp.zeros_like(pair))


def turned(values):
    back = pltpu.roll(values, HEAD_DIM // 2, 1)
    ahead = pltpu.roll(values, LANES - HEAD_DIM // 2, 1)
    return jnp.where(lane_of(values.shape) % HEAD_DIM < HEAD_DIM // 2, ahead, back)


def row_stats(values):
    mean = jnp.mean(values, axis=1, keepdims=True)
    centered = values - mean
    scale = lax.rsqrt(jnp.mean(centered * centered, axis=1, keepdims=True) + NORM_EPSILON)
    return centered * scale, scale


def norm_back(grad, unit, scale, gain):
    weighted = grad * gain
    along = jnp.mean(weighted, axis=1, keepdims=True)
    across = jnp.mean(weighted * unit, axis=1, keepdims=True)
    return scale * (weighted - along - unit * across)


def bit_of(index, weight):
    return (index // weight) % 2


def flipped(index, weight):
    return index + weight - 2 * weight * bit_of(index, weight)


def greet(partners):
    barrier = pltpu.get_barrier_semaphore()
    for partner in partners:
        pl.semaphore_signal(barrier, inc=1, device_id=partner, device_id_type=MESH)
    pl.semaphore_wait(barrier, len(partners))


def group_partners(doc, seq, n_seq):
    core = doc % 2
    found = []
    for other_core in range(2):
        for step in range(n_seq):
            if other_core == 0 and step == 0:
                continue
            found.append(
                (doc - core + (core + other_core) % 2, (seq + step) % n_seq)
            )
    return found


class Exchange:
    def __init__(self, doc, seq, n_seq):
        assert n_seq == 4
        core = doc % 2
        self.doc, self.seq, self.core = doc, seq, core
        self.base = doc - core
        side = seq // 2
        self.near_first = [seq, flipped(seq, 1), 2 - side, 3 - 3 * side]
        self.block_first = (1 - core) * side

    def out_piece(self, n):
        block = self.block_first + n // 2 - 2 * self.block_first * (n // 2)
        half = n % 2
        return block, half, (self.base + half, 2 * self.core + block)

    def back_target(self, quarter):
        return (self.base + self.seq // 2, quarter)

    def is_self(self, target):
        return jnp.logical_and(target[0] == self.doc, target[1] == self.seq)


def send_or_keep(ex, target, src, dst, send_sem, recv_sem):
    mine = ex.is_self(target)

    @pl.when(mine)
    def _():
        pltpu.make_async_copy(src, dst, recv_sem).start()

    @pl.when(jnp.logical_not(mine))
    def _():
        pltpu.make_async_remote_copy(
            src_ref=src, dst_ref=dst, send_sem=send_sem, recv_sem=recv_sem,
            device_id=target, device_id_type=MESH,
        ).start()


def wait_sent(ex, target, src, dst, send_sem, recv_sem):
    @pl.when(jnp.logical_not(ex.is_self(target)))
    def _():
        pltpu.make_async_remote_copy(
            src_ref=src, dst_ref=dst, send_sem=send_sem, recv_sem=recv_sem,
            device_id=target, device_id_type=MESH,
        ).wait_send()


def wait_bytes(ref, sem):
    pltpu.make_async_copy(ref, ref, sem).wait()


LINK_RATE, CORE_RATE, ROUND_LATENCY = 42.3e3, 474e3, 3.0
STEP_TIME, ADD_TIME = 0.1, 0.4e-6
PIECE_TIME = {"feed": 1.1, "mix": 1.2, "norm": 5.0, "wo": 1.0, "do": 2.2, "far": 1.25, "near": 1.25, "join": 2.5, "dx": 4.0}
FEED_GROUPS = ((0, 2), (2, 4), (4, 6), (6, 8))
FIRST_PAIRS = 4
ORDERS = "10304211011410131011330222"
OUT, DX = -1, -2
OUT_AFTER, DX_GAP = (9, 9, 9, 12), 12.0


def log2(n):
    return n.bit_length() - 1


class Stream:
    def __init__(self, first, second, count):
        self.first, self.second, self.count = first, second, count


def halvings(rows, rounds):
    kept, extent = [], rows
    for _ in range(rounds):
        split = (extent // 2) % 16 == 0
        extent = extent // 2 if split else extent
        kept.append((extent, split))
    return kept


def axes_of(n_doc, n_seq):
    doc_axes = [("doc", 1 << i) for i in range(1, log2(n_doc))]
    seq_axes = [("seq", 1 << i) for i in range(log2(n_seq))]
    return doc_axes, seq_axes


def axis_order(index, n_doc, n_seq):
    doc_axes, seq_axes = axes_of(n_doc, n_seq)
    code = int(ORDERS[index % len(ORDERS)])
    turn = code % 2 * (len(doc_axes) // 2)
    doc_axes = doc_axes[turn:] + doc_axes[:turn]
    place = len(doc_axes) * (2 - code // 2) // 2
    return doc_axes[:place] + seq_axes[:-1] + doc_axes[place:] + seq_axes[-1:]


def stream_plan(width, ff):
    ffs, pairs = ff // LANES, width // LANES
    streams, ready = [], {}

    def add(piece, first, second, count):
        ready.setdefault(piece, []).append(len(streams))
        streams.append(Stream(first, second, count))

    for low, high in FEED_GROUPS:
        for base in (0, ffs, 2 * ffs):
            add(("feed", high - 1), base + low, base + low + 1, 1)
    covered = FEED_GROUPS[-1][1]
    assert ffs - covered == 1 and pairs % 2 == 0
    add(("feed", ffs - 1), covered, ffs + covered, 1)
    add(("norm", 0), 2 * ffs + covered, 3 * ffs + pairs, 1)
    for start in range(3 * ffs, 3 * ffs + pairs, 2):
        add(("wo", 0), start, start + 1, 1)
    base = 3 * ffs + pairs + 1
    for part, (low, high) in enumerate(((0, FIRST_PAIRS), (FIRST_PAIRS, pairs))):
        for third in range(3):
            for start in range(base + third * pairs + low, base + third * pairs + high, 2):
                add(("join", part), start, start + 1, 1)
    return streams, ready, base + 3 * pairs


def piece_list(ff, pairs):
    ffs = ff // LANES
    pieces = [("feed", j) for j in range(ffs)]
    pieces += [("mix", 0), ("norm", 0), ("wo", 0), ("do", 0)]
    for part, (low, high) in enumerate(((0, FIRST_PAIRS), (FIRST_PAIRS, pairs))):
        pieces += [("far", j) for j in range(low, high)] + [("near", j) for j in range(low, high)]
        pieces.append(("join", part))
    return pieces + [("dx", 0)]


def agenda(streams, ready, pieces, rows, n_doc, n_seq):
    rounds = log2(n_doc) - 1 + log2(n_seq)
    kept = halvings(rows, rounds)
    ups = [r for r in reversed(range(rounds)) if kept[r][1]]
    free, flying, steps = {}, [], {}
    near, far = axes_of(n_doc, n_seq)[1]

    def legs(index):
        order = axis_order(index, n_doc, n_seq)
        unit = streams[index].count * LANES * 2
        trip = [("core", rows * unit)]
        trip += [(order[r], kept[r][0] * unit) for r in range(rounds)]
        trip += [(order[r], kept[r][0] * unit) for r in ups]
        return trip + [("core", rows * unit)]

    def occupy(axis, size, when):
        rate = CORE_RATE if axis == "core" else LINK_RATE / 2 if axis == far else LINK_RATE
        begin = max(when, free.get(axis, 0.0))
        free[axis] = begin + size / rate
        if axis == far:
            free[near] = max(free.get(near, 0.0), begin) + size / LINK_RATE
        return free[axis]

    def leave(chunk, when):
        if chunk:
            occupy(near if chunk == 1 else far, 196e3, when)

    def depart(index, leg, when):
        flying.append((occupy(*legs(index)[leg], when) + ROUND_LATENCY, index, leg))

    def serve(now):
        flying.sort()
        done, index, leg = flying.pop(0)
        trip = legs(index)
        now = max(now, done) + STEP_TIME + (trip[leg][1] * ADD_TIME if leg <= rounds else 0.0)
        if leg + 1 < len(trip):
            depart(index, leg + 1, now)
        return now, (index, leg)

    now = 0.0
    for piece in pieces:
        now += PIECE_TIME[piece[0]]
        actions = steps.setdefault(piece, [])
        for index in ready.get(piece, ()):
            actions.append((index, -1))
            depart(index, 0, now)
            now += STEP_TIME
        for chunk, place in enumerate(OUT_AFTER):
            if piece == pieces[place]:
                actions.append((OUT, chunk))
                leave(chunk, now)
                now += STEP_TIME
        while flying and min(flying)[0] <= now:
            now, action = serve(now)
            actions.append(action)
    last = steps.setdefault("end", [])
    begin, chunk = now, 0
    while flying or chunk < n_seq:
        upcoming = max(now, min(flying)[0]) if flying else now
        if chunk < n_seq and (not flying or upcoming >= begin + chunk * DX_GAP):
            leave(chunk, now)
            last.append((DX, chunk))
            now += STEP_TIME
            chunk += 1
            continue
        now, action = serve(now)
        last.append(action)
    return steps


class Reducer:
    def __init__(self, streams, n_doc, n_seq, doc, seq, grads, landing, final, out, send_sem, recv_sem, own_sem):
        self.streams, self.grads, self.landing, self.final, self.out = streams, grads, landing, final, out
        self.send_sem, self.recv_sem, self.own_sem = send_sem, recv_sem, own_sem
        self.core = doc % 2
        self.rows = grads.shape[1]
        self.rounds = log2(n_doc) - 1 + log2(n_seq)
        self.kept = halvings(self.rows, self.rounds)
        self.ups = [r for r in reversed(range(self.rounds)) if self.kept[r][1]]
        self.legs = 2 + self.rounds + len(self.ups)
        self.sibling = (flipped(doc, 1), seq)
        self.bits, self.partners = {}, {}
        for name, weight in sum(axes_of(n_doc, n_seq), []):
            index = doc if name == "doc" else seq
            self.bits[name, weight] = bit_of(index, weight)
            self.partners[name, weight] = (flipped(doc, weight), seq) if name == "doc" else (doc, flipped(seq, weight))
        self.orders = [axis_order(i, n_doc, n_seq) for i in range(len(streams))]
        self.slots, used = [], 0
        for stream in streams:
            self.slots.append(pl.ds(used, stream.count))
            used += stream.count
        self.plans = []
        for order in self.orders:
            offset, base, plan = 0, 0, []
            for (keep, split), axis in zip(self.kept, order):
                bit = self.bits[axis]
                mine = offset + bit * keep if split else offset
                theirs = offset + (1 - bit) * keep if split else offset
                plan.append((mine, theirs, base, keep))
                base += keep
                offset = mine
            self.plans.append(plan)

    @staticmethod
    def landing_rows(rows, rounds):
        return sum(keep for keep, _ in halvings(rows, rounds))

    def tiles(self, index, other=False):
        stream = self.streams[index]
        side = 1 - self.core if other else self.core
        return pl.ds(stream.first + side * (stream.second - stream.first), stream.count)

    def span(self, start, extent):
        return pl.ds(start if isinstance(start, int) else pl.multiple_of(start, 16), extent)

    def copy(self, index, leg, receiving=False):
        slot = self.slots[index]
        if leg == 0:
            src, dst, partner = self.grads.at[self.tiles(index, True)], self.final.at[slot], self.sibling
        elif leg <= self.rounds:
            mine, theirs, base, keep = self.plans[index][leg - 1]
            src = self.grads.at[self.tiles(index), self.span(theirs, keep)]
            dst, partner = self.landing.at[slot, pl.ds(base, keep)], self.partners[self.orders[index][leg - 1]]
        elif leg < self.legs - 1:
            r = self.ups[leg - 1 - self.rounds]
            mine, theirs, base, keep = self.plans[index][r]
            src = dst = self.final.at[slot, self.span(theirs if receiving else mine, keep)]
            partner = self.partners[self.orders[index][r]]
        else:
            src, dst, partner = self.final.at[slot], self.out.at[self.tiles(index, receiving)], self.sibling
        return pltpu.make_async_remote_copy(
            src_ref=src, dst_ref=dst, send_sem=self.send_sem.at[index, leg], recv_sem=self.recv_sem.at[index, leg],
            device_id=partner, device_id_type=MESH,
        )

    def own(self, index):
        return pltpu.make_async_copy(self.final.at[self.slots[index]], self.out.at[self.tiles(index)], self.own_sem.at[index])

    def add(self, index, leg):
        stream, slot = self.streams[index], self.slots[index]
        start = stream.first + self.core * (stream.second - stream.first)
        low = slot.start
        if leg == 0:
            mine, base, keep = 0, 0, self.rows
        else:
            mine, _, base, keep = self.plans[index][leg - 1]
        block = keep
        while block > 96:
            block //= 2

        def body(i, _):
            here = self.span(mine + i * block, block)
            for t in range(stream.count):
                if leg == 0:
                    other = self.final[low + t, here]
                else:
                    other = self.landing[low + t, self.span(base + i * block, block)]
                total = (self.grads[start + t, here].astype(F32) + other.astype(F32)).astype(BF16)
                if leg == self.rounds:
                    self.final[low + t, here] = total
                else:
                    self.grads[start + t, here] = total
            return 0

        lax.fori_loop(0, keep // block, body, 0)

    def act(self, index, leg):
        if leg >= 0:
            self.copy(index, leg).wait_send()
            self.copy(index, leg, True).wait_recv()
            if leg <= self.rounds:
                self.add(index, leg)
            if leg == self.legs - 1:
                self.own(index).wait()
        if leg + 1 < self.legs:
            self.copy(index, leg + 1).start()
        if leg + 1 == self.legs - 1:
            self.own(index).start()


def layer_kernel(
    n_doc, n_seq,
    x_in, cot_in, gain1_in, gain2_in, wqkv_in, wo_in, win_in, wout_in, cos_in, sin_in,
    out_o, dx_o, g_o,
    xs, cs, outs, wqkv, wo, win, wout, cos, sin, xn, q, k, v, att, h, xn2, xn2t, hid, dgu, dmt, do, dh, acc, lse, dd,
    dqt, landed, grads, landing, final,
    w_sem, send_sem, recv_sem, kv_send, kv_recv, sum_send, sum_recv, own_sem,
):
    doc, seq = lax.axis_index("doc"), lax.axis_index("seq")
    core = doc % 2
    ex = Exchange(doc, seq, n_seq)
    half = x_in.shape[1] // 2
    tokens, width = xs.shape
    ff = wout.shape[0]
    ffs, pairs = ff // LANES, width // LANES
    sibling = (flipped(doc, 1), seq)

    loads = [
        pltpu.make_async_copy(s, d, w_sem.at[i])
        for i, (s, d) in enumerate(
            [(wqkv_in, wqkv), (wo_in, wo), (win_in, win), (wout_in, wout)]
            + [
                (t.at[pl.ds((2 * quarter + core) * half, half)], d.at[pl.ds(quarter * half, half)])
                for t, d in ((cos_in, cos), (sin_in, sin))
                for quarter in range(n_seq)
            ]
        )
    ]
    loads[0].start()
    for load in loads[4:]:
        load.start()
    greet(group_partners(doc, seq, n_seq) + [(flipped(doc, w), seq) for _, w in axes_of(n_doc, n_seq)[0]])

    def rows_of(slot):
        return pl.ds(pl.multiple_of(slot * half, half), half)

    def spread(src, dst, base, act):
        for n in range(n_seq):
            block, part, target = ex.out_piece(n)
            act(
                ex, target, src.at[block, pl.ds(part * half, half)], dst.at[rows_of(seq)],
                send_sem.at[base + n], recv_sem.at[base + seq],
            )

    def gather(src, dst, base, n, act):
        quarter = ex.near_first[n]
        act(
            ex, ex.back_target(quarter), src.at[rows_of(quarter)], dst.at[seq % 2, rows_of(core)],
            send_sem.at[base + n], recv_sem.at[base + 2 * (seq % 2) + core],
        )

    spread(x_in, xs, 0, send_or_keep)
    for load in loads[1:4]:
        load.start()
    gain1, gain2 = gain1_in[...].reshape(1, width), gain2_in[...].reshape(1, width)

    streams, ready, _ = stream_plan(width, ff)
    steps = agenda(streams, ready, piece_list(ff, pairs), width, n_doc, n_seq)
    reducer = Reducer(streams, n_doc, n_seq, doc, seq, grads, landing, final, g_o, sum_send, sum_recv, own_sem)

    def after(piece):
        for index, leg in steps.get(piece, ()):
            if index == OUT:
                gather(outs, out_o, 8, leg, send_or_keep)
            elif index == DX:
                gather(do, dx_o, 12, leg, send_or_keep)
            else:
                reducer.act(index, leg)

    def loop(name, low, high, body):
        def one(j, _):
            body(j)
            for at in range(low, high):
                if steps.get((name, at)):
                    pl.when(j == at)(functools.partial(after, (name, at)))
            return 0

        lax.fori_loop(low, high, one, 0)

    def tile(j, base=0, count=1):
        return pl.ds(pl.multiple_of(base + j * LANES * count, LANES), LANES * count)

    def roped(part, here, scale):
        return ((part * cos[here] + turned(part) * sin[here]) * scale).astype(BF16)

    def kv_copies(n):
        here = rows_of(ex.near_first[n])
        there = pl.ds(pl.multiple_of(tokens + ex.near_first[n] * half, half), half)
        return [
            pltpu.make_async_remote_copy(
                src_ref=ref.at[here], dst_ref=ref.at[there], send_sem=kv_send.at[2 * n + i],
                recv_sem=kv_recv.at[2 * n + i], device_id=sibling, device_id_type=MESH,
            )
            for i, ref in enumerate((k, v))
        ]

    loads[0].wait()
    for load in loads[4:]:
        load.wait()
    for n in range(n_seq):
        here = rows_of(ex.near_first[n])
        wait_bytes(xs.at[here], recv_sem.at[ex.near_first[n]])
        if n == n_seq - 2:
            spread(cot_in, cs, 4, send_or_keep)
        unit, _ = row_stats(xs[here].astype(F32))
        normed = (unit * gain1).astype(BF16)
        xn[here] = normed

        def project(j, _, here=here):
            weights = jnp.concatenate([wqkv[:, tile(j, width)], wqkv[:, tile(j, 2 * width)]], axis=1)
            both = nn(xn[here], weights)
            k[here, tile(j)] = roped(both[:, :LANES], here, 1.0)
            v[here, tile(j)] = both[:, LANES:].astype(BF16)
            return 0

        lax.fori_loop(0, pairs, project, 0)
        for copy in kv_copies(n):
            copy.start()

        def project_q(j, _, here=here):
            both = nn(xn[here], wqkv[:, tile(j, 0, 2)])
            for t in range(2):
                q[here, tile(2 * j + t)] = roped(both[:, t * LANES : (t + 1) * LANES], here, 0.125)
            return 0

        lax.fori_loop(0, pairs // 2, project_q, 0)

    def attend(j):
        lanes = tile(j)
        k2, vt, q2 = k[:, lanes], v[:, lanes].T, q[:, lanes]
        scores = [nt(one_head(k2, sub), q2) for sub in range(2)]
        mixed = []
        for sub in range(2):
            top = jnp.max(scores[sub], axis=0, keepdims=True)
            weights = jnp.exp(scores[sub] - top)
            total = jnp.sum(weights, axis=0, keepdims=True)
            lse[j, sub : sub + 1, :] = top + jnp.log(total)
            mixed.append(
                nn(vt[sub * HEAD_DIM : (sub + 1) * HEAD_DIM], weights.astype(BF16)) * (1.0 / total)
            )
        att[:, lanes] = jnp.concatenate(mixed, axis=0).T.astype(BF16)

    def attend_group(group, _):
        for j in range(pairs // 2):
            attend(group * (pairs // 2) + j)
        return 0

    for n in range(n_seq):
        for copy in kv_copies(n):
            copy.wait()
    lax.fori_loop(0, 2, attend_group, 0)

    loads[1].wait()
    h[...] = xs[...].astype(F32) + nn(att[...], wo[...])
    unit2, _ = row_stats(h[...])
    xn2[...] = (unit2 * gain2).astype(BF16)
    xn2t[...] = xn2[...].T
    loads[2].wait()
    loads[3].wait()
    for slot in range(n_seq):
        wait_bytes(cs.at[rows_of(slot)], recv_sem.at[4 + slot])
    dmt[...] = cs[...].T

    def feed(j):
        both = nn(xn2[...], jnp.concatenate([win[:, tile(j)], win[:, tile(j, ff)]], axis=1))
        gate, up = both[:, :LANES], both[:, LANES:]
        phi = 0.5 * (1.0 + lax.erf(gate * 0.7071067811865476))
        slope = phi + gate * (0.3989422804014327 * jnp.exp(-0.5 * gate * gate))
        active = gate * phi
        inner = (active * up).astype(BF16)
        hid[:, tile(j)] = inner
        dhid = nt(cs[...], wout[tile(j), :])
        dgate, dup = (dhid * up * slope).astype(BF16), (dhid * active).astype(BF16)
        dgu[:, tile(j)] = dgate
        dgu[:, tile(j, ff)] = dup
        grads[j] = nn(dmt[...], inner).astype(BF16)
        pair = nn(xn2t[...], jnp.concatenate([dgate, dup], axis=1)).astype(BF16)
        grads[ffs + j] = pair[:, :LANES]
        grads[2 * ffs + j] = pair[:, LANES:]

    loop("feed", 0, ffs, feed)

    outs[...] = (h[...] + nn(hid[...], wout[...])).astype(BF16)
    after(("mix", 0))

    acc[...] = nt(dgu[...], win[...])
    unit2, scale2 = row_stats(h[...])
    grad2 = acc[...]
    dh[...] = cs[...].astype(F32) + norm_back(grad2, unit2, scale2, gain2)
    gain_terms = (grad2 * unit2).astype(BF16).T
    grads[3 * ffs + pairs] = nn(gain_terms, jnp.ones((tokens, LANES), BF16)).astype(BF16)
    after(("norm", 0))

    datt = dh[...].astype(BF16)
    att_t = att[...].T
    for j in range(pairs // 2):
        both = nn(att_t, datt[:, 2 * j * LANES : (2 * j + 2) * LANES]).astype(BF16)
        for t in range(2):
            grads[3 * ffs + 2 * j + t] = both[:, t * LANES : (t + 1) * LANES]
    after(("wo", 0))

    do[...] = nt(datt, wo[...]).astype(BF16)
    lane = lax.broadcasted_iota(jnp.int32, (8, LANES), 1)
    row = lax.broadcasted_iota(jnp.int32, (8, LANES), 0)
    pick = jnp.where(lane // HEAD_DIM == row, 1.0, 0.0).astype(F32)
    for j in range(pairs):
        lanes = slice(j * LANES, (j + 1) * LANES)
        product = do[:, lanes].astype(F32) * att[:, lanes].astype(F32)
        sums = lax.dot_general(
            pick, product, (((1,), (1,)), ((), ())),
            precision=lax.Precision.HIGHEST, preferred_element_type=F32,
        )
        dd[j] = sums[:2]
    after(("do", 0))

    dqkv, xnt, dx = win.at[pl.ds(0, tokens)], xn2t, do
    away, own = (xn2, att), (h, acc)
    xnt[...] = xn[...].T

    def attend_back(keys, j):
        lanes = tile(j)
        q2, do2 = q[:, lanes], do[:, lanes]
        k2, v2 = k[keys, lanes], v[keys, lanes]
        kt = k2.T
        dks, dvs, dqs = [], [], []
        for sub in range(2):
            probs = jnp.exp(nt(one_head(k2, sub), q2) - lse[j, sub : sub + 1, :])
            dprobs = nt(one_head(v2, sub), do2)
            dscores = (probs * (dprobs - dd[j, sub : sub + 1, :])).astype(BF16)
            dvs.append(nn(probs.astype(BF16), do2))
            dks.append(nn(dscores, q2))
            dqs.append(nn(kt[sub * HEAD_DIM : (sub + 1) * HEAD_DIM], dscores))
        low = lane_of(dks[0].shape) < HEAD_DIM
        return jnp.where(low, dks[0], dks[1]), jnp.where(low, dvs[0], dvs[1]), jnp.concatenate(dqs, axis=0)

    def unrope(part):
        return (part * cos[...] - turned(part) * sin[...]).astype(BF16)

    def far(j):
        dk, dv, dq = attend_back(pl.ds(tokens, tokens), j)
        away[0][:, tile(j)] = dk.astype(BF16)
        away[1][:, tile(j)] = dv.astype(BF16)
        dqt[j] = dq

    def near(j):
        dk, dv, dq = attend_back(pl.ds(0, tokens), j)
        own[0][:, tile(j)] = dk
        own[1][:, tile(j)] = dv
        dqkv[:, tile(j)] = unrope((dqt[j] + dq).T * 0.125)

    def join(j, _):
        dqkv[:, tile(j, width)] = unrope(own[0][:, tile(j)] + landed[0, :, tile(j)].astype(F32))
        dqkv[:, tile(j, 2 * width)] = (own[1][:, tile(j)] + landed[1, :, tile(j)].astype(F32)).astype(BF16)
        return 0

    base = 3 * ffs + pairs + 1
    for part, (low, high) in enumerate(((0, FIRST_PAIRS), (FIRST_PAIRS, pairs))):
        loop("far", low, high, far)
        lanes = pl.ds(low * LANES, (high - low) * LANES)
        sends = [
            pltpu.make_async_remote_copy(
                src_ref=away[i].at[:, lanes], dst_ref=landed.at[i, :, lanes],
                send_sem=kv_send.at[8 + 2 * part + i], recv_sem=kv_recv.at[8 + 2 * part + i],
                device_id=sibling, device_id_type=MESH,
            )
            for i in range(2)
        ]
        for send in sends:
            send.start()
        loop("near", low, high, near)
        for send in sends:
            send.wait()
        lax.fori_loop(low, high, join, 0)

        def weight_grads(j, _):
            for third in range(3):
                both = nn(xnt[...], dqkv[:, tile(j, third * width, 2)]).astype(BF16)
                for t in range(2):
                    grads[base + third * pairs + 2 * j + t] = both[:, t * LANES : (t + 1) * LANES]
            return 0

        lax.fori_loop(low // 2, high // 2, weight_grads, 0)
        after(("join", part))

    grad1 = nt(dqkv[...], wqkv[...])
    unit, scale = row_stats(xs[...].astype(F32))
    dx[...] = (dh[...] + norm_back(grad1, unit, scale, gain1)).astype(BF16)
    after(("dx", 0))
    after("end")

    spread(x_in, xs, 0, wait_sent)
    spread(cot_in, cs, 4, wait_sent)
    for src, dst, base in ((outs, out_o, 8), (dx, dx_o, 12)):
        for n in range(n_seq):
            gather(src, dst, base, n, wait_sent)
        for block in range(2):
            for part in range(2):
                wait_bytes(dst.at[block, pl.ds(part * half, half)], recv_sem.at[base + 2 * block + part])


def layer(n_doc, n_seq, inputs, cotangent, gain1, gain2, wqkv, wo, win, wout, cos, sin):
    blocks, rows, width = inputs.shape
    tokens = blocks * rows
    ff = wout.shape[0]
    pairs = width // LANES
    streams, _, total = stream_plan(width, ff)
    rounds = log2(n_doc) - 1 + log2(n_seq)
    kept = halvings(width, rounds)
    legs = 2 + rounds + sum(1 for _, split in kept if split)
    slots = sum(stream.count for stream in streams)
    hbm, vmem = pl.BlockSpec(memory_space=pl.ANY), pl.BlockSpec(memory_space=pltpu.VMEM)
    sds, dma = jax.ShapeDtypeStruct, pltpu.SemaphoreType.DMA
    row_b = pltpu.VMEM((tokens, width), BF16)
    row_f = pltpu.VMEM((tokens, width), F32)
    return pl.pallas_call(
        functools.partial(layer_kernel, n_doc, n_seq),
        out_shape=[
            sds((blocks, rows, width), BF16), sds((blocks, rows, width), BF16), sds((total, width, LANES), BF16),
        ],
        in_specs=[hbm, hbm, vmem, vmem] + [hbm] * 6,
        out_specs=[hbm] * 3,
        scratch_shapes=[
            row_b, row_b, row_b,
            pltpu.VMEM(wqkv.shape, BF16), pltpu.VMEM(wo.shape, BF16), pltpu.VMEM(win.shape, BF16), pltpu.VMEM(wout.shape, BF16),
            pltpu.VMEM((tokens, LANES), F32), pltpu.VMEM((tokens, LANES), F32),
            row_b, row_b, pltpu.VMEM((2 * tokens, width), BF16), pltpu.VMEM((2 * tokens, width), BF16),
            row_b, row_f, row_b, pltpu.VMEM((width, tokens), BF16),
            pltpu.VMEM((tokens, ff), BF16), pltpu.VMEM((tokens, 2 * ff), BF16), pltpu.VMEM((width, tokens), BF16),
            row_b, row_f, row_f,
            pltpu.VMEM((pairs, 2, tokens), F32), pltpu.VMEM((pairs, 2, tokens), F32),
            pltpu.VMEM((pairs, LANES, tokens), F32), pltpu.VMEM((2, tokens, width), BF16),
            pltpu.VMEM((total, width, LANES), BF16),
            pltpu.VMEM((slots, Reducer.landing_rows(width, rounds), LANES), BF16),
            pltpu.VMEM((slots, width, LANES), BF16),
            dma((12,)), dma((16,)), dma((16,)), dma((12,)), dma((12,)),
            dma((len(streams), legs)), dma((len(streams), legs)), dma((len(streams),)),
        ],
        compiler_params=pltpu.CompilerParams(collective_id=0, has_side_effects=True, vmem_limit_bytes=VMEM_LIMIT),
        name="layer",
    )(inputs, cotangent, gain1, gain2, wqkv, wo, win, wout, cos, sin)


def widen_kernel(ff, width, g, wqkv, gain1, out, dx, dqkv_o, dwo_o, dwin_o, dwout_o, gain1_o, gain2_o, out_o, dx_o):
    out_o[...] = out[...]
    dx_o[...] = dx[...]
    ffs, pairs = ff // LANES, width // LANES
    base = 3 * ffs + pairs + 1
    for j in range(ffs):
        dwout_o[j * LANES : (j + 1) * LANES, :] = g[j].astype(F32).T
    for j in range(2 * ffs):
        dwin_o[:, j * LANES : (j + 1) * LANES] = g[ffs + j].astype(F32)
    for j in range(pairs):
        dwo_o[:, j * LANES : (j + 1) * LANES] = g[3 * ffs + j].astype(F32)
    gain2_o[...] = g[base - 1].astype(F32).T[0]
    along = jnp.zeros((LANES, LANES), F32)
    for j in range(3 * pairs):
        lanes = slice(j * LANES, (j + 1) * LANES)
        part = g[base + j].astype(F32)
        dqkv_o[:, lanes] = part
        along += part * wqkv[:, lanes].astype(F32)
    total = jnp.sum(along.T, axis=0, keepdims=True)
    gain1_o[...] = (total / gain1[...].reshape(1, LANES))[0]


def widen(ff, g, wqkv, gain1, out, dx):
    total, width, _ = g.shape
    sds = jax.ShapeDtypeStruct
    across = lambda i: (i, 0)
    down = lambda i: (0, i)
    flat = pl.BlockSpec((LANES,), lambda i: (i,))
    blocks, rows, _ = out.shape
    token = pl.BlockSpec((blocks, rows, LANES), lambda i: (0, 0, i))
    return pl.pallas_call(
        functools.partial(widen_kernel, ff, width),
        grid=(width // LANES,),
        out_shape=[
            sds(wqkv.shape, F32), sds((width, width), F32), sds((width, 2 * ff), F32), sds((ff, width), F32),
            sds((width,), F32), sds((width,), F32), sds(out.shape, BF16), sds(dx.shape, BF16),
        ],
        in_specs=[
            pl.BlockSpec((total, LANES, LANES), lambda i: (0, i, 0)), pl.BlockSpec((LANES, wqkv.shape[1]), across), flat, token, token,
        ],
        out_specs=[
            pl.BlockSpec((LANES, wqkv.shape[1]), across), pl.BlockSpec((LANES, width), across),
            pl.BlockSpec((LANES, 2 * ff), across), pl.BlockSpec((ff, LANES), down), flat, flat, token, token,
        ],
        compiler_params=pltpu.CompilerParams(vmem_limit_bytes=VMEM_LIMIT),
        name="widen",
    )(g, wqkv, gain1, out, dx)


def rotary_tables(length):
    half = HEAD_DIM // 2
    frequency = ROPE_THETA ** (-(np.arange(half) * 2.0) / HEAD_DIM)
    angles = np.arange(length)[:, None] * frequency[None, :]
    cos, sin = np.cos(angles), np.sin(angles)
    per_tile = LANES // HEAD_DIM
    cos = np.tile(np.concatenate([cos, cos], axis=1), (1, per_tile))
    sin = np.tile(np.concatenate([-sin, sin], axis=1), (1, per_tile))
    return jnp.asarray(cos, F32), jnp.asarray(sin, F32)


def per_device(
    n_doc, n_seq,
    inputs, attn_gain, qkv_weight, attn_out_weight, mlp_gain, mlp_in_weight, mlp_out_weight, cotangent,
):
    blocks, rows, width = inputs.shape
    ff = mlp_out_weight.shape[0]
    cos, sin = rotary_tables(rows * n_seq)
    output, dx, grads = layer(
        n_doc, n_seq, inputs, cotangent, attn_gain, mlp_gain,
        qkv_weight, attn_out_weight, mlp_in_weight, mlp_out_weight, cos, sin,
    )
    dqkv, dwo, dwin, dwout, dgain1, dgain2, output, dx = widen(ff, grads, qkv_weight, attn_gain, output, dx)
    return output, dx, dgain1, dqkv, dwo, dgain2, dwin, dwout


def solution(mesh):
    n_doc, n_seq = mesh.shape["doc"], mesh.shape["seq"]
    placed = (P("doc", "seq", None), P(), P(), P(), P(), P(), P(), P("doc", "seq", None))
    return jax.shard_map(
        functools.partial(per_device, n_doc, n_seq),
        mesh=mesh,
        in_specs=placed,
        out_specs=(P("doc", "seq", None), P("doc", "seq", None), P(), P(), P(), P(), P(), P()),
        check_vma=False,
    )
```

```python
import functools

import jax
import jax.numpy as jnp
import numpy as np
from jax import lax
from jax.experimental import pallas as pl
from jax.experimental.pallas import tpu as pltpu
from jax.sharding import PartitionSpec as P

HEAD_DIM = 64
ROPE_THETA = 160000.0
NORM_EPSILON = 1e-05
F32 = jnp.float32
BF16 = jnp.bfloat16
MESH = pl.DeviceIdType.MESH
LANES = 128
VMEM_LIMIT = 60 << 20


def nn(a, b):
    return lax.dot_general(a, b, (((1,), (0,)), ((), ())), preferred_element_type=F32)


def nt(a, b):
    return lax.dot_general(a, b, (((1,), (1,)), ((), ())), preferred_element_type=F32)


def lane_of(shape):
    return lax.broadcasted_iota(jnp.int32, shape, 1)


def one_head(pair, sub):
    lane = lane_of(pair.shape)
    mine = (lane < HEAD_DIM) if sub == 0 else (lane >= HEAD_DIM)
    return jnp.where(mine, pair, jnp.zeros_like(pair))


def turned(values):
    back = pltpu.roll(values, HEAD_DIM // 2, 1)
    ahead = pltpu.roll(values, LANES - HEAD_DIM // 2, 1)
    return jnp.where(lane_of(values.shape) % HEAD_DIM < HEAD_DIM // 2, ahead, back)


def row_stats(values):
    mean = jnp.mean(values, axis=1, keepdims=True)
    centered = values - mean
    scale = lax.rsqrt(jnp.mean(centered * centered, axis=1, keepdims=True) + NORM_EPSILON)
    return centered * scale, scale


def norm_back(grad, unit, scale, gain):
    weighted = grad * gain
    along = jnp.mean(weighted, axis=1, keepdims=True)
    across = jnp.mean(weighted * unit, axis=1, keepdims=True)
    return scale * (weighted - along - unit * across)


def bit_of(index, weight):
    return (index // weight) % 2


def flipped(index, weight):
    return index + weight - 2 * weight * bit_of(index, weight)


def greet(partners):
    barrier = pltpu.get_barrier_semaphore()
    for partner in partners:
        pl.semaphore_signal(barrier, inc=1, device_id=partner, device_id_type=MESH)
    pl.semaphore_wait(barrier, len(partners))


def group_partners(doc, seq, n_seq):
    core = doc % 2
    found = []
    for other_core in range(2):
        for step in range(n_seq):
            if other_core == 0 and step == 0:
                continue
            found.append(
                (doc - core + (core + other_core) % 2, (seq + step) % n_seq)
            )
    return found


class Exchange:
    def __init__(self, doc, seq, n_seq):
        assert n_seq == 4
        core = doc % 2
        self.doc, self.seq, self.core = doc, seq, core
        self.base = doc - core
        side = seq // 2
        self.near_first = [seq, flipped(seq, 1), 2 - side, 3 - 3 * side]
        self.block_first = (1 - core) * side

    def out_piece(self, n):
        block = self.block_first + n // 2 - 2 * self.block_first * (n // 2)
        half = n % 2
        return block, half, (self.base + half, 2 * self.core + block)

    def back_target(self, quarter):
        return (self.base + self.seq // 2, quarter)

    def is_self(self, target):
        return jnp.logical_and(target[0] == self.doc, target[1] == self.seq)


def send_or_keep(ex, target, src, dst, send_sem, recv_sem):
    mine = ex.is_self(target)

    @pl.when(mine)
    def _():
        pltpu.make_async_copy(src, dst, recv_sem).start()

    @pl.when(jnp.logical_not(mine))
    def _():
        pltpu.make_async_remote_copy(
            src_ref=src, dst_ref=dst, send_sem=send_sem, recv_sem=recv_sem,
            device_id=target, device_id_type=MESH,
        ).start()


def wait_sent(ex, target, src, dst, send_sem, recv_sem):
    @pl.when(jnp.logical_not(ex.is_self(target)))
    def _():
        pltpu.make_async_remote_copy(
            src_ref=src, dst_ref=dst, send_sem=send_sem, recv_sem=recv_sem,
            device_id=target, device_id_type=MESH,
        ).wait_send()


def wait_bytes(ref, sem):
    pltpu.make_async_copy(ref, ref, sem).wait()


LINK_RATE, CORE_RATE, ROUND_LATENCY, SPARE = 43225.0, 484500.0, 2.6, 1.0
STEP_TIME, ADD_TIME = 0.1, 0.4e-6
PIECE_TIME = {"feed": 2.0, "last": 1.1, "mix": 1.2, "norm": 3.5, "wo": 1.0, "do": 1.4, "far": 1.25, "near": 1.25, "join": 2.5, "dx": 4.0}
FIRST_PAIRS = 4
ORDERS = "01"
OUT, DX = -1, -2
OUT_AFTER, DX_GAP = (5, 5, 6, 12), 12.0


def log2(n):
    return n.bit_length() - 1


class Stream:
    def __init__(self, first, second, count):
        self.first, self.second, self.count = first, second, count


def halvings(rows, rounds):
    kept, extent = [], rows
    for _ in range(rounds):
        split = (extent // 2) % 16 == 0
        extent = extent // 2 if split else extent
        kept.append((extent, split))
    return kept


def axes_of(n_doc, n_seq):
    doc_axes = [("doc", 1 << i) for i in range(1, log2(n_doc))]
    seq_axes = [("seq", 1 << i) for i in range(log2(n_seq))]
    return doc_axes, seq_axes


def axis_order(index, n_doc, n_seq):
    doc_axes, seq_axes = axes_of(n_doc, n_seq)
    code = int(ORDERS[index % len(ORDERS)])
    turn = code % 2 * (len(doc_axes) // 2)
    doc_axes = doc_axes[turn:] + doc_axes[:turn]
    place = len(doc_axes) * (2 - code // 2) // 2
    return doc_axes[:place] + seq_axes[:-1] + doc_axes[place:] + seq_axes[-1:]


def stream_plan(width, ff):
    ffs, pairs = ff // LANES, width // LANES
    streams, ready = [], {}

    def add(piece, first, second, count):
        ready.setdefault(piece, []).append(len(streams))
        streams.append(Stream(first, second, count))

    assert ffs % 2 == 1 and pairs % 2 == 0
    covered = ffs - 1
    for low in range(0, covered, 2):
        for base in (0, ffs, 2 * ffs):
            add(("feed", low // 2), base + low, base + low + 1, 1)
    add(("last", 0), covered, ffs + covered, 1)
    add(("norm", 0), 2 * ffs + covered, 3 * ffs + pairs, 1)
    for start in range(3 * ffs, 3 * ffs + pairs, 2):
        add(("wo", 0), start, start + 1, 1)
    base = 3 * ffs + pairs + 1
    for part, (low, high) in enumerate(((0, FIRST_PAIRS), (FIRST_PAIRS, pairs))):
        for third in range(3):
            for start in range(base + third * pairs + low, base + third * pairs + high, 2):
                add(("join", part), start, start + 1, 1)
    return streams, ready, base + 3 * pairs


def piece_list(ff, pairs):
    ffs = ff // LANES
    pieces = [("feed", j) for j in range(ffs // 2)] + [("last", 0)]
    pieces += [("mix", 0), ("norm", 0), ("wo", 0), ("do", 0)]
    for part, (low, high) in enumerate(((0, FIRST_PAIRS), (FIRST_PAIRS, pairs))):
        pieces += [("far", j) for j in range(low, high)] + [("near", j) for j in range(low, high)]
        pieces.append(("join", part))
    return pieces + [("dx", 0)]


def agenda(streams, ready, pieces, rows, n_doc, n_seq):
    rounds = log2(n_doc) - 1 + log2(n_seq)
    kept = halvings(rows, rounds)
    ups = [r for r in reversed(range(rounds)) if kept[r][1]]
    free, flying, steps = {}, [], {}
    near, far = axes_of(n_doc, n_seq)[1]

    def legs(index):
        order = axis_order(index, n_doc, n_seq)
        unit = streams[index].count * LANES * 2
        trip = [("core", rows * unit)]
        trip += [(order[r], kept[r][0] * unit) for r in range(rounds)]
        trip += [(order[r], kept[r][0] * unit) for r in ups]
        return trip + [("core", rows * unit)]

    def occupy(axis, size, when):
        rate = CORE_RATE if axis == "core" else LINK_RATE / 2 if axis == far else LINK_RATE
        begin = max(when, free.get(axis, 0.0))
        free[axis] = begin + size / rate
        if axis == far:
            free[near] = max(free.get(near, 0.0), begin) + size / LINK_RATE
        return free[axis]

    def leave(chunk, when):
        if chunk:
            occupy(near if chunk == 1 else far, 196e3, when)

    def depart(index, leg, when):
        flying.append((occupy(*legs(index)[leg], when) + ROUND_LATENCY, index, leg))

    def serve(now):
        flying.sort()
        done, index, leg = flying.pop(0)
        trip = legs(index)
        now = max(now, done) + STEP_TIME + (trip[leg][1] * ADD_TIME if leg <= rounds else 0.0)
        if leg + 1 < len(trip):
            depart(index, leg + 1, now)
        return now, (index, leg)

    now = 0.0
    for piece in pieces:
        now += PIECE_TIME[piece[0]]
        actions = steps.setdefault(piece, [])
        for index in ready.get(piece, ()):
            actions.append((index, -1))
            depart(index, 0, now)
            now += STEP_TIME
        for chunk, place in enumerate(OUT_AFTER):
            if piece == pieces[place]:
                actions.append((OUT, chunk))
                leave(chunk, now)
                now += STEP_TIME
        while flying and min(flying)[0] + SPARE <= now:
            now, action = serve(now)
            actions.append(action)
    last = steps.setdefault("end", [])
    begin, chunk = now, 0
    while flying or chunk < n_seq:
        upcoming = max(now, min(flying)[0]) if flying else now
        if chunk < n_seq and (not flying or upcoming >= begin + chunk * DX_GAP):
            leave(chunk, now)
            last.append((DX, chunk))
            now += STEP_TIME
            chunk += 1
            continue
        now, action = serve(now)
        last.append(action)
    return steps


class Reducer:
    def __init__(self, streams, n_doc, n_seq, doc, seq, grads, landing, final, out, send_sem, recv_sem, own_sem):
        self.streams, self.grads, self.landing, self.final, self.out = streams, grads, landing, final, out
        self.send_sem, self.recv_sem, self.own_sem = send_sem, recv_sem, own_sem
        self.busy, self.unsent = False, []
        self.core = doc % 2
        self.rows = grads.shape[1]
        self.rounds = log2(n_doc) - 1 + log2(n_seq)
        self.kept = halvings(self.rows, self.rounds)
        self.ups = [r for r in reversed(range(self.rounds)) if self.kept[r][1]]
        self.legs = 2 + self.rounds + len(self.ups)
        self.sibling = (flipped(doc, 1), seq)
        self.bits, self.partners = {}, {}
        for name, weight in sum(axes_of(n_doc, n_seq), []):
            index = doc if name == "doc" else seq
            self.bits[name, weight] = bit_of(index, weight)
            self.partners[name, weight] = (flipped(doc, weight), seq) if name == "doc" else (doc, flipped(seq, weight))
        self.orders = [axis_order(i, n_doc, n_seq) for i in range(len(streams))]
        self.slots, used = [], 0
        for stream in streams:
            self.slots.append(pl.ds(used, stream.count))
            used += stream.count
        self.plans = []
        for order in self.orders:
            offset, base, plan = 0, 0, []
            for (keep, split), axis in zip(self.kept, order):
                bit = self.bits[axis]
                mine = offset + bit * keep if split else offset
                theirs = offset + (1 - bit) * keep if split else offset
                plan.append((mine, theirs, base, keep))
                base += keep
                offset = mine
            self.plans.append(plan)

    @staticmethod
    def landing_rows(rows, rounds):
        return sum(keep for keep, _ in halvings(rows, rounds))

    def tiles(self, index, other=False):
        stream = self.streams[index]
        side = 1 - self.core if other else self.core
        return pl.ds(stream.first + side * (stream.second - stream.first), stream.count)

    def span(self, start, extent):
        return pl.ds(start if isinstance(start, int) else pl.multiple_of(start, 16), extent)

    def copy(self, index, leg, receiving=False):
        slot = self.slots[index]
        if leg == 0:
            src, dst, partner = self.grads.at[self.tiles(index, True)], self.final.at[slot], self.sibling
        elif leg <= self.rounds:
            mine, theirs, base, keep = self.plans[index][leg - 1]
            src = self.grads.at[self.tiles(index), self.span(theirs, keep)]
            dst, partner = self.landing.at[slot, pl.ds(base, keep)], self.partners[self.orders[index][leg - 1]]
        elif leg < self.legs - 1:
            r = self.ups[leg - 1 - self.rounds]
            mine, theirs, base, keep = self.plans[index][r]
            src = dst = self.final.at[slot, self.span(theirs if receiving else mine, keep)]
            partner = self.partners[self.orders[index][r]]
        else:
            src, dst, partner = self.final.at[slot], self.out.at[self.tiles(index, receiving)], self.sibling
        return pltpu.make_async_remote_copy(
            src_ref=src, dst_ref=dst, send_sem=self.send_sem.at[index, leg], recv_sem=self.recv_sem.at[index, leg],
            device_id=partner, device_id_type=MESH,
        )

    def own(self, index):
        return pltpu.make_async_copy(self.final.at[self.slots[index]], self.out.at[self.tiles(index)], self.own_sem.at[index])

    def add(self, index, leg):
        stream, slot = self.streams[index], self.slots[index]
        start = stream.first + self.core * (stream.second - stream.first)
        low = slot.start
        if leg == 0:
            mine, base, keep = 0, 0, self.rows
        else:
            mine, _, base, keep = self.plans[index][leg - 1]
        block = keep
        while block > 96:
            block //= 2

        def body(i, _):
            here = self.span(mine + i * block, block)
            for t in range(stream.count):
                if leg == 0:
                    other = self.final[low + t, here]
                else:
                    other = self.landing[low + t, self.span(base + i * block, block)]
                total = (self.grads[start + t, here].astype(F32) + other.astype(F32)).astype(BF16)
                if leg == self.rounds:
                    self.final[low + t, here] = total
                else:
                    self.grads[start + t, here] = total
            return 0

        lax.fori_loop(0, keep // block, body, 0)

    def settle(self):
        self.busy = False
        for index, leg in self.unsent:
            self.copy(index, leg).wait_send()

    def act(self, index, leg):
        if leg >= 0:
            if self.busy:
                self.unsent.append((index, leg))
            else:
                self.copy(index, leg).wait_send()
            self.copy(index, leg, True).wait_recv()
            if leg <= self.rounds:
                self.add(index, leg)
            if leg == self.legs - 1:
                self.own(index).wait()
        if leg + 1 < self.legs:
            self.copy(index, leg + 1).start()
        if leg + 1 == self.legs - 1:
            self.own(index).start()


def layer_kernel(
    n_doc, n_seq,
    x_in, cot_in, gain1_in, gain2_in, wqkv_in, wo_in, win_in, wout_in, cos_in, sin_in,
    out_o, dx_o, g_o,
    xs, cs, outs, wqkv, wo, win, wout, cos, sin, xn, q, k, v, att, h, xn2, xn2t, hid, dgu, dmt, do, dh, acc, lse, dd,
    dqt, landed, grads, landing, final, rms,
    w_sem, send_sem, recv_sem, kv_send, kv_recv, sum_send, sum_recv, own_sem,
):
    doc, seq = lax.axis_index("doc"), lax.axis_index("seq")
    core = doc % 2
    ex = Exchange(doc, seq, n_seq)
    half = x_in.shape[1] // 2
    tokens, width = xs.shape
    ff = wout.shape[0]
    ffs, pairs = ff // LANES, width // LANES
    sibling = (flipped(doc, 1), seq)

    loads = [
        pltpu.make_async_copy(s, d, w_sem.at[i])
        for i, (s, d) in enumerate(
            [(wqkv_in, wqkv), (wo_in, wo), (win_in, win), (wout_in, wout)]
            + [
                (t.at[pl.ds((2 * quarter + core) * half, half)], d.at[pl.ds(quarter * half, half)])
                for t, d in ((cos_in, cos), (sin_in, sin))
                for quarter in range(n_seq)
            ]
        )
    ]
    loads[0].start()
    for load in loads[4:]:
        load.start()
    greet(group_partners(doc, seq, n_seq) + [(flipped(doc, w), seq) for _, w in axes_of(n_doc, n_seq)[0]])

    def rows_of(slot):
        return pl.ds(pl.multiple_of(slot * half, half), half)

    def spread(src, dst, base, act):
        for n in range(n_seq):
            block, part, target = ex.out_piece(n)
            act(
                ex, target, src.at[block, pl.ds(part * half, half)], dst.at[rows_of(seq)],
                send_sem.at[base + n], recv_sem.at[base + seq],
            )

    def gather(src, dst, base, n, act):
        quarter = ex.near_first[n]
        act(
            ex, ex.back_target(quarter), src.at[rows_of(quarter)], dst.at[seq % 2, rows_of(core)],
            send_sem.at[base + n], recv_sem.at[base + 2 * (seq % 2) + core],
        )

    spread(x_in, xs, 0, send_or_keep)
    for load in loads[1:4]:
        load.start()
    gain1, gain2 = gain1_in[...].reshape(1, width), gain2_in[...].reshape(1, width)

    streams, ready, _ = stream_plan(width, ff)
    steps = agenda(streams, ready, piece_list(ff, pairs), width, n_doc, n_seq)
    reducer = Reducer(streams, n_doc, n_seq, doc, seq, grads, landing, final, g_o, sum_send, sum_recv, own_sem)

    def after(piece):
        for index, leg in steps.get(piece, ()):
            if index == OUT:
                gather(outs, out_o, 8, leg, send_or_keep)
            elif index == DX:
                gather(do, dx_o, 12, leg, send_or_keep)
            else:
                reducer.act(index, leg)

    def loop(name, low, high, body):
        def one(j, _):
            body(j)
            for at in range(low, high):
                if steps.get((name, at)):
                    pl.when(j == at)(functools.partial(after, (name, at)))
            return 0

        lax.fori_loop(low, high, one, 0)

    def tile(j, base=0, count=1):
        return pl.ds(pl.multiple_of(base + j * LANES * count, LANES), LANES * count)

    def roped(part, here, scale):
        return ((part * cos[here] + turned(part) * sin[here]) * scale).astype(BF16)

    def kv_copies(n):
        here = rows_of(ex.near_first[n])
        there = pl.ds(pl.multiple_of(tokens + ex.near_first[n] * half, half), half)
        return [
            pltpu.make_async_remote_copy(
                src_ref=ref.at[here], dst_ref=ref.at[there], send_sem=kv_send.at[2 * n + i],
                recv_sem=kv_recv.at[2 * n + i], device_id=sibling, device_id_type=MESH,
            )
            for i, ref in enumerate((k, v))
        ]

    loads[0].wait()
    for load in loads[4:]:
        load.wait()
    for n in range(n_seq):
        here = rows_of(ex.near_first[n])
        wait_bytes(xs.at[here], recv_sem.at[ex.near_first[n]])
        if n == n_seq - 2:
            spread(cot_in, cs, 4, send_or_keep)
        unit, _ = row_stats(xs[here].astype(F32))
        normed = (unit * gain1).astype(BF16)
        xn[here] = normed

        def project(j, _, here=here):
            weights = jnp.concatenate([wqkv[:, tile(j, width)], wqkv[:, tile(j, 2 * width)]], axis=1)
            both = nn(xn[here], weights)
            k[here, tile(j)] = roped(both[:, :LANES], here, 1.0)
            v[here, tile(j)] = both[:, LANES:].astype(BF16)
            return 0

        lax.fori_loop(0, pairs, project, 0)
        for copy in kv_copies(n):
            copy.start()

        def project_q(j, _, here=here):
            both = nn(xn[here], wqkv[:, tile(j, 0, 2)])
            for t in range(2):
                q[here, tile(2 * j + t)] = roped(both[:, t * LANES : (t + 1) * LANES], here, 0.125)
            return 0

        lax.fori_loop(0, pairs // 2, project_q, 0)

    def attend(j):
        lanes = tile(j)
        k2, vt, q2 = k[:, lanes], v[:, lanes].T, q[:, lanes]
        scores = [nt(one_head(k2, sub), q2) for sub in range(2)]
        mixed = []
        for sub in range(2):
            top = jnp.max(scores[sub], axis=0, keepdims=True)
            weights = jnp.exp(scores[sub] - top)
            total = jnp.sum(weights, axis=0, keepdims=True)
            lse[j, sub : sub + 1, :] = top + jnp.log(total)
            mixed.append(
                nn(vt[sub * HEAD_DIM : (sub + 1) * HEAD_DIM], weights.astype(BF16)) * (1.0 / total)
            )
        att[:, lanes] = jnp.concatenate(mixed, axis=0).T.astype(BF16)

    def attend_group(group, _):
        for j in range(pairs // 2):
            attend(group * (pairs // 2) + j)
        return 0

    for n in range(n_seq):
        for copy in kv_copies(n):
            copy.wait()
    lax.fori_loop(0, 2, attend_group, 0)

    loads[1].wait()
    h[...] = xs[...].astype(F32) + nn(att[...], wo[...])
    unit2, scale2 = row_stats(h[...])
    dh[...] = unit2
    rms[...] = scale2
    xn2[...] = (unit2 * gain2).astype(BF16)
    xn2t[...] = xn2[...].T
    loads[2].wait()
    loads[3].wait()
    for slot in range(n_seq):
        wait_bytes(cs.at[rows_of(slot)], recv_sem.at[4 + slot])
    dmt[...] = cs[...].T

    def feed(j, count):
        first = 2 * j
        wide = count * LANES
        lanes = pl.ds(pl.multiple_of(first * LANES, LANES), wide)
        up_lanes = pl.ds(pl.multiple_of(ff + first * LANES, LANES), wide)
        gate, up = nn(xn2[...], win[:, lanes]), nn(xn2[...], win[:, up_lanes])
        phi = 0.5 * (1.0 + lax.erf(gate * 0.7071067811865476))
        slope = phi + gate * (0.3989422804014327 * jnp.exp(-0.5 * gate * gate))
        active = gate * phi
        inner = (active * up).astype(BF16)
        hid[:, lanes] = inner
        dhid = nt(cs[...], wout[lanes, :])
        dgate, dup = (dhid * up * slope).astype(BF16), (dhid * active).astype(BF16)
        dgu[:, lanes] = dgate
        dgu[:, up_lanes] = dup
        for base, left, right in ((0, dmt, inner), (ffs, xn2t, dgate), (2 * ffs, xn2t, dup)):
            part = nn(left[...], right).astype(BF16)
            for t in range(count):
                grads[base + first + t] = part[:, t * LANES : (t + 1) * LANES]

    loop("feed", 0, ffs // 2, lambda j: feed(j, 2))
    feed(ffs // 2, 1)
    after(("last", 0))

    outs[...] = (h[...] + nn(hid[...], wout[...])).astype(BF16)
    after(("mix", 0))

    acc[...] = nt(dgu[...], win[...])
    unit2, grad2 = dh[...], acc[...]
    gain_terms = jnp.sum(grad2 * unit2, axis=0, keepdims=True)
    grads[3 * ffs + pairs] = jnp.broadcast_to(gain_terms, (LANES, width)).T.astype(BF16)
    dh[...] = cs[...].astype(F32) + norm_back(grad2, unit2, rms[...], gain2)
    after(("norm", 0))

    datt = dh[...].astype(BF16)
    att_t = att[...].T
    for j in range(pairs // 2):
        both = nn(att_t, datt[:, 2 * j * LANES : (2 * j + 2) * LANES]).astype(BF16)
        for t in range(2):
            grads[3 * ffs + 2 * j + t] = both[:, t * LANES : (t + 1) * LANES]
    after(("wo", 0))

    do[...] = nt(datt, wo[...]).astype(BF16)
    lane = lax.broadcasted_iota(jnp.int32, (16, width), 1)
    row = lax.broadcasted_iota(jnp.int32, (16, width), 0)
    pick = jnp.where(lane // HEAD_DIM == row, 1.0, 0.0).astype(BF16)
    product = do[...].astype(F32) * att[...].astype(F32)
    high = product.astype(BF16)
    sums = nt(pick, high) + nt(pick, (product - high.astype(F32)).astype(BF16))
    for j in range(pairs):
        dd[j] = sums[2 * j : 2 * j + 2]
    after(("do", 0))

    dqkv, xnt, dx = win.at[pl.ds(0, tokens)], xn2t, do
    away, own = (xn2, att), (h, acc)
    xnt[...] = xn[...].T

    def attend_back(keys, j):
        lanes = tile(j)
        q2, do2 = q[:, lanes], do[:, lanes]
        k2, v2 = k[keys, lanes], v[keys, lanes]
        kt = k2.T
        dks, dvs, dqs = [], [], []
        for sub in range(2):
            probs = jnp.exp(nt(one_head(k2, sub), q2) - lse[j, sub : sub + 1, :])
            dprobs = nt(one_head(v2, sub), do2)
            dscores = (probs * (dprobs - dd[j, sub : sub + 1, :])).astype(BF16)
            dvs.append(nn(probs.astype(BF16), do2))
            dks.append(nn(dscores, q2))
            dqs.append(nn(kt[sub * HEAD_DIM : (sub + 1) * HEAD_DIM], dscores))
        low = lane_of(dks[0].shape) < HEAD_DIM
        return jnp.where(low, dks[0], dks[1]), jnp.where(low, dvs[0], dvs[1]), jnp.concatenate(dqs, axis=0)

    def unrope(part):
        return (part * cos[...] - turned(part) * sin[...]).astype(BF16)

    def far(j):
        dk, dv, dq = attend_back(pl.ds(tokens, tokens), j)
        away[0][:, tile(j)] = dk.astype(BF16)
        away[1][:, tile(j)] = dv.astype(BF16)
        dqt[j] = dq

    def near(j):
        dk, dv, dq = attend_back(pl.ds(0, tokens), j)
        own[0][:, tile(j)] = dk
        own[1][:, tile(j)] = dv
        dqkv[:, tile(j)] = unrope((dqt[j] + dq).T * 0.125)

    def join(j, _):
        dqkv[:, tile(j, width)] = unrope(own[0][:, tile(j)] + landed[0, :, tile(j)].astype(F32))
        dqkv[:, tile(j, 2 * width)] = (own[1][:, tile(j)] + landed[1, :, tile(j)].astype(F32)).astype(BF16)
        return 0

    base = 3 * ffs + pairs + 1
    for part, (low, high) in enumerate(((0, FIRST_PAIRS), (FIRST_PAIRS, pairs))):
        loop("far", low, high, far)
        lanes = pl.ds(low * LANES, (high - low) * LANES)
        sends = [
            pltpu.make_async_remote_copy(
                src_ref=away[i].at[:, lanes], dst_ref=landed.at[i, :, lanes],
                send_sem=kv_send.at[8 + 2 * part + i], recv_sem=kv_recv.at[8 + 2 * part + i],
                device_id=sibling, device_id_type=MESH,
            )
            for i in range(2)
        ]
        for send in sends:
            send.start()
        loop("near", low, high, near)
        for send in sends:
            send.wait()
        lax.fori_loop(low, high, join, 0)

        def weight_grads(j, _):
            for third in range(3):
                both = nn(xnt[...], dqkv[:, tile(j, third * width, 2)]).astype(BF16)
                for t in range(2):
                    grads[base + third * pairs + 2 * j + t] = both[:, t * LANES : (t + 1) * LANES]
            return 0

        lax.fori_loop(low // 2, high // 2, weight_grads, 0)
        after(("join", part))

    grad1 = nt(dqkv[...], wqkv[...])
    unit, scale = row_stats(xs[...].astype(F32))
    dx[...] = (dh[...] + norm_back(grad1, unit, scale, gain1)).astype(BF16)
    after(("dx", 0))
    reducer.settle()
    after("end")

    spread(x_in, xs, 0, wait_sent)
    spread(cot_in, cs, 4, wait_sent)
    for src, dst, base in ((outs, out_o, 8), (dx, dx_o, 12)):
        for n in range(n_seq):
            gather(src, dst, base, n, wait_sent)
        for block in range(2):
            for part in range(2):
                wait_bytes(dst.at[block, pl.ds(part * half, half)], recv_sem.at[base + 2 * block + part])


def layer(n_doc, n_seq, inputs, cotangent, gain1, gain2, wqkv, wo, win, wout, cos, sin):
    blocks, rows, width = inputs.shape
    tokens = blocks * rows
    ff = wout.shape[0]
    pairs = width // LANES
    streams, _, total = stream_plan(width, ff)
    rounds = log2(n_doc) - 1 + log2(n_seq)
    kept = halvings(width, rounds)
    legs = 2 + rounds + sum(1 for _, split in kept if split)
    slots = sum(stream.count for stream in streams)
    hbm, vmem = pl.BlockSpec(memory_space=pl.ANY), pl.BlockSpec(memory_space=pltpu.VMEM)
    sds, dma = jax.ShapeDtypeStruct, pltpu.SemaphoreType.DMA
    row_b = pltpu.VMEM((tokens, width), BF16)
    row_f = pltpu.VMEM((tokens, width), F32)
    return pl.pallas_call(
        functools.partial(layer_kernel, n_doc, n_seq),
        out_shape=[
            sds((blocks, rows, width), BF16), sds((blocks, rows, width), BF16), sds((total, width, LANES), BF16),
        ],
        in_specs=[hbm, hbm, vmem, vmem] + [hbm] * 6,
        out_specs=[hbm] * 3,
        scratch_shapes=[
            row_b, row_b, row_b,
            pltpu.VMEM(wqkv.shape, BF16), pltpu.VMEM(wo.shape, BF16), pltpu.VMEM(win.shape, BF16), pltpu.VMEM(wout.shape, BF16),
            pltpu.VMEM((tokens, LANES), F32), pltpu.VMEM((tokens, LANES), F32),
            row_b, row_b, pltpu.VMEM((2 * tokens, width), BF16), pltpu.VMEM((2 * tokens, width), BF16),
            row_b, row_f, row_b, pltpu.VMEM((width, tokens), BF16),
            pltpu.VMEM((tokens, ff), BF16), pltpu.VMEM((tokens, 2 * ff), BF16), pltpu.VMEM((width, tokens), BF16),
            row_b, row_f, row_f,
            pltpu.VMEM((pairs, 2, tokens), F32), pltpu.VMEM((pairs, 2, tokens), F32),
            pltpu.VMEM((pairs, LANES, tokens), F32), pltpu.VMEM((2, tokens, width), BF16),
            pltpu.VMEM((total, width, LANES), BF16),
            pltpu.VMEM((slots, Reducer.landing_rows(width, rounds), LANES), BF16),
            pltpu.VMEM((slots, width, LANES), BF16), pltpu.VMEM((tokens, 1), F32),
            dma((12,)), dma((16,)), dma((16,)), dma((12,)), dma((12,)),
            dma((len(streams), legs)), dma((len(streams), legs)), dma((len(streams),)),
        ],
        compiler_params=pltpu.CompilerParams(collective_id=0, has_side_effects=True, vmem_limit_bytes=VMEM_LIMIT),
        name="layer",
    )(inputs, cotangent, gain1, gain2, wqkv, wo, win, wout, cos, sin)


def widen_kernel(ff, width, g, wqkv, gain1, out, dx, dqkv_o, dwo_o, dwin_o, dwout_o, gain1_o, gain2_o, out_o, dx_o):
    out_o[...] = out[...]
    dx_o[...] = dx[...]
    ffs, pairs = ff // LANES, width // LANES
    base = 3 * ffs + pairs + 1
    for j in range(ffs):
        dwout_o[j * LANES : (j + 1) * LANES, :] = g[j].astype(F32).T
    for j in range(2 * ffs):
        dwin_o[:, j * LANES : (j + 1) * LANES] = g[ffs + j].astype(F32)
    for j in range(pairs):
        dwo_o[:, j * LANES : (j + 1) * LANES] = g[3 * ffs + j].astype(F32)
    gain2_o[...] = g[base - 1].astype(F32).T[0]
    along = jnp.zeros((LANES, LANES), F32)
    for j in range(3 * pairs):
        lanes = slice(j * LANES, (j + 1) * LANES)
        part = g[base + j].astype(F32)
        dqkv_o[:, lanes] = part
        along += part * wqkv[:, lanes].astype(F32)
    total = jnp.sum(along.T, axis=0, keepdims=True)
    gain1_o[...] = (total / gain1[...].reshape(1, LANES))[0]


def widen(ff, g, wqkv, gain1, out, dx):
    total, width, _ = g.shape
    sds = jax.ShapeDtypeStruct
    across = lambda i: (i, 0)
    down = lambda i: (0, i)
    flat = pl.BlockSpec((LANES,), lambda i: (i,))
    blocks, rows, _ = out.shape
    token = pl.BlockSpec((blocks, rows, LANES), lambda i: (0, 0, i))
    return pl.pallas_call(
        functools.partial(widen_kernel, ff, width),
        grid=(width // LANES,),
        out_shape=[
            sds(wqkv.shape, F32), sds((width, width), F32), sds((width, 2 * ff), F32), sds((ff, width), F32),
            sds((width,), F32), sds((width,), F32), sds(out.shape, BF16), sds(dx.shape, BF16),
        ],
        in_specs=[
            pl.BlockSpec((total, LANES, LANES), lambda i: (0, i, 0)), pl.BlockSpec((LANES, wqkv.shape[1]), across), flat, token, token,
        ],
        out_specs=[
            pl.BlockSpec((LANES, wqkv.shape[1]), across), pl.BlockSpec((LANES, width), across),
            pl.BlockSpec((LANES, 2 * ff), across), pl.BlockSpec((ff, LANES), down), flat, flat, token, token,
        ],
        compiler_params=pltpu.CompilerParams(vmem_limit_bytes=VMEM_LIMIT),
        name="widen",
    )(g, wqkv, gain1, out, dx)


def rotary_tables(length):
    half = HEAD_DIM // 2
    frequency = ROPE_THETA ** (-(np.arange(half) * 2.0) / HEAD_DIM)
    angles = np.arange(length)[:, None] * frequency[None, :]
    cos, sin = np.cos(angles), np.sin(angles)
    per_tile = LANES // HEAD_DIM
    cos = np.tile(np.concatenate([cos, cos], axis=1), (1, per_tile))
    sin = np.tile(np.concatenate([-sin, sin], axis=1), (1, per_tile))
    return jnp.asarray(cos, F32), jnp.asarray(sin, F32)


def per_device(
    n_doc, n_seq,
    inputs, attn_gain, qkv_weight, attn_out_weight, mlp_gain, mlp_in_weight, mlp_out_weight, cotangent,
):
    blocks, rows, width = inputs.shape
    ff = mlp_out_weight.shape[0]
    cos, sin = rotary_tables(rows * n_seq)
    output, dx, grads = layer(
        n_doc, n_seq, inputs, cotangent, attn_gain, mlp_gain,
        qkv_weight, attn_out_weight, mlp_in_weight, mlp_out_weight, cos, sin,
    )
    dqkv, dwo, dwin, dwout, dgain1, dgain2, output, dx = widen(ff, grads, qkv_weight, attn_gain, output, dx)
    return output, dx, dgain1, dqkv, dwo, dgain2, dwin, dwout


def solution(mesh):
    n_doc, n_seq = mesh.shape["doc"], mesh.shape["seq"]
    placed = (P("doc", "seq", None), P(), P(), P(), P(), P(), P(), P("doc", "seq", None))
    return jax.shard_map(
        functools.partial(per_device, n_doc, n_seq),
        mesh=mesh,
        in_specs=placed,
        out_specs=(P("doc", "seq", None), P("doc", "seq", None), P(), P(), P(), P(), P(), P()),
        check_vma=False,
    )
```

```python
import functools

import jax
import jax.numpy as jnp
import numpy as np
from jax import lax
from jax.experimental import pallas as pl
from jax.experimental.pallas import tpu as pltpu
from jax.sharding import PartitionSpec as P

HEAD_DIM = 64
ROPE_THETA = 160000.0
NORM_EPSILON = 1e-05
F32 = jnp.float32
BF16 = jnp.bfloat16
MESH = pl.DeviceIdType.MESH
LANES = 128
VMEM_LIMIT = 60 << 20


def nn(a, b):
    return lax.dot_general(a, b, (((1,), (0,)), ((), ())), preferred_element_type=F32)


def nt(a, b):
    return lax.dot_general(a, b, (((1,), (1,)), ((), ())), preferred_element_type=F32)


def lane_of(shape):
    return lax.broadcasted_iota(jnp.int32, shape, 1)


def one_head(pair, sub):
    lane = lane_of(pair.shape)
    mine = (lane < HEAD_DIM) if sub == 0 else (lane >= HEAD_DIM)
    return jnp.where(mine, pair, jnp.zeros_like(pair))


def turned(values):
    back = pltpu.roll(values, HEAD_DIM // 2, 1)
    ahead = pltpu.roll(values, LANES - HEAD_DIM // 2, 1)
    return jnp.where(lane_of(values.shape) % HEAD_DIM < HEAD_DIM // 2, ahead, back)


def row_stats(values):
    mean = jnp.mean(values, axis=1, keepdims=True)
    centered = values - mean
    scale = lax.rsqrt(jnp.mean(centered * centered, axis=1, keepdims=True) + NORM_EPSILON)
    return centered * scale, scale


def norm_back(grad, unit, scale, gain):
    weighted = grad * gain
    along = jnp.mean(weighted, axis=1, keepdims=True)
    across = jnp.mean(weighted * unit, axis=1, keepdims=True)
    return scale * (weighted - along - unit * across)


def bit_of(index, weight):
    return (index // weight) % 2


def flipped(index, weight):
    return index + weight - 2 * weight * bit_of(index, weight)


def greet(partners):
    barrier = pltpu.get_barrier_semaphore()
    for partner in partners:
        pl.semaphore_signal(barrier, inc=1, device_id=partner, device_id_type=MESH)
    pl.semaphore_wait(barrier, len(partners))


def group_partners(doc, seq, n_seq):
    core = doc % 2
    found = []
    for other_core in range(2):
        for step in range(n_seq):
            if other_core == 0 and step == 0:
                continue
            found.append(
                (doc - core + (core + other_core) % 2, (seq + step) % n_seq)
            )
    return found


class Exchange:
    def __init__(self, doc, seq, n_seq):
        assert n_seq == 4
        core = doc % 2
        self.doc, self.seq, self.core = doc, seq, core
        self.base = doc - core
        side = seq // 2
        self.near_first = [seq, flipped(seq, 1), 2 - side, 3 - 3 * side]
        self.block_first = (1 - core) * side

    def out_piece(self, n):
        block = self.block_first + n // 2 - 2 * self.block_first * (n // 2)
        half = n % 2
        return block, half, (self.base + half, 2 * self.core + block)

    def back_target(self, quarter):
        return (self.base + self.seq // 2, quarter)

    def is_self(self, target):
        return jnp.logical_and(target[0] == self.doc, target[1] == self.seq)


def send_or_keep(ex, target, src, dst, send_sem, recv_sem):
    mine = ex.is_self(target)

    @pl.when(mine)
    def _():
        pltpu.make_async_copy(src, dst, recv_sem).start()

    @pl.when(jnp.logical_not(mine))
    def _():
        pltpu.make_async_remote_copy(
            src_ref=src, dst_ref=dst, send_sem=send_sem, recv_sem=recv_sem,
            device_id=target, device_id_type=MESH,
        ).start()


def wait_sent(ex, target, src, dst, send_sem, recv_sem):
    @pl.when(jnp.logical_not(ex.is_self(target)))
    def _():
        pltpu.make_async_remote_copy(
            src_ref=src, dst_ref=dst, send_sem=send_sem, recv_sem=recv_sem,
            device_id=target, device_id_type=MESH,
        ).wait_send()


def wait_bytes(ref, sem):
    pltpu.make_async_copy(ref, ref, sem).wait()


LINK_RATE, CORE_RATE, ROUND_LATENCY, SPARE = 44135.0, 510e3, 2.6, 1.5
NEAR_SHARE, FAR_SHARE = 1.0, 0.25
STEP_TIME, ADD_TIME = 0.1, 0.4e-6
PIECE_TIME = {"feed": 2.0, "last": 1.1, "mix": 1.2, "norm": 3.5, "wo": 1.0, "do": 1.4, "far": 1.25, "near": 1.25, "join": 2.5, "dx": 4.0}
FIRST_PAIRS = 4
ORDERS = "11000110001010111001101100"
OUT, DX = -1, -2
OUT_AFTER, DX_GAP = (5, 5, 5, 8), 14.0


def log2(n):
    return n.bit_length() - 1


class Stream:
    def __init__(self, first, second, count):
        self.first, self.second, self.count = first, second, count


def halvings(rows, rounds):
    kept, extent = [], rows
    for _ in range(rounds):
        split = (extent // 2) % 16 == 0
        extent = extent // 2 if split else extent
        kept.append((extent, split))
    return kept


def axes_of(n_doc, n_seq):
    doc_axes = [("doc", 1 << i) for i in range(1, log2(n_doc))]
    seq_axes = [("seq", 1 << i) for i in range(log2(n_seq))]
    return doc_axes, seq_axes


def axis_order(index, n_doc, n_seq):
    doc_axes, seq_axes = axes_of(n_doc, n_seq)
    code = int(ORDERS[index % len(ORDERS)])
    turn = code % 2 * (len(doc_axes) // 2)
    doc_axes = doc_axes[turn:] + doc_axes[:turn]
    place = len(doc_axes) * (2 - code // 2) // 2
    return doc_axes[:place] + seq_axes[:-1] + doc_axes[place:] + seq_axes[-1:]


def stream_plan(width, ff):
    ffs, pairs = ff // LANES, width // LANES
    streams, ready = [], {}

    def add(piece, first, second, count):
        ready.setdefault(piece, []).append(len(streams))
        streams.append(Stream(first, second, count))

    assert ffs % 2 == 1 and pairs % 2 == 0
    covered = ffs - 1
    for low in range(0, covered, 2):
        for base in (0, ffs, 2 * ffs):
            add(("feed", low // 2), base + low, base + low + 1, 1)
    add(("last", 0), covered, ffs + covered, 1)
    add(("norm", 0), 2 * ffs + covered, 3 * ffs + pairs, 1)
    for start in range(3 * ffs, 3 * ffs + pairs, 2):
        add(("wo", 0), start, start + 1, 1)
    base = 3 * ffs + pairs + 1
    for part, (low, high) in enumerate(((0, FIRST_PAIRS), (FIRST_PAIRS, pairs))):
        for third in range(3):
            for start in range(base + third * pairs + low, base + third * pairs + high, 2):
                add(("join", part), start, start + 1, 1)
    return streams, ready, base + 3 * pairs


def piece_list(ff, pairs):
    ffs = ff // LANES
    pieces = [("feed", j) for j in range(ffs // 2)] + [("last", 0)]
    pieces += [("mix", 0), ("norm", 0), ("wo", 0), ("do", 0)]
    for part, (low, high) in enumerate(((0, FIRST_PAIRS), (FIRST_PAIRS, pairs))):
        pieces += [("far", j) for j in range(low, high)] + [("near", j) for j in range(low, high)]
        pieces.append(("join", part))
    return pieces + [("dx", 0)]


def agenda(streams, ready, pieces, rows, n_doc, n_seq):
    rounds = log2(n_doc) - 1 + log2(n_seq)
    kept = halvings(rows, rounds)
    ups = [r for r in reversed(range(rounds)) if kept[r][1]]
    free, flying, steps = {}, [], {}
    near, far = axes_of(n_doc, n_seq)[1]

    def legs(index):
        order = axis_order(index, n_doc, n_seq)
        unit = streams[index].count * LANES * 2
        trip = [("core", rows * unit)]
        trip += [(order[r], kept[r][0] * unit) for r in range(rounds)]
        trip += [(order[r], kept[r][0] * unit) for r in ups]
        return trip + [("core", rows * unit)]

    def occupy(axis, size, when):
        rate = CORE_RATE if axis == "core" else LINK_RATE / 2 if axis == far else LINK_RATE
        begin = max(when, free.get(axis, 0.0))
        free[axis] = begin + size / rate
        for axis_from, axis_to, share, speed in ((far, near, NEAR_SHARE, LINK_RATE), (near, far, FAR_SHARE, LINK_RATE / 2)):
            if axis == axis_from and share:
                free[axis_to] = max(free.get(axis_to, 0.0), begin) + share * size / speed
        return free[axis]

    def leave(chunk, when):
        if chunk:
            occupy(near if chunk == 1 else far, 196e3, when)

    def depart(index, leg, when):
        flying.append((occupy(*legs(index)[leg], when) + ROUND_LATENCY, index, leg))

    def serve(now):
        flying.sort()
        done, index, leg = flying.pop(0)
        trip = legs(index)
        now = max(now, done) + STEP_TIME + (trip[leg][1] * ADD_TIME if leg <= rounds else 0.0)
        if leg + 1 < len(trip):
            depart(index, leg + 1, now)
        return now, (index, leg)

    now = 0.0
    for piece in pieces:
        now += PIECE_TIME[piece[0]]
        actions = steps.setdefault(piece, [])
        for index in ready.get(piece, ()):
            actions.append((index, -1))
            depart(index, 0, now)
            now += STEP_TIME
        for chunk, place in enumerate(OUT_AFTER):
            if piece == pieces[place]:
                actions.append((OUT, chunk))
                leave(chunk, now)
                now += STEP_TIME
        while flying and min(flying)[0] + SPARE <= now:
            now, action = serve(now)
            actions.append(action)
    last = steps.setdefault("end", [])
    begin, chunk = now, 0
    while flying or chunk < n_seq:
        upcoming = max(now, min(flying)[0]) if flying else now
        if chunk < n_seq and (not flying or upcoming >= begin + chunk * DX_GAP):
            leave(chunk, now)
            last.append((DX, chunk))
            now += STEP_TIME
            chunk += 1
            continue
        now, action = serve(now)
        last.append(action)
    return steps


class Reducer:
    def __init__(self, streams, n_doc, n_seq, doc, seq, grads, landing, final, out, send_sem, recv_sem, own_sem):
        self.streams, self.grads, self.landing, self.final, self.out = streams, grads, landing, final, out
        self.send_sem, self.recv_sem, self.own_sem = send_sem, recv_sem, own_sem
        self.busy, self.unsent = False, []
        self.core = doc % 2
        self.rows = grads.shape[1]
        self.rounds = log2(n_doc) - 1 + log2(n_seq)
        self.kept = halvings(self.rows, self.rounds)
        self.ups = [r for r in reversed(range(self.rounds)) if self.kept[r][1]]
        self.legs = 2 + self.rounds + len(self.ups)
        self.sibling = (flipped(doc, 1), seq)
        self.bits, self.partners = {}, {}
        for name, weight in sum(axes_of(n_doc, n_seq), []):
            index = doc if name == "doc" else seq
            self.bits[name, weight] = bit_of(index, weight)
            self.partners[name, weight] = (flipped(doc, weight), seq) if name == "doc" else (doc, flipped(seq, weight))
        self.orders = [axis_order(i, n_doc, n_seq) for i in range(len(streams))]
        self.slots, used = [], 0
        for stream in streams:
            self.slots.append(pl.ds(used, stream.count))
            used += stream.count
        self.plans = []
        for order in self.orders:
            offset, base, plan = 0, 0, []
            for (keep, split), axis in zip(self.kept, order):
                bit = self.bits[axis]
                mine = offset + bit * keep if split else offset
                theirs = offset + (1 - bit) * keep if split else offset
                plan.append((mine, theirs, base, keep))
                base += keep
                offset = mine
            self.plans.append(plan)

    @staticmethod
    def landing_rows(rows, rounds):
        return sum(keep for keep, _ in halvings(rows, rounds))

    def tiles(self, index, other=False):
        stream = self.streams[index]
        side = 1 - self.core if other else self.core
        return pl.ds(stream.first + side * (stream.second - stream.first), stream.count)

    def span(self, start, extent):
        return pl.ds(start if isinstance(start, int) else pl.multiple_of(start, 16), extent)

    def copy(self, index, leg, receiving=False):
        slot = self.slots[index]
        if leg == 0:
            src, dst, partner = self.grads.at[self.tiles(index, True)], self.final.at[slot], self.sibling
        elif leg <= self.rounds:
            mine, theirs, base, keep = self.plans[index][leg - 1]
            src = self.grads.at[self.tiles(index), self.span(theirs, keep)]
            dst, partner = self.landing.at[slot, pl.ds(base, keep)], self.partners[self.orders[index][leg - 1]]
        elif leg < self.legs - 1:
            r = self.ups[leg - 1 - self.rounds]
            mine, theirs, base, keep = self.plans[index][r]
            src = dst = self.final.at[slot, self.span(theirs if receiving else mine, keep)]
            partner = self.partners[self.orders[index][r]]
        else:
            src, dst, partner = self.final.at[slot], self.out.at[self.tiles(index, receiving)], self.sibling
        return pltpu.make_async_remote_copy(
            src_ref=src, dst_ref=dst, send_sem=self.send_sem.at[index, leg], recv_sem=self.recv_sem.at[index, leg],
            device_id=partner, device_id_type=MESH,
        )

    def own(self, index):
        return pltpu.make_async_copy(self.final.at[self.slots[index]], self.out.at[self.tiles(index)], self.own_sem.at[index])

    def add(self, index, leg):
        stream, slot = self.streams[index], self.slots[index]
        start = stream.first + self.core * (stream.second - stream.first)
        low = slot.start
        if leg == 0:
            mine, base, keep = 0, 0, self.rows
        else:
            mine, _, base, keep = self.plans[index][leg - 1]
        block = keep
        while block > 96:
            block //= 2

        def body(i, _):
            here = self.span(mine + i * block, block)
            for t in range(stream.count):
                if leg == 0:
                    other = self.final[low + t, here]
                else:
                    other = self.landing[low + t, self.span(base + i * block, block)]
                total = (self.grads[start + t, here].astype(F32) + other.astype(F32)).astype(BF16)
                if leg == self.rounds:
                    self.final[low + t, here] = total
                else:
                    self.grads[start + t, here] = total
            return 0

        lax.fori_loop(0, keep // block, body, 0)

    def settle(self):
        self.busy = False
        for index, leg in self.unsent:
            self.copy(index, leg).wait_send()

    def act(self, index, leg):
        if leg >= 0:
            if self.busy:
                self.unsent.append((index, leg))
            else:
                self.copy(index, leg).wait_send()
            self.copy(index, leg, True).wait_recv()
            if leg <= self.rounds:
                self.add(index, leg)
            if leg == self.legs - 1:
                self.own(index).wait()
        if leg + 1 < self.legs:
            self.copy(index, leg + 1).start()
        if leg + 1 == self.legs - 1:
            self.own(index).start()


def layer_kernel(
    n_doc, n_seq,
    x_in, cot_in, gain1_in, gain2_in, wqkv_in, wo_in, win_in, wout_in, cos_in, sin_in,
    out_o, dx_o, g_o,
    xs, cs, outs, wqkv, wo, win, wout, cos, sin, xn, q, k, v, att, h, xn2, xn2t, hid, dgu, dmt, do, dh, acc, lse, dd,
    dqt, landed, grads, landing, final, rms,
    w_sem, send_sem, recv_sem, kv_send, kv_recv, sum_send, sum_recv, own_sem,
):
    doc, seq = lax.axis_index("doc"), lax.axis_index("seq")
    core = doc % 2
    ex = Exchange(doc, seq, n_seq)
    half = x_in.shape[1] // 2
    tokens, width = xs.shape
    ff = wout.shape[0]
    ffs, pairs = ff // LANES, width // LANES
    sibling = (flipped(doc, 1), seq)

    loads = [
        pltpu.make_async_copy(s, d, w_sem.at[i])
        for i, (s, d) in enumerate(
            [(wqkv_in, wqkv), (wo_in, wo), (win_in, win), (wout_in, wout)]
            + [
                (t.at[pl.ds((2 * quarter + core) * half, half)], d.at[pl.ds(quarter * half, half)])
                for t, d in ((cos_in, cos), (sin_in, sin))
                for quarter in range(n_seq)
            ]
        )
    ]
    loads[0].start()
    for load in loads[4:]:
        load.start()
    greet(group_partners(doc, seq, n_seq) + [(flipped(doc, w), seq) for _, w in axes_of(n_doc, n_seq)[0]])

    def rows_of(slot):
        return pl.ds(pl.multiple_of(slot * half, half), half)

    def spread(src, dst, base, act):
        for n in range(n_seq):
            block, part, target = ex.out_piece(n)
            act(
                ex, target, src.at[block, pl.ds(part * half, half)], dst.at[rows_of(seq)],
                send_sem.at[base + n], recv_sem.at[base + seq],
            )

    def gather(src, dst, base, n, act):
        quarter = ex.near_first[n]
        act(
            ex, ex.back_target(quarter), src.at[rows_of(quarter)], dst.at[seq % 2, rows_of(core)],
            send_sem.at[base + n], recv_sem.at[base + 2 * (seq % 2) + core],
        )

    spread(x_in, xs, 0, send_or_keep)
    for load in loads[1:4]:
        load.start()
    gain1, gain2 = gain1_in[...].reshape(1, width), gain2_in[...].reshape(1, width)

    streams, ready, _ = stream_plan(width, ff)
    steps = agenda(streams, ready, piece_list(ff, pairs), width, n_doc, n_seq)
    reducer = Reducer(streams, n_doc, n_seq, doc, seq, grads, landing, final, g_o, sum_send, sum_recv, own_sem)

    def after(piece):
        for index, leg in steps.get(piece, ()):
            if index == OUT:
                gather(outs, out_o, 8, leg, send_or_keep)
            elif index == DX:
                gather(do, dx_o, 12, leg, send_or_keep)
            else:
                reducer.act(index, leg)

    def loop(name, low, high, body):
        def one(j, _):
            body(j)
            for at in range(low, high):
                if steps.get((name, at)):
                    pl.when(j == at)(functools.partial(after, (name, at)))
            return 0

        lax.fori_loop(low, high, one, 0)

    def tile(j, base=0, count=1):
        return pl.ds(pl.multiple_of(base + j * LANES * count, LANES), LANES * count)

    def roped(part, here, scale):
        return ((part * cos[here] + turned(part) * sin[here]) * scale).astype(BF16)

    def kv_copies(n):
        here = rows_of(ex.near_first[n])
        there = pl.ds(pl.multiple_of(tokens + ex.near_first[n] * half, half), half)
        return [
            pltpu.make_async_remote_copy(
                src_ref=ref.at[here], dst_ref=ref.at[there], send_sem=kv_send.at[2 * n + i],
                recv_sem=kv_recv.at[2 * n + i], device_id=sibling, device_id_type=MESH,
            )
            for i, ref in enumerate((k, v))
        ]

    loads[0].wait()
    for load in loads[4:]:
        load.wait()
    for n in range(n_seq):
        here = rows_of(ex.near_first[n])
        wait_bytes(xs.at[here], recv_sem.at[ex.near_first[n]])
        if n == n_seq - 2:
            spread(cot_in, cs, 4, send_or_keep)
        unit, _ = row_stats(xs[here].astype(F32))
        normed = (unit * gain1).astype(BF16)
        xn[here] = normed

        def project(j, _, here=here):
            weights = jnp.concatenate([wqkv[:, tile(j, width)], wqkv[:, tile(j, 2 * width)]], axis=1)
            both = nn(xn[here], weights)
            k[here, tile(j)] = roped(both[:, :LANES], here, 1.0)
            v[here, tile(j)] = both[:, LANES:].astype(BF16)
            return 0

        lax.fori_loop(0, pairs, project, 0)
        for copy in kv_copies(n):
            copy.start()

        def project_q(j, _, here=here):
            both = nn(xn[here], wqkv[:, tile(j, 0, 2)])
            for t in range(2):
                q[here, tile(2 * j + t)] = roped(both[:, t * LANES : (t + 1) * LANES], here, 0.125)
            return 0

        lax.fori_loop(0, pairs // 2, project_q, 0)

    def attend(j):
        lanes = tile(j)
        k2, vt, q2 = k[:, lanes], v[:, lanes].T, q[:, lanes]
        scores = [nt(one_head(k2, sub), q2) for sub in range(2)]
        mixed = []
        for sub in range(2):
            top = jnp.max(scores[sub], axis=0, keepdims=True)
            weights = jnp.exp(scores[sub] - top)
            total = jnp.sum(weights, axis=0, keepdims=True)
            lse[j, sub : sub + 1, :] = top + jnp.log(total)
            mixed.append(
                nn(vt[sub * HEAD_DIM : (sub + 1) * HEAD_DIM], weights.astype(BF16)) * (1.0 / total)
            )
        att[:, lanes] = jnp.concatenate(mixed, axis=0).T.astype(BF16)

    def attend_group(group, _):
        for j in range(pairs // 2):
            attend(group * (pairs // 2) + j)
        return 0

    for n in range(n_seq):
        for copy in kv_copies(n):
            copy.wait()
    lax.fori_loop(0, 2, attend_group, 0)

    loads[1].wait()
    h[...] = xs[...].astype(F32) + nn(att[...], wo[...])
    unit2, scale2 = row_stats(h[...])
    dh[...] = unit2
    rms[...] = scale2
    xn2[...] = (unit2 * gain2).astype(BF16)
    xn2t[...] = xn2[...].T
    loads[2].wait()
    loads[3].wait()
    for slot in range(n_seq):
        wait_bytes(cs.at[rows_of(slot)], recv_sem.at[4 + slot])
    dmt[...] = cs[...].T

    def feed(j, count):
        first = 2 * j
        wide = count * LANES
        lanes = pl.ds(pl.multiple_of(first * LANES, LANES), wide)
        up_lanes = pl.ds(pl.multiple_of(ff + first * LANES, LANES), wide)
        gate, up = nn(xn2[...], win[:, lanes]), nn(xn2[...], win[:, up_lanes])
        phi = 0.5 * (1.0 + lax.erf(gate * 0.7071067811865476))
        slope = phi + gate * (0.3989422804014327 * jnp.exp(-0.5 * gate * gate))
        active = gate * phi
        inner = (active * up).astype(BF16)
        hid[:, lanes] = inner
        dhid = nt(cs[...], wout[lanes, :])
        dgate, dup = (dhid * up * slope).astype(BF16), (dhid * active).astype(BF16)
        dgu[:, lanes] = dgate
        dgu[:, up_lanes] = dup
        for base, left, right in ((0, dmt, inner), (ffs, xn2t, dgate), (2 * ffs, xn2t, dup)):
            part = nn(left[...], right).astype(BF16)
            for t in range(count):
                grads[base + first + t] = part[:, t * LANES : (t + 1) * LANES]

    loop("feed", 0, ffs // 2, lambda j: feed(j, 2))
    feed(ffs // 2, 1)
    after(("last", 0))

    outs[...] = (h[...] + nn(hid[...], wout[...])).astype(BF16)
    after(("mix", 0))

    acc[...] = nt(dgu[...], win[...])
    unit2, grad2 = dh[...], acc[...]
    gain_terms = jnp.sum(grad2 * unit2, axis=0, keepdims=True)
    grads[3 * ffs + pairs] = jnp.broadcast_to(gain_terms, (LANES, width)).T.astype(BF16)
    dh[...] = cs[...].astype(F32) + norm_back(grad2, unit2, rms[...], gain2)
    after(("norm", 0))

    datt = dh[...].astype(BF16)
    att_t = att[...].T
    for j in range(pairs // 2):
        both = nn(att_t, datt[:, 2 * j * LANES : (2 * j + 2) * LANES]).astype(BF16)
        for t in range(2):
            grads[3 * ffs + 2 * j + t] = both[:, t * LANES : (t + 1) * LANES]
    after(("wo", 0))

    do[...] = nt(datt, wo[...]).astype(BF16)
    lane = lax.broadcasted_iota(jnp.int32, (16, width), 1)
    row = lax.broadcasted_iota(jnp.int32, (16, width), 0)
    pick = jnp.where(lane // HEAD_DIM == row, 1.0, 0.0).astype(BF16)
    product = do[...].astype(F32) * att[...].astype(F32)
    high = product.astype(BF16)
    sums = nt(pick, high) + nt(pick, (product - high.astype(F32)).astype(BF16))
    for j in range(pairs):
        dd[j] = sums[2 * j : 2 * j + 2]
    after(("do", 0))

    dqkv, xnt, dx = win.at[pl.ds(0, tokens)], xn2t, do
    away, own = (xn2, att), (h, acc)
    xnt[...] = xn[...].T

    def attend_back(keys, j):
        lanes = tile(j)
        q2, do2 = q[:, lanes], do[:, lanes]
        k2, v2 = k[keys, lanes], v[keys, lanes]
        kt = k2.T
        dks, dvs, dqs = [], [], []
        for sub in range(2):
            probs = jnp.exp(nt(one_head(k2, sub), q2) - lse[j, sub : sub + 1, :])
            dprobs = nt(one_head(v2, sub), do2)
            dscores = (probs * (dprobs - dd[j, sub : sub + 1, :])).astype(BF16)
            dvs.append(nn(probs.astype(BF16), do2))
            dks.append(nn(dscores, q2))
            dqs.append(nn(kt[sub * HEAD_DIM : (sub + 1) * HEAD_DIM], dscores))
        low = lane_of(dks[0].shape) < HEAD_DIM
        return jnp.where(low, dks[0], dks[1]), jnp.where(low, dvs[0], dvs[1]), jnp.concatenate(dqs, axis=0)

    def unrope(part):
        return (part * cos[...] - turned(part) * sin[...]).astype(BF16)

    def far(j):
        dk, dv, dq = attend_back(pl.ds(tokens, tokens), j)
        away[0][:, tile(j)] = dk.astype(BF16)
        away[1][:, tile(j)] = dv.astype(BF16)
        dqt[j] = dq

    def near(j):
        dk, dv, dq = attend_back(pl.ds(0, tokens), j)
        own[0][:, tile(j)] = dk
        own[1][:, tile(j)] = dv
        dqkv[:, tile(j)] = unrope((dqt[j] + dq).T * 0.125)

    def join(j, _):
        dqkv[:, tile(j, width)] = unrope(own[0][:, tile(j)] + landed[0, :, tile(j)].astype(F32))
        dqkv[:, tile(j, 2 * width)] = (own[1][:, tile(j)] + landed[1, :, tile(j)].astype(F32)).astype(BF16)
        return 0

    base = 3 * ffs + pairs + 1
    for part, (low, high) in enumerate(((0, FIRST_PAIRS), (FIRST_PAIRS, pairs))):
        loop("far", low, high, far)
        lanes = pl.ds(low * LANES, (high - low) * LANES)
        sends = [
            pltpu.make_async_remote_copy(
                src_ref=away[i].at[:, lanes], dst_ref=landed.at[i, :, lanes],
                send_sem=kv_send.at[8 + 2 * part + i], recv_sem=kv_recv.at[8 + 2 * part + i],
                device_id=sibling, device_id_type=MESH,
            )
            for i in range(2)
        ]
        for send in sends:
            send.start()
        loop("near", low, high, near)
        for send in sends:
            send.wait()
        lax.fori_loop(low, high, join, 0)

        def weight_grads(j, _):
            for third in range(3):
                both = nn(xnt[...], dqkv[:, tile(j, third * width, 2)]).astype(BF16)
                for t in range(2):
                    grads[base + third * pairs + 2 * j + t] = both[:, t * LANES : (t + 1) * LANES]
            return 0

        lax.fori_loop(low // 2, high // 2, weight_grads, 0)
        after(("join", part))

    grad1 = nt(dqkv[...], wqkv[...])
    unit, scale = row_stats(xs[...].astype(F32))
    dx[...] = (dh[...] + norm_back(grad1, unit, scale, gain1)).astype(BF16)
    after(("dx", 0))
    reducer.settle()
    after("end")

    spread(x_in, xs, 0, wait_sent)
    spread(cot_in, cs, 4, wait_sent)
    for src, dst, base in ((outs, out_o, 8), (dx, dx_o, 12)):
        for n in range(n_seq):
            gather(src, dst, base, n, wait_sent)
        for block in range(2):
            for part in range(2):
                wait_bytes(dst.at[block, pl.ds(part * half, half)], recv_sem.at[base + 2 * block + part])


def layer(n_doc, n_seq, inputs, cotangent, gain1, gain2, wqkv, wo, win, wout, cos, sin):
    blocks, rows, width = inputs.shape
    tokens = blocks * rows
    ff = wout.shape[0]
    pairs = width // LANES
    streams, _, total = stream_plan(width, ff)
    rounds = log2(n_doc) - 1 + log2(n_seq)
    kept = halvings(width, rounds)
    legs = 2 + rounds + sum(1 for _, split in kept if split)
    slots = sum(stream.count for stream in streams)
    hbm, vmem = pl.BlockSpec(memory_space=pl.ANY), pl.BlockSpec(memory_space=pltpu.VMEM)
    sds, dma = jax.ShapeDtypeStruct, pltpu.SemaphoreType.DMA
    row_b = pltpu.VMEM((tokens, width), BF16)
    row_f = pltpu.VMEM((tokens, width), F32)
    return pl.pallas_call(
        functools.partial(layer_kernel, n_doc, n_seq),
        out_shape=[
            sds((blocks, rows, width), BF16), sds((blocks, rows, width), BF16), sds((total, width, LANES), BF16),
        ],
        in_specs=[hbm, hbm, vmem, vmem] + [hbm] * 6,
        out_specs=[hbm] * 3,
        scratch_shapes=[
            row_b, row_b, row_b,
            pltpu.VMEM(wqkv.shape, BF16), pltpu.VMEM(wo.shape, BF16), pltpu.VMEM(win.shape, BF16), pltpu.VMEM(wout.shape, BF16),
            pltpu.VMEM((tokens, LANES), F32), pltpu.VMEM((tokens, LANES), F32),
            row_b, row_b, pltpu.VMEM((2 * tokens, width), BF16), pltpu.VMEM((2 * tokens, width), BF16),
            row_b, row_f, row_b, pltpu.VMEM((width, tokens), BF16),
            pltpu.VMEM((tokens, ff), BF16), pltpu.VMEM((tokens, 2 * ff), BF16), pltpu.VMEM((width, tokens), BF16),
            row_b, row_f, row_f,
            pltpu.VMEM((pairs, 2, tokens), F32), pltpu.VMEM((pairs, 2, tokens), F32),
            pltpu.VMEM((pairs, LANES, tokens), F32), pltpu.VMEM((2, tokens, width), BF16),
            pltpu.VMEM((total, width, LANES), BF16),
            pltpu.VMEM((slots, Reducer.landing_rows(width, rounds), LANES), BF16),
            pltpu.VMEM((slots, width, LANES), BF16), pltpu.VMEM((tokens, 1), F32),
            dma((12,)), dma((16,)), dma((16,)), dma((12,)), dma((12,)),
            dma((len(streams), legs)), dma((len(streams), legs)), dma((len(streams),)),
        ],
        compiler_params=pltpu.CompilerParams(collective_id=0, has_side_effects=True, vmem_limit_bytes=VMEM_LIMIT),
        name="layer",
    )(inputs, cotangent, gain1, gain2, wqkv, wo, win, wout, cos, sin)


def widen_kernel(ff, width, g, wqkv, gain1, out, dx, dqkv_o, dwo_o, dwin_o, dwout_o, gain1_o, gain2_o, out_o, dx_o):
    out_o[...] = out[...]
    dx_o[...] = dx[...]
    ffs, pairs = ff // LANES, width // LANES
    base = 3 * ffs + pairs + 1
    for j in range(ffs):
        dwout_o[j * LANES : (j + 1) * LANES, :] = g[j].astype(F32).T
    for j in range(2 * ffs):
        dwin_o[:, j * LANES : (j + 1) * LANES] = g[ffs + j].astype(F32)
    for j in range(pairs):
        dwo_o[:, j * LANES : (j + 1) * LANES] = g[3 * ffs + j].astype(F32)
    gain2_o[...] = g[base - 1].astype(F32).T[0]
    along = jnp.zeros((LANES, LANES), F32)
    for j in range(3 * pairs):
        lanes = slice(j * LANES, (j + 1) * LANES)
        part = g[base + j].astype(F32)
        dqkv_o[:, lanes] = part
        along += part * wqkv[:, lanes].astype(F32)
    total = jnp.sum(along.T, axis=0, keepdims=True)
    gain1_o[...] = (total / gain1[...].reshape(1, LANES))[0]


def widen(ff, g, wqkv, gain1, out, dx):
    total, width, _ = g.shape
    sds = jax.ShapeDtypeStruct
    across = lambda i: (i, 0)
    down = lambda i: (0, i)
    flat = pl.BlockSpec((LANES,), lambda i: (i,))
    blocks, rows, _ = out.shape
    token = pl.BlockSpec((blocks, rows, LANES), lambda i: (0, 0, i))
    return pl.pallas_call(
        functools.partial(widen_kernel, ff, width),
        grid=(width // LANES,),
        out_shape=[
            sds(wqkv.shape, F32), sds((width, width), F32), sds((width, 2 * ff), F32), sds((ff, width), F32),
            sds((width,), F32), sds((width,), F32), sds(out.shape, BF16), sds(dx.shape, BF16),
        ],
        in_specs=[
            pl.BlockSpec((total, LANES, LANES), lambda i: (0, i, 0)), pl.BlockSpec((LANES, wqkv.shape[1]), across), flat, token, token,
        ],
        out_specs=[
            pl.BlockSpec((LANES, wqkv.shape[1]), across), pl.BlockSpec((LANES, width), across),
            pl.BlockSpec((LANES, 2 * ff), across), pl.BlockSpec((ff, LANES), down), flat, flat, token, token,
        ],
        compiler_params=pltpu.CompilerParams(vmem_limit_bytes=VMEM_LIMIT),
        name="widen",
    )(g, wqkv, gain1, out, dx)


def rotary_tables(length):
    half = HEAD_DIM // 2
    frequency = ROPE_THETA ** (-(np.arange(half) * 2.0) / HEAD_DIM)
    angles = np.arange(length)[:, None] * frequency[None, :]
    cos, sin = np.cos(angles), np.sin(angles)
    per_tile = LANES // HEAD_DIM
    cos = np.tile(np.concatenate([cos, cos], axis=1), (1, per_tile))
    sin = np.tile(np.concatenate([-sin, sin], axis=1), (1, per_tile))
    return jnp.asarray(cos, F32), jnp.asarray(sin, F32)


def per_device(
    n_doc, n_seq,
    inputs, attn_gain, qkv_weight, attn_out_weight, mlp_gain, mlp_in_weight, mlp_out_weight, cotangent,
):
    blocks, rows, width = inputs.shape
    ff = mlp_out_weight.shape[0]
    cos, sin = rotary_tables(rows * n_seq)
    output, dx, grads = layer(
        n_doc, n_seq, inputs, cotangent, attn_gain, mlp_gain,
        qkv_weight, attn_out_weight, mlp_in_weight, mlp_out_weight, cos, sin,
    )
    dqkv, dwo, dwin, dwout, dgain1, dgain2, output, dx = widen(ff, grads, qkv_weight, attn_gain, output, dx)
    return output, dx, dgain1, dqkv, dwo, dgain2, dwin, dwout


def solution(mesh):
    n_doc, n_seq = mesh.shape["doc"], mesh.shape["seq"]
    placed = (P("doc", "seq", None), P(), P(), P(), P(), P(), P(), P("doc", "seq", None))
    return jax.shard_map(
        functools.partial(per_device, n_doc, n_seq),
        mesh=mesh,
        in_specs=placed,
        out_specs=(P("doc", "seq", None), P("doc", "seq", None), P(), P(), P(), P(), P(), P()),
        check_vma=False,
    )
```

```python
import functools

import jax
import jax.numpy as jnp
import numpy as np
from jax import lax
from jax.experimental import pallas as pl
from jax.experimental.pallas import tpu as pltpu
from jax.sharding import PartitionSpec as P

HEAD_DIM = 64
ROPE_THETA = 160000.0
NORM_EPSILON = 1e-05
F32 = jnp.float32
BF16 = jnp.bfloat16
MESH = pl.DeviceIdType.MESH
LANES = 128
VMEM_LIMIT = 60 << 20


def nn(a, b):
    return lax.dot_general(a, b, (((1,), (0,)), ((), ())), preferred_element_type=F32)


def nt(a, b):
    return lax.dot_general(a, b, (((1,), (1,)), ((), ())), preferred_element_type=F32)


def lane_of(shape):
    return lax.broadcasted_iota(jnp.int32, shape, 1)


def one_head(pair, sub):
    lane = lane_of(pair.shape)
    mine = (lane < HEAD_DIM) if sub == 0 else (lane >= HEAD_DIM)
    return jnp.where(mine, pair, jnp.zeros_like(pair))


def turned(values):
    back = pltpu.roll(values, HEAD_DIM // 2, 1)
    ahead = pltpu.roll(values, LANES - HEAD_DIM // 2, 1)
    return jnp.where(lane_of(values.shape) % HEAD_DIM < HEAD_DIM // 2, ahead, back)


def row_stats(values):
    mean = jnp.mean(values, axis=1, keepdims=True)
    centered = values - mean
    scale = lax.rsqrt(jnp.mean(centered * centered, axis=1, keepdims=True) + NORM_EPSILON)
    return centered * scale, scale


def norm_back(grad, unit, scale, gain):
    weighted = grad * gain
    along = jnp.mean(weighted, axis=1, keepdims=True)
    across = jnp.mean(weighted * unit, axis=1, keepdims=True)
    return scale * (weighted - along - unit * across)


def bit_of(index, weight):
    return (index // weight) % 2


def flipped(index, weight):
    return index + weight - 2 * weight * bit_of(index, weight)


def greet(partners):
    barrier = pltpu.get_barrier_semaphore()
    for partner in partners:
        pl.semaphore_signal(barrier, inc=1, device_id=partner, device_id_type=MESH)
    pl.semaphore_wait(barrier, len(partners))


def group_partners(doc, seq, n_seq):
    core = doc % 2
    found = []
    for other_core in range(2):
        for step in range(n_seq):
            if other_core == 0 and step == 0:
                continue
            found.append(
                (doc - core + (core + other_core) % 2, (seq + step) % n_seq)
            )
    return found


class Exchange:
    def __init__(self, doc, seq, n_seq):
        assert n_seq == 4
        core = doc % 2
        self.doc, self.seq, self.core = doc, seq, core
        self.base = doc - core
        side = seq // 2
        self.near_first = [seq, flipped(seq, 1), 2 - side, 3 - 3 * side]
        self.block_first = (1 - core) * side

    def out_piece(self, n):
        block = self.block_first + n // 2 - 2 * self.block_first * (n // 2)
        half = n % 2
        return block, half, (self.base + half, 2 * self.core + block)

    def back_target(self, quarter):
        return (self.base + self.seq // 2, quarter)

    def is_self(self, target):
        return jnp.logical_and(target[0] == self.doc, target[1] == self.seq)


def send_or_keep(ex, target, src, dst, send_sem, recv_sem):
    mine = ex.is_self(target)

    @pl.when(mine)
    def _():
        pltpu.make_async_copy(src, dst, recv_sem).start()

    @pl.when(jnp.logical_not(mine))
    def _():
        pltpu.make_async_remote_copy(
            src_ref=src, dst_ref=dst, send_sem=send_sem, recv_sem=recv_sem,
            device_id=target, device_id_type=MESH,
        ).start()


def wait_sent(ex, target, src, dst, send_sem, recv_sem):
    @pl.when(jnp.logical_not(ex.is_self(target)))
    def _():
        pltpu.make_async_remote_copy(
            src_ref=src, dst_ref=dst, send_sem=send_sem, recv_sem=recv_sem,
            device_id=target, device_id_type=MESH,
        ).wait_send()


def wait_bytes(ref, sem):
    pltpu.make_async_copy(ref, ref, sem).wait()


LINK_RATE, CORE_RATE, ROUND_LATENCY, SPARE = 44135.0, 510e3, 2.6, 1.5
NEAR_SHARE, FAR_SHARE = 1.0, 0.25
STEP_TIME, ADD_TIME = 0.1, 0.4e-6
PIECE_TIME = {"feed": 2.0, "last": 1.1, "mix": 1.2, "norm": 3.5, "wo": 1.0, "do": 1.4, "far": 1.25, "near": 1.25, "join": 2.5, "dx": 4.0}
FIRST_PAIRS = 4
ORDERS = "11000110001010111001101100"
OUT, DX = -1, -2
OUT_AFTER, DX_GAP = (5, 5, 5, 8), 14.0


def log2(n):
    return n.bit_length() - 1


class Stream:
    def __init__(self, first, second, count):
        self.first, self.second, self.count = first, second, count


def halvings(rows, rounds):
    kept, extent = [], rows
    for _ in range(rounds):
        split = (extent // 2) % 16 == 0
        extent = extent // 2 if split else extent
        kept.append((extent, split))
    return kept


def axes_of(n_doc, n_seq):
    doc_axes = [("doc", 1 << i) for i in range(1, log2(n_doc))]
    seq_axes = [("seq", 1 << i) for i in range(log2(n_seq))]
    return doc_axes, seq_axes


def axis_order(index, n_doc, n_seq):
    doc_axes, seq_axes = axes_of(n_doc, n_seq)
    code = int(ORDERS[index % len(ORDERS)])
    turn = code % 2 * (len(doc_axes) // 2)
    doc_axes = doc_axes[turn:] + doc_axes[:turn]
    place = len(doc_axes) * (2 - code // 2) // 2
    return doc_axes[:place] + seq_axes[:-1] + doc_axes[place:] + seq_axes[-1:]


def stream_plan(width, ff):
    ffs, pairs = ff // LANES, width // LANES
    streams, ready = [], {}

    def add(piece, first, second, count):
        ready.setdefault(piece, []).append(len(streams))
        streams.append(Stream(first, second, count))

    assert ffs % 2 == 1 and pairs % 2 == 0
    covered = ffs - 1
    for low in range(0, covered, 2):
        for base in (0, ffs, 2 * ffs):
            add(("feed", low // 2), base + low, base + low + 1, 1)
    add(("last", 0), covered, ffs + covered, 1)
    add(("norm", 0), 2 * ffs + covered, 3 * ffs + pairs, 1)
    for start in range(3 * ffs, 3 * ffs + pairs, 2):
        add(("wo", 0), start, start + 1, 1)
    base = 3 * ffs + pairs + 1
    for part, (low, high) in enumerate(((0, FIRST_PAIRS), (FIRST_PAIRS, pairs))):
        for third in range(3):
            for start in range(base + third * pairs + low, base + third * pairs + high, 2):
                add(("join", part), start, start + 1, 1)
    return streams, ready, base + 3 * pairs


def piece_list(ff, pairs):
    ffs = ff // LANES
    pieces = [("feed", j) for j in range(ffs // 2)] + [("last", 0)]
    pieces += [("mix", 0), ("norm", 0), ("do", 0), ("wo", 0)]
    for part, (low, high) in enumerate(((0, FIRST_PAIRS), (FIRST_PAIRS, pairs))):
        pieces += [("far", j) for j in range(low, high)] + [("near", j) for j in range(low, high)]
        pieces.append(("join", part))
    return pieces + [("dx", 0)]


def agenda(streams, ready, pieces, rows, n_doc, n_seq):
    rounds = log2(n_doc) - 1 + log2(n_seq)
    kept = halvings(rows, rounds)
    ups = [r for r in reversed(range(rounds)) if kept[r][1]]
    free, flying, steps = {}, [], {}
    near, far = axes_of(n_doc, n_seq)[1]

    def legs(index):
        order = axis_order(index, n_doc, n_seq)
        unit = streams[index].count * LANES * 2
        trip = [("core", rows * unit)]
        trip += [(order[r], kept[r][0] * unit) for r in range(rounds)]
        trip += [(order[r], kept[r][0] * unit) for r in ups]
        return trip + [("core", rows * unit)]

    def occupy(axis, size, when):
        rate = CORE_RATE if axis == "core" else LINK_RATE / 2 if axis == far else LINK_RATE
        begin = max(when, free.get(axis, 0.0))
        free[axis] = begin + size / rate
        for axis_from, axis_to, share, speed in ((far, near, NEAR_SHARE, LINK_RATE), (near, far, FAR_SHARE, LINK_RATE / 2)):
            if axis == axis_from and share:
                free[axis_to] = max(free.get(axis_to, 0.0), begin) + share * size / speed
        return free[axis]

    def leave(chunk, when):
        if chunk:
            occupy(near if chunk == 1 else far, 196e3, when)

    def depart(index, leg, when):
        flying.append((occupy(*legs(index)[leg], when) + ROUND_LATENCY, index, leg))

    def serve(now):
        flying.sort()
        done, index, leg = flying.pop(0)
        trip = legs(index)
        now = max(now, done) + STEP_TIME + (trip[leg][1] * ADD_TIME if leg <= rounds else 0.0)
        if leg + 1 < len(trip):
            depart(index, leg + 1, now)
        return now, (index, leg)

    now = 0.0
    for piece in pieces:
        now += PIECE_TIME[piece[0]]
        actions = steps.setdefault(piece, [])
        for index in ready.get(piece, ()):
            actions.append((index, -1))
            depart(index, 0, now)
            now += STEP_TIME
        for chunk, place in enumerate(OUT_AFTER):
            if piece == pieces[place]:
                actions.append((OUT, chunk))
                leave(chunk, now)
                now += STEP_TIME
        while flying and min(flying)[0] + SPARE <= now:
            now, action = serve(now)
            actions.append(action)
    last = steps.setdefault("end", [])
    begin, chunk = now, 0
    while flying or chunk < n_seq:
        upcoming = max(now, min(flying)[0]) if flying else now
        if chunk < n_seq and (not flying or upcoming >= begin + chunk * DX_GAP):
            leave(chunk, now)
            last.append((DX, chunk))
            now += STEP_TIME
            chunk += 1
            continue
        now, action = serve(now)
        last.append(action)
    return steps


class Reducer:
    def __init__(self, streams, n_doc, n_seq, doc, seq, grads, landing, final, out, send_sem, recv_sem, own_sem):
        self.streams, self.grads, self.landing, self.final, self.out = streams, grads, landing, final, out
        self.send_sem, self.recv_sem, self.own_sem = send_sem, recv_sem, own_sem
        self.busy, self.unsent = False, []
        self.core = doc % 2
        self.rows = grads.shape[1]
        self.rounds = log2(n_doc) - 1 + log2(n_seq)
        self.kept = halvings(self.rows, self.rounds)
        self.ups = [r for r in reversed(range(self.rounds)) if self.kept[r][1]]
        self.legs = 2 + self.rounds + len(self.ups)
        self.sibling = (flipped(doc, 1), seq)
        self.bits, self.partners = {}, {}
        for name, weight in sum(axes_of(n_doc, n_seq), []):
            index = doc if name == "doc" else seq
            self.bits[name, weight] = bit_of(index, weight)
            self.partners[name, weight] = (flipped(doc, weight), seq) if name == "doc" else (doc, flipped(seq, weight))
        self.orders = [axis_order(i, n_doc, n_seq) for i in range(len(streams))]
        self.slots, used = [], 0
        for stream in streams:
            self.slots.append(pl.ds(used, stream.count))
            used += stream.count
        self.plans = []
        for order in self.orders:
            offset, base, plan = 0, 0, []
            for (keep, split), axis in zip(self.kept, order):
                bit = self.bits[axis]
                mine = offset + bit * keep if split else offset
                theirs = offset + (1 - bit) * keep if split else offset
                plan.append((mine, theirs, base, keep))
                base += keep
                offset = mine
            self.plans.append(plan)

    @staticmethod
    def landing_rows(rows, rounds):
        return sum(keep for keep, _ in halvings(rows, rounds))

    def tiles(self, index, other=False):
        stream = self.streams[index]
        side = 1 - self.core if other else self.core
        return pl.ds(stream.first + side * (stream.second - stream.first), stream.count)

    def span(self, start, extent):
        return pl.ds(start if isinstance(start, int) else pl.multiple_of(start, 16), extent)

    def copy(self, index, leg, receiving=False):
        slot = self.slots[index]
        if leg == 0:
            src, dst, partner = self.grads.at[self.tiles(index, True)], self.final.at[slot], self.sibling
        elif leg <= self.rounds:
            mine, theirs, base, keep = self.plans[index][leg - 1]
            src = self.grads.at[self.tiles(index), self.span(theirs, keep)]
            dst, partner = self.landing.at[slot, pl.ds(base, keep)], self.partners[self.orders[index][leg - 1]]
        elif leg < self.legs - 1:
            r = self.ups[leg - 1 - self.rounds]
            mine, theirs, base, keep = self.plans[index][r]
            src = dst = self.final.at[slot, self.span(theirs if receiving else mine, keep)]
            partner = self.partners[self.orders[index][r]]
        else:
            src, dst, partner = self.final.at[slot], self.out.at[self.tiles(index, receiving)], self.sibling
        return pltpu.make_async_remote_copy(
            src_ref=src, dst_ref=dst, send_sem=self.send_sem.at[index, leg], recv_sem=self.recv_sem.at[index, leg],
            device_id=partner, device_id_type=MESH,
        )

    def own(self, index):
        return pltpu.make_async_copy(self.final.at[self.slots[index]], self.out.at[self.tiles(index)], self.own_sem.at[index])

    def add(self, index, leg):
        stream, slot = self.streams[index], self.slots[index]
        start = stream.first + self.core * (stream.second - stream.first)
        low = slot.start
        if leg == 0:
            mine, base, keep = 0, 0, self.rows
        else:
            mine, _, base, keep = self.plans[index][leg - 1]
        block = keep
        while block > 96:
            block //= 2

        def body(i, _):
            here = self.span(mine + i * block, block)
            for t in range(stream.count):
                if leg == 0:
                    other = self.final[low + t, here]
                else:
                    other = self.landing[low + t, self.span(base + i * block, block)]
                total = (self.grads[start + t, here].astype(F32) + other.astype(F32)).astype(BF16)
                if leg == self.rounds:
                    self.final[low + t, here] = total
                else:
                    self.grads[start + t, here] = total
            return 0

        lax.fori_loop(0, keep // block, body, 0)

    def settle(self):
        self.busy = False
        for index, leg in self.unsent:
            self.copy(index, leg).wait_send()

    def act(self, index, leg):
        if leg >= 0:
            if self.busy:
                self.unsent.append((index, leg))
            else:
                self.copy(index, leg).wait_send()
            self.copy(index, leg, True).wait_recv()
            if leg <= self.rounds:
                self.add(index, leg)
            if leg == self.legs - 1:
                self.own(index).wait()
        if leg + 1 < self.legs:
            self.copy(index, leg + 1).start()
        if leg + 1 == self.legs - 1:
            self.own(index).start()


def layer_kernel(
    n_doc, n_seq,
    x_in, cot_in, gain1_in, gain2_in, wqkv_in, wo_in, win_in, wout_in, cos_in, sin_in,
    out_o, dx_o, g_o,
    xs, cs, outs, wqkv, wo, win, wout, cos, sin, xn, q, k, v, att, h, xn2, xn2t, hid, dgu, dmt, do, dh, acc, lse, dd,
    dqt, landed, grads, landing, final, rms,
    w_sem, send_sem, recv_sem, kv_send, kv_recv, sum_send, sum_recv, own_sem,
):
    doc, seq = lax.axis_index("doc"), lax.axis_index("seq")
    core = doc % 2
    ex = Exchange(doc, seq, n_seq)
    half = x_in.shape[1] // 2
    tokens, width = xs.shape
    ff = wout.shape[0]
    ffs, pairs = ff // LANES, width // LANES
    sibling = (flipped(doc, 1), seq)

    loads = [
        pltpu.make_async_copy(s, d, w_sem.at[i])
        for i, (s, d) in enumerate(
            [(wqkv_in, wqkv), (wo_in, wo), (win_in, win), (wout_in, wout)]
            + [
                (t.at[pl.ds((2 * quarter + core) * half, half)], d.at[pl.ds(quarter * half, half)])
                for t, d in ((cos_in, cos), (sin_in, sin))
                for quarter in range(n_seq)
            ]
        )
    ]
    loads[0].start()
    for load in loads[4:]:
        load.start()
    greet(group_partners(doc, seq, n_seq) + [(flipped(doc, w), seq) for _, w in axes_of(n_doc, n_seq)[0]])

    def rows_of(slot):
        return pl.ds(pl.multiple_of(slot * half, half), half)

    def spread(src, dst, base, act):
        for n in range(n_seq):
            block, part, target = ex.out_piece(n)
            act(
                ex, target, src.at[block, pl.ds(part * half, half)], dst.at[rows_of(seq)],
                send_sem.at[base + n], recv_sem.at[base + seq],
            )

    def gather(src, dst, base, n, act):
        quarter = ex.near_first[n]
        act(
            ex, ex.back_target(quarter), src.at[rows_of(quarter)], dst.at[seq % 2, rows_of(core)],
            send_sem.at[base + n], recv_sem.at[base + 2 * (seq % 2) + core],
        )

    spread(x_in, xs, 0, send_or_keep)
    for load in loads[1:4]:
        load.start()
    gain1, gain2 = gain1_in[...].reshape(1, width), gain2_in[...].reshape(1, width)

    streams, ready, _ = stream_plan(width, ff)
    steps = agenda(streams, ready, piece_list(ff, pairs), width, n_doc, n_seq)
    reducer = Reducer(streams, n_doc, n_seq, doc, seq, grads, landing, final, g_o, sum_send, sum_recv, own_sem)

    def after(piece):
        for index, leg in steps.get(piece, ()):
            if index == OUT:
                gather(outs, out_o, 8, leg, send_or_keep)
            elif index == DX:
                gather(do, dx_o, 12, leg, send_or_keep)
            else:
                reducer.act(index, leg)

    def loop(name, low, high, body):
        def one(j, _):
            body(j)
            for at in range(low, high):
                if steps.get((name, at)):
                    pl.when(j == at)(functools.partial(after, (name, at)))
            return 0

        lax.fori_loop(low, high, one, 0)

    def tile(j, base=0, count=1):
        return pl.ds(pl.multiple_of(base + j * LANES * count, LANES), LANES * count)

    def roped(part, here, scale):
        return ((part * cos[here] + turned(part) * sin[here]) * scale).astype(BF16)

    def kv_copies(n):
        here = rows_of(ex.near_first[n])
        there = pl.ds(pl.multiple_of(tokens + ex.near_first[n] * half, half), half)
        return [
            pltpu.make_async_remote_copy(
                src_ref=ref.at[here], dst_ref=ref.at[there], send_sem=kv_send.at[2 * n + i],
                recv_sem=kv_recv.at[2 * n + i], device_id=sibling, device_id_type=MESH,
            )
            for i, ref in enumerate((k, v))
        ]

    loads[0].wait()
    for load in loads[4:]:
        load.wait()
    for n in range(n_seq):
        here = rows_of(ex.near_first[n])
        wait_bytes(xs.at[here], recv_sem.at[ex.near_first[n]])
        if n == n_seq - 2:
            spread(cot_in, cs, 4, send_or_keep)
        unit, _ = row_stats(xs[here].astype(F32))
        normed = (unit * gain1).astype(BF16)
        xn[here] = normed

        def project(j, _, here=here):
            weights = jnp.concatenate([wqkv[:, tile(j, width)], wqkv[:, tile(j, 2 * width)]], axis=1)
            both = nn(xn[here], weights)
            k[here, tile(j)] = roped(both[:, :LANES], here, 1.0)
            v[here, tile(j)] = both[:, LANES:].astype(BF16)
            return 0

        lax.fori_loop(0, pairs, project, 0)
        for copy in kv_copies(n):
            copy.start()

        def project_q(j, _, here=here):
            both = nn(xn[here], wqkv[:, tile(j, 0, 2)])
            for t in range(2):
                q[here, tile(2 * j + t)] = roped(both[:, t * LANES : (t + 1) * LANES], here, 0.125)
            return 0

        lax.fori_loop(0, pairs // 2, project_q, 0)

    def attend(j):
        lanes = tile(j)
        k2, vt, q2 = k[:, lanes], v[:, lanes].T, q[:, lanes]
        scores = [nt(one_head(k2, sub), q2) for sub in range(2)]
        mixed = []
        for sub in range(2):
            top = jnp.max(scores[sub], axis=0, keepdims=True)
            weights = jnp.exp(scores[sub] - top)
            total = jnp.sum(weights, axis=0, keepdims=True)
            lse[j, sub : sub + 1, :] = top + jnp.log(total)
            mixed.append(
                nn(vt[sub * HEAD_DIM : (sub + 1) * HEAD_DIM], weights.astype(BF16)) * (1.0 / total)
            )
        att[:, lanes] = jnp.concatenate(mixed, axis=0).T.astype(BF16)

    def attend_group(group, _):
        for j in range(pairs // 2):
            attend(group * (pairs // 2) + j)
        return 0

    for n in range(n_seq):
        for copy in kv_copies(n):
            copy.wait()
    lax.fori_loop(0, 2, attend_group, 0)

    loads[1].wait()
    h[...] = xs[...].astype(F32) + nn(att[...], wo[...])
    unit2, scale2 = row_stats(h[...])
    dh[...] = unit2
    rms[...] = scale2
    xn2[...] = (unit2 * gain2).astype(BF16)
    xn2t[...] = xn2[...].T
    loads[2].wait()
    loads[3].wait()
    for slot in range(n_seq):
        wait_bytes(cs.at[rows_of(slot)], recv_sem.at[4 + slot])
    dmt[...] = cs[...].T

    def feed(j, count):
        first = 2 * j
        wide = count * LANES
        lanes = pl.ds(pl.multiple_of(first * LANES, LANES), wide)
        up_lanes = pl.ds(pl.multiple_of(ff + first * LANES, LANES), wide)
        gate, up = nn(xn2[...], win[:, lanes]), nn(xn2[...], win[:, up_lanes])
        phi = 0.5 * (1.0 + lax.erf(gate * 0.7071067811865476))
        slope = phi + gate * (0.3989422804014327 * jnp.exp(-0.5 * gate * gate))
        active = gate * phi
        inner = (active * up).astype(BF16)
        hid[:, lanes] = inner
        dhid = nt(cs[...], wout[lanes, :])
        dgate, dup = (dhid * up * slope).astype(BF16), (dhid * active).astype(BF16)
        dgu[:, lanes] = dgate
        dgu[:, up_lanes] = dup
        for base, left, right in ((0, dmt, inner), (ffs, xn2t, dgate), (2 * ffs, xn2t, dup)):
            part = nn(left[...], right).astype(BF16)
            for t in range(count):
                grads[base + first + t] = part[:, t * LANES : (t + 1) * LANES]

    loop("feed", 0, ffs // 2, lambda j: feed(j, 2))
    feed(ffs // 2, 1)
    after(("last", 0))

    outs[...] = (h[...] + nn(hid[...], wout[...])).astype(BF16)
    after(("mix", 0))

    acc[...] = nt(dgu[...], win[...])
    unit2, grad2 = dh[...], acc[...]
    gain_terms = jnp.sum(grad2 * unit2, axis=0, keepdims=True)
    grads[3 * ffs + pairs] = jnp.broadcast_to(gain_terms, (LANES, width)).T.astype(BF16)
    dh[...] = cs[...].astype(F32) + norm_back(grad2, unit2, rms[...], gain2)
    after(("norm", 0))

    datt = dh[...].astype(BF16)
    do[...] = nt(datt, wo[...]).astype(BF16)
    lane = lax.broadcasted_iota(jnp.int32, (16, width), 1)
    row = lax.broadcasted_iota(jnp.int32, (16, width), 0)
    pick = jnp.where(lane // HEAD_DIM == row, 1.0, 0.0).astype(BF16)
    product = do[...].astype(F32) * att[...].astype(F32)
    high = product.astype(BF16)
    sums = nt(pick, high) + nt(pick, (product - high.astype(F32)).astype(BF16))
    for j in range(pairs):
        dd[j] = sums[2 * j : 2 * j + 2]
    after(("do", 0))

    att_t = att[...].T
    for j in range(pairs // 2):
        both = nn(att_t, datt[:, 2 * j * LANES : (2 * j + 2) * LANES]).astype(BF16)
        for t in range(2):
            grads[3 * ffs + 2 * j + t] = both[:, t * LANES : (t + 1) * LANES]
    after(("wo", 0))

    dqkv, xnt, dx = win.at[pl.ds(0, tokens)], xn2t, do
    away, own = (xn2, att), (h, acc)
    xnt[...] = xn[...].T

    def attend_back(keys, j):
        lanes = tile(j)
        q2, do2 = q[:, lanes], do[:, lanes]
        k2, v2 = k[keys, lanes], v[keys, lanes]
        kt = k2.T
        dks, dvs, dqs = [], [], []
        for sub in range(2):
            probs = jnp.exp(nt(one_head(k2, sub), q2) - lse[j, sub : sub + 1, :])
            dprobs = nt(one_head(v2, sub), do2)
            dscores = (probs * (dprobs - dd[j, sub : sub + 1, :])).astype(BF16)
            dvs.append(nn(probs.astype(BF16), do2))
            dks.append(nn(dscores, q2))
            dqs.append(nn(kt[sub * HEAD_DIM : (sub + 1) * HEAD_DIM], dscores))
        low = lane_of(dks[0].shape) < HEAD_DIM
        return jnp.where(low, dks[0], dks[1]), jnp.where(low, dvs[0], dvs[1]), jnp.concatenate(dqs, axis=0)

    def unrope(part):
        return (part * cos[...] - turned(part) * sin[...]).astype(BF16)

    def far(j):
        dk, dv, dq = attend_back(pl.ds(tokens, tokens), j)
        away[0][:, tile(j)] = dk.astype(BF16)
        away[1][:, tile(j)] = dv.astype(BF16)
        dqt[j] = dq

    def near(j):
        dk, dv, dq = attend_back(pl.ds(0, tokens), j)
        own[0][:, tile(j)] = dk
        own[1][:, tile(j)] = dv
        dqkv[:, tile(j)] = unrope((dqt[j] + dq).T * 0.125)

    def join(j, _):
        dqkv[:, tile(j, width)] = unrope(own[0][:, tile(j)] + landed[0, :, tile(j)].astype(F32))
        dqkv[:, tile(j, 2 * width)] = (own[1][:, tile(j)] + landed[1, :, tile(j)].astype(F32)).astype(BF16)
        return 0

    base = 3 * ffs + pairs + 1
    for part, (low, high) in enumerate(((0, FIRST_PAIRS), (FIRST_PAIRS, pairs))):
        loop("far", low, high, far)
        lanes = pl.ds(low * LANES, (high - low) * LANES)
        sends = [
            pltpu.make_async_remote_copy(
                src_ref=away[i].at[:, lanes], dst_ref=landed.at[i, :, lanes],
                send_sem=kv_send.at[8 + 2 * part + i], recv_sem=kv_recv.at[8 + 2 * part + i],
                device_id=sibling, device_id_type=MESH,
            )
            for i in range(2)
        ]
        for send in sends:
            send.start()
        loop("near", low, high, near)
        for send in sends:
            send.wait()
        lax.fori_loop(low, high, join, 0)

        def weight_grads(j, _):
            for third in range(3):
                both = nn(xnt[...], dqkv[:, tile(j, third * width, 2)]).astype(BF16)
                for t in range(2):
                    grads[base + third * pairs + 2 * j + t] = both[:, t * LANES : (t + 1) * LANES]
            return 0

        lax.fori_loop(low // 2, high // 2, weight_grads, 0)
        after(("join", part))

    grad1 = nt(dqkv[...], wqkv[...])
    unit, scale = row_stats(xs[...].astype(F32))
    dx[...] = (dh[...] + norm_back(grad1, unit, scale, gain1)).astype(BF16)
    after(("dx", 0))
    reducer.settle()
    after("end")

    spread(x_in, xs, 0, wait_sent)
    spread(cot_in, cs, 4, wait_sent)
    for src, dst, base in ((outs, out_o, 8), (dx, dx_o, 12)):
        for n in range(n_seq):
            gather(src, dst, base, n, wait_sent)
        for block in range(2):
            for part in range(2):
                wait_bytes(dst.at[block, pl.ds(part * half, half)], recv_sem.at[base + 2 * block + part])


def layer(n_doc, n_seq, inputs, cotangent, gain1, gain2, wqkv, wo, win, wout, cos, sin):
    blocks, rows, width = inputs.shape
    tokens = blocks * rows
    ff = wout.shape[0]
    pairs = width // LANES
    streams, _, total = stream_plan(width, ff)
    rounds = log2(n_doc) - 1 + log2(n_seq)
    kept = halvings(width, rounds)
    legs = 2 + rounds + sum(1 for _, split in kept if split)
    slots = sum(stream.count for stream in streams)
    hbm, vmem = pl.BlockSpec(memory_space=pl.ANY), pl.BlockSpec(memory_space=pltpu.VMEM)
    sds, dma = jax.ShapeDtypeStruct, pltpu.SemaphoreType.DMA
    row_b = pltpu.VMEM((tokens, width), BF16)
    row_f = pltpu.VMEM((tokens, width), F32)
    return pl.pallas_call(
        functools.partial(layer_kernel, n_doc, n_seq),
        out_shape=[
            sds((blocks, rows, width), BF16), sds((blocks, rows, width), BF16), sds((total, width, LANES), BF16),
        ],
        in_specs=[hbm, hbm, vmem, vmem] + [hbm] * 6,
        out_specs=[hbm] * 3,
        scratch_shapes=[
            row_b, row_b, row_b,
            pltpu.VMEM(wqkv.shape, BF16), pltpu.VMEM(wo.shape, BF16), pltpu.VMEM(win.shape, BF16), pltpu.VMEM(wout.shape, BF16),
            pltpu.VMEM((tokens, LANES), F32), pltpu.VMEM((tokens, LANES), F32),
            row_b, row_b, pltpu.VMEM((2 * tokens, width), BF16), pltpu.VMEM((2 * tokens, width), BF16),
            row_b, row_f, row_b, pltpu.VMEM((width, tokens), BF16),
            pltpu.VMEM((tokens, ff), BF16), pltpu.VMEM((tokens, 2 * ff), BF16), pltpu.VMEM((width, tokens), BF16),
            row_b, row_f, row_f,
            pltpu.VMEM((pairs, 2, tokens), F32), pltpu.VMEM((pairs, 2, tokens), F32),
            pltpu.VMEM((pairs, LANES, tokens), F32), pltpu.VMEM((2, tokens, width), BF16),
            pltpu.VMEM((total, width, LANES), BF16),
            pltpu.VMEM((slots, Reducer.landing_rows(width, rounds), LANES), BF16),
            pltpu.VMEM((slots, width, LANES), BF16), pltpu.VMEM((tokens, 1), F32),
            dma((12,)), dma((16,)), dma((16,)), dma((12,)), dma((12,)),
            dma((len(streams), legs)), dma((len(streams), legs)), dma((len(streams),)),
        ],
        compiler_params=pltpu.CompilerParams(collective_id=0, has_side_effects=True, vmem_limit_bytes=VMEM_LIMIT),
        name="layer",
    )(inputs, cotangent, gain1, gain2, wqkv, wo, win, wout, cos, sin)


def widen_kernel(ff, width, g, wqkv, gain1, out, dx, dqkv_o, dwo_o, dwin_o, dwout_o, gain1_o, gain2_o, out_o, dx_o):
    out_o[...] = out[...]
    dx_o[...] = dx[...]
    ffs, pairs = ff // LANES, width // LANES
    base = 3 * ffs + pairs + 1
    for j in range(ffs):
        dwout_o[j * LANES : (j + 1) * LANES, :] = g[j].astype(F32).T
    for j in range(2 * ffs):
        dwin_o[:, j * LANES : (j + 1) * LANES] = g[ffs + j].astype(F32)
    for j in range(pairs):
        dwo_o[:, j * LANES : (j + 1) * LANES] = g[3 * ffs + j].astype(F32)
    gain2_o[...] = g[base - 1].astype(F32).T[0]
    along = jnp.zeros((LANES, LANES), F32)
    for j in range(3 * pairs):
        lanes = slice(j * LANES, (j + 1) * LANES)
        part = g[base + j].astype(F32)
        dqkv_o[:, lanes] = part
        along += part * wqkv[:, lanes].astype(F32)
    total = jnp.sum(along.T, axis=0, keepdims=True)
    gain1_o[...] = (total / gain1[...].reshape(1, LANES))[0]


def widen(ff, g, wqkv, gain1, out, dx):
    total, width, _ = g.shape
    sds = jax.ShapeDtypeStruct
    across = lambda i: (i, 0)
    down = lambda i: (0, i)
    flat = pl.BlockSpec((LANES,), lambda i: (i,))
    blocks, rows, _ = out.shape
    token = pl.BlockSpec((blocks, rows, LANES), lambda i: (0, 0, i))
    return pl.pallas_call(
        functools.partial(widen_kernel, ff, width),
        grid=(width // LANES,),
        out_shape=[
            sds(wqkv.shape, F32), sds((width, width), F32), sds((width, 2 * ff), F32), sds((ff, width), F32),
            sds((width,), F32), sds((width,), F32), sds(out.shape, BF16), sds(dx.shape, BF16),
        ],
        in_specs=[
            pl.BlockSpec((total, LANES, LANES), lambda i: (0, i, 0)), pl.BlockSpec((LANES, wqkv.shape[1]), across), flat, token, token,
        ],
        out_specs=[
            pl.BlockSpec((LANES, wqkv.shape[1]), across), pl.BlockSpec((LANES, width), across),
            pl.BlockSpec((LANES, 2 * ff), across), pl.BlockSpec((ff, LANES), down), flat, flat, token, token,
        ],
        compiler_params=pltpu.CompilerParams(vmem_limit_bytes=VMEM_LIMIT),
        name="widen",
    )(g, wqkv, gain1, out, dx)


def rotary_tables(length):
    half = HEAD_DIM // 2
    frequency = ROPE_THETA ** (-(np.arange(half) * 2.0) / HEAD_DIM)
    angles = np.arange(length)[:, None] * frequency[None, :]
    cos, sin = np.cos(angles), np.sin(angles)
    per_tile = LANES // HEAD_DIM
    cos = np.tile(np.concatenate([cos, cos], axis=1), (1, per_tile))
    sin = np.tile(np.concatenate([-sin, sin], axis=1), (1, per_tile))
    return jnp.asarray(cos, F32), jnp.asarray(sin, F32)


def per_device(
    n_doc, n_seq,
    inputs, attn_gain, qkv_weight, attn_out_weight, mlp_gain, mlp_in_weight, mlp_out_weight, cotangent,
):
    blocks, rows, width = inputs.shape
    ff = mlp_out_weight.shape[0]
    cos, sin = rotary_tables(rows * n_seq)
    output, dx, grads = layer(
        n_doc, n_seq, inputs, cotangent, attn_gain, mlp_gain,
        qkv_weight, attn_out_weight, mlp_in_weight, mlp_out_weight, cos, sin,
    )
    dqkv, dwo, dwin, dwout, dgain1, dgain2, output, dx = widen(ff, grads, qkv_weight, attn_gain, output, dx)
    return output, dx, dgain1, dqkv, dwo, dgain2, dwin, dwout


def solution(mesh):
    n_doc, n_seq = mesh.shape["doc"], mesh.shape["seq"]
    placed = (P("doc", "seq", None), P(), P(), P(), P(), P(), P(), P("doc", "seq", None))
    return jax.shard_map(
        functools.partial(per_device, n_doc, n_seq),
        mesh=mesh,
        in_specs=placed,
        out_specs=(P("doc", "seq", None), P("doc", "seq", None), P(), P(), P(), P(), P(), P()),
        check_vma=False,
    )
```
